32 devices in a mesh: body: 4 (over z), gx: 2 (over y), gy: 4 (over x, core).
Axes of the slice: x: 2, y: 2, z: 4, core: 2. Of those that a mesh axis runs over, the one named last changes fastest.
Arguments:
- load: float32 [64, 128, 512], P('body', 'gx', 'gy'), may hold values from -8 to 8
- stiffness: float32 [64, 128, 512], P('body', 'gx', 'gy'), may hold values from 0.1 to 3
- pair_code: int32 [4, 128, 512], P(None, 'gx', 'gy'), may hold values from 0 to 24
- pair_weight: float32 [4, 128, 512], P(None, 'gx', 'gy'), may hold values from 0.05 to 0.5
Outputs:
- solution: float32 [64, 128, 512], P('body', 'gx', 'gy')
- interface_load: float32 [64, 128, 512], P('body', 'gx', 'gy')
The draws below stay inside these ranges and needn't reach their ends.
Inputs may be any that keep to these rules, and one draw needn't show every extreme that they name: `pair_code`: entry k of slave node (i, j) ties it to the master node (i + c // 5 - 2, j + c % 5 - 2) of the top layer of the body below, c being the entry; the same pairing holds at every interface; masters outside the grid count as zero.
All inputs are finite; a program needn't handle non-finite values.
Results may differ from the reference program's by a relative error of at most 0.0001.
Values sent between devices are 32-bit elements; how exact they have to be, the bound alone decides.
No kernel may reach another device: no remote copies, remote signals or barrier semaphores. Data moves between devices by JAX's collectives and lax.ppermute only.
A program may use at most 64 MiB of HBM per device.

```python
import math
import jax
import jax.numpy as jnp

CZ = 16
REACH = 2
PAIRS = 4
UZAWA = 2
INNER = 3
NZ = 64
NX = 128
NY = 512


def plant(result, rng, smallest, largest):
    shape = result.shape
    place = [jax.random.randint(jax.random.fold_in(rng, axis), (), 0, shape[axis]) for axis in range(len(shape))]
    result = result.at[tuple(place)].set(smallest)
    longest = shape.index(max(shape))
    place[longest] = (place[longest] + 1) % shape[longest]
    return result.at[tuple(place)].set(largest)


def shard_levels(own_key, extent, split, smallest, top_value):
    def one(axis_at, parts):
        steps = jax.random.uniform(jax.random.fold_in(jax.random.fold_in(own_key, 6), axis_at), (parts,), jnp.float32, smallest / len(split), top_value / len(split))
        return jnp.repeat(jnp.exp(steps), extent[axis_at] // parts).reshape((-1,) + (1,) * (len(extent) - axis_at - 1))

    level = one(*split[0])
    for cut in split[1:]:
        level = level * one(*cut)
    return level


def scatter_about(key, dims, scale, bound, pieces=(), dtype=jnp.bfloat16):
    array = jax.random.normal(key, dims, jnp.float32) * scale
    if len(pieces) > 0:
        array = shard_levels(key, dims, pieces, -0.22, 0.18) * array
    return jnp.clip(array, min=-bound, max=bound).astype(dtype)


def setup_inputs(seed: int = 0) -> dict:
    keys = jax.random.split(jax.random.key(seed), 5)
    return {
        "load": scatter_about(keys[0], (NZ, NX, NY), 1.0, 8.0, ((0, 4), (1, 2), (2, 4)), jnp.float32),
        "stiffness": jnp.clip(jnp.exp(math.log(3.0) - 3.4011974 * jax.random.uniform(keys[1], (NZ, NX, NY), jnp.float32) ** shard_levels(keys[1], (NZ, NX, NY), ((0, 4), (1, 2), (2, 4)), -0.2, 0.2)), 0.1, 3.0),
        "pair_code": plant(jax.random.randint(keys[2], (PAIRS, NX, NY), 0, (2 * REACH + 1) ** 2), jax.random.fold_in(keys[2], 1), 0, ((2 * REACH + 1) ** 2) - 1).astype(jnp.int32),
        "pair_weight": jnp.clip(0.05 + 0.45 * jax.random.uniform(keys[3], (PAIRS, NX, NY), jnp.float32) ** shard_levels(keys[3], (PAIRS, NX, NY), ((1, 2), (2, 4)), -0.2, 0.2), 0.05, 0.5),
    }


RATE = 2.0


def apply_operator(vector, stiffness):
    padded = jnp.pad(vector, 1)
    layer_index = jnp.arange(vector.shape[0])[:, None, None]
    upper_term = jnp.where(layer_index % CZ == CZ - 1, 0.0, padded[2:, 1:-1, 1:-1])
    lower_term = jnp.where(layer_index % CZ == 0, 0.0, padded[:-2, 1:-1, 1:-1])
    beside = upper_term + lower_term + padded[1:-1, 2:, 1:-1] + padded[1:-1, :-2, 1:-1]
    beside = beside + padded[1:-1, 1:-1, 2:] + padded[1:-1, 1:-1, :-2]
    return (6.0 + stiffness) * vector - beside


def body_sums(first, second):
    bodies = first.shape[0] // CZ
    product = (first * second).reshape(bodies, CZ, -1)
    sums = jnp.sum(product, axis=(1, 2))
    return jnp.repeat(sums, CZ)[:, None, None]


def offset_table(codes, weights):
    offset_span = 2 * REACH + 1
    tables = []
    for offset in range(offset_span * offset_span):
        tables.append(jnp.sum(jnp.where(codes == offset, weights, 0.0), axis=0))
    return tables


def reference(load, stiffness, pair_code, pair_weight):
    offset_span = 2 * REACH + 1
    layers = load.shape[0]
    bodies = layers // CZ
    face_rows = load.shape[1]
    face_cols = load.shape[2]
    tables = offset_table(pair_code, pair_weight)
    multiplier = jnp.zeros((bodies - 1, face_rows, face_cols), jnp.float32)
    solution = jnp.zeros_like(load)
    interface_load = jnp.zeros_like(load)
    for outer_step in range(UZAWA):
        residual = load + interface_load - apply_operator(solution, stiffness)
        direction = residual
        norm_now = body_sums(residual, residual)
        for inner_step in range(INNER):
            image = apply_operator(direction, stiffness)
            alpha = norm_now / body_sums(direction, image)
            solution = solution + alpha * direction
            residual = residual - alpha * image
            norm_next = body_sums(residual, residual)
            direction = residual + (norm_next / norm_now) * direction
            norm_now = norm_next
        stacked = solution.reshape(bodies, CZ, face_rows, face_cols)
        master = jnp.pad(stacked[:-1, CZ - 1], ((0, 0), (REACH, REACH), (REACH, REACH)))
        slave = stacked[1:, 0]
        pulled = jnp.zeros_like(slave)
        for offset in range(offset_span * offset_span):
            shift_row = offset // offset_span - REACH
            shift_col = offset % offset_span - REACH
            window = master[:, REACH + shift_row:REACH + shift_row + face_rows, REACH + shift_col:REACH + shift_col + face_cols]
            pulled = pulled + tables[offset][None] * window
        multiplier = multiplier + RATE * (slave - pulled)
        force = jnp.zeros_like(slave)
        for offset in range(offset_span * offset_span):
            shift_row = offset // offset_span - REACH
            shift_col = offset % offset_span - REACH
            spread = jnp.pad(tables[offset][None] * multiplier, ((0, 0), (REACH, REACH), (REACH, REACH)))
            force = force + spread[:, REACH - shift_row:REACH - shift_row + face_rows, REACH - shift_col:REACH - shift_col + face_cols]
        shaped = jnp.zeros((bodies, CZ, face_rows, face_cols), jnp.float32)
        shaped = shaped.at[:-1, CZ - 1].set(force).at[1:, 0].set(-multiplier)
        interface_load = shaped.reshape(layers, face_rows, face_cols)
    return solution, interface_load
```

```python
import functools

import jax
import jax.numpy as jnp
from jax import lax
from jax.experimental import pallas as pl
from jax.experimental.pallas import tpu as pltpu
from jax.sharding import PartitionSpec as P

REACH = 2
SPAN = 2 * REACH + 1
RATE = 2.0
CENTRE = 7.5
SCALE = 4.0
LANES = 128
STRIP = 16
SLOTS = LANES // STRIP
MARGIN = 8
PAD = STRIP + MARGIN
F32 = jnp.float32
G = ("gx", "gy")
ALL = ("body", "gx", "gy")


def swaps_of(count):
    return () if count < 2 else (("A",) if count == 2 else ("A", "B"))


def swap_perm(kind, count):
    if kind == "":
        return [(i, i) for i in range(count)]
    step = 1 if kind == "A" else -1
    return [(i, (i + (step if i % 2 == 0 else -step)) % count) for i in range(count)]


def swap_up(kind, index):
    even = lax.rem(index, 2) == 0
    return even if kind == "A" else jnp.logical_not(even)


def swap_valid(kind, index, count):
    if kind == "A":
        return index >= 0
    return jnp.where(swap_up(kind, index), index < count - 1, index > 0)


def row_units(layers, pairs):
    wide_load = (0, 1, layers - 3, layers - 2, layers - 1)
    wide_stiff = (0, layers - 3, layers - 2, layers - 1)
    units = []
    for which, wide in ((0, wide_load), (1, wide_stiff)):
        for layer in range(layers):
            units.append((which, layer, False))
            if layer in wide:
                units.append((which, layer, True))
    for which in (2, 3):
        units += [(which, k, False) for k in range(pairs)]
    return units


def strip_list(layers, pairs):
    return [(w, k) for w in (0, 1) for k in range(layers)] + [(w, k) for w in (2, 3) for k in range(pairs)]


def lane_iota(rows):
    return lax.broadcasted_iota(jnp.int32, (rows, LANES), 1)


def aligned(start):
    return pl.multiple_of(start, 8)


class Plan:
    def __init__(self, mesh, layers, rows, pairs):
        self.nb, self.nx, self.ny = (mesh.shape[a] for a in ALL)
        self.layers, self.rows, self.pairs = layers, rows, pairs
        self.buf = rows + 2 * PAD
        self.units = row_units(layers, pairs)
        self.strips = strip_list(layers, pairs)
        self.sx, self.sy, self.sb = swaps_of(self.nx), swaps_of(self.ny), swaps_of(self.nb)
        self.face = rows + 16
        self.vec = (2, layers + 2, self.buf, LANES)


def pack_kernel(plan, load, stiff, code, weight, *outs):
    ix, iy = lax.axis_index("gx"), lax.axis_index("gy")
    refs = (load, stiff, code, weight)
    rows = plan.rows

    def take(which, k, start, size):
        return refs[which][k, pl.ds(start, size), :].astype(F32)

    def starts(kind):
        up = swap_up(kind, ix)
        near = aligned(jnp.where(up, rows - 8, 0))
        far = aligned(jnp.where(up, rows - 16, 8))
        return near, far

    def turn(kind, slot):
        up = swap_up(kind, iy)
        return jnp.where(up, (STRIP * slot + STRIP) % LANES, STRIP * slot)

    outs = list(outs)
    for kind in plan.sx:
        out = outs.pop(0)
        near, far = starts(kind)
        for u, (which, k, is_far) in enumerate(plan.units):
            out[u] = take(which, k, far if is_far else near, 8)
    slot_of = lane_iota(rows) // STRIP
    for kind in plan.sy:
        out = outs.pop(0)
        for tile in range(-(-len(plan.strips) // SLOTS)):
            total = jnp.zeros((rows, LANES), F32)
            for slot, (which, k) in enumerate(plan.strips[tile * SLOTS : (tile + 1) * SLOTS]):
                moved = pltpu.roll(take(which, k, 0, rows), turn(kind, slot), 1)
                total = jnp.where(slot_of == slot, moved, total)
            out[tile] = total
    slot_of = lane_iota(8) // STRIP
    for row_kind in plan.sx:
        near, far = starts(row_kind)
        for kind in plan.sy:
            out = outs.pop(0)
            for tile in range(-(-len(plan.units) // SLOTS)):
                total = jnp.zeros((8, LANES), F32)
                for slot, (which, k, is_far) in enumerate(plan.units[tile * SLOTS : (tile + 1) * SLOTS]):
                    moved = pltpu.roll(take(which, k, far if is_far else near, 8), turn(kind, slot), 1)
                    total = jnp.where(slot_of == slot, moved, total)
                out[tile] = total


def beside(first, second, lane):
    a, b = pltpu.roll(first, 1, 1), pltpu.roll(second, 1, 1)
    c, d = pltpu.roll(first, LANES - 1, 1), pltpu.roll(second, LANES - 1, 1)
    start, end = lane == 0, lane == LANES - 1
    return (
        jnp.where(start, b, a) + jnp.where(end, d, c),
        jnp.where(start, a, b) + jnp.where(end, c, d),
    )


def operate(src, diag, inside, layer, first, size, tiles=(0, 1)):
    lane = lane_iota(size)
    rows = pl.ds(first, size)
    middle = [src[t, layer + 1, rows, :] for t in (0, 1)]
    sides = beside(middle[0], middle[1], lane)
    done = []
    for t in tiles:
        total = sides[t] + src[t, layer + 1, pl.ds(first - 1, size), :]
        total = total + src[t, layer + 1, pl.ds(first + 1, size), :]
        total = total + src[t, layer, rows, :] + src[t, layer + 2, rows, :]
        done.append(diag[t, layer, rows, :] * middle[t] - inside[t, rows, :] * total)
    return done


def chunks(first, size, step):
    return [(at, min(step, first + size - at)) for at in range(first, first + size, step)]


def clear_frame(plan, vec):
    zero = jnp.zeros((16, LANES), F32)
    for t in (0, 1):
        for edge in (0, plan.layers + 1):
            vec[t, edge] = jnp.zeros((plan.buf, LANES), F32)

    def one(layer, carry):
        for t in (0, 1):
            vec[t, layer, pl.ds(0, 16), :] = zero
            vec[t, layer, pl.ds(plan.buf - 16, 16), :] = zero
        return carry

    lax.fori_loop(1, plan.layers + 1, one, 0)


def fill_inside(plan, inside):
    ix, iy = lax.axis_index("gx"), lax.axis_index("gy")
    row = lax.broadcasted_iota(jnp.int32, (plan.buf, LANES), 0) + ix * plan.rows - PAD
    lane = lane_iota(plan.buf)
    in_rows = jnp.logical_and(row >= 0, row < plan.nx * plan.rows)
    right = jnp.logical_and(lane < STRIP, iy < plan.ny - 1)
    left = jnp.logical_and(lane >= LANES - STRIP, iy > 0)
    inside[0] = jnp.where(in_rows, 1.0 / SCALE, 0.0)
    inside[1] = jnp.where(jnp.logical_and(in_rows, jnp.logical_or(right, left)), 1.0 / SCALE, 0.0)


def six_sums(parts):
    lane = lax.broadcasted_iota(jnp.int32, (1, LANES), 1)
    row = jnp.zeros((1, LANES), F32)
    for k, part in enumerate(parts):
        row = jnp.where(lane == k, jnp.sum(part), row)
    return row


def fold(value):
    return jnp.sum(value.reshape(-1, 8, LANES), axis=0)


def last_step(plan, vecs, diag, inside, store):
    own = pl.ds(PAD, plan.rows)

    def one(layer, sums):
        if store is not None:
            for first, size in chunks(PAD - 8, plan.face, 40):
                for t, value in enumerate(operate(vecs[2], diag, inside, layer, first, size)):
                    store[t, layer + 1, pl.ds(first, size), :] = value
            top = store[0, layer + 1, own, :]
        else:
            top = operate(vecs[2], diag, inside, layer, PAD, plan.rows, (0,))[0]
        v0, v1, v2 = (v[0, layer + 1, own, :] for v in vecs)
        pairs = ((v0, v0), (v0, v1), (v1, v1), (v1, v2), (v2, v2), (v2, top))
        return tuple(s + fold(a * b) for s, (a, b) in zip(sums, pairs))

    zero = jnp.zeros((8, LANES), F32)
    return six_sums(lax.fori_loop(0, plan.layers, one, (zero,) * 6))


def put_faces(plan, vecs, outs):
    ib = lax.axis_index("body")
    lane = lane_iota(plan.face)
    rows = pl.ds(PAD - 8, plan.face)
    for kind, out in zip(plan.sb, outs):
        layer = jnp.where(swap_up(kind, ib), plan.layers, 1)
        packed = jnp.zeros((plan.face, LANES), F32)
        for k in range(3):
            out[k] = vecs[k][0, layer, rows, :]
            moved = pltpu.roll(vecs[k][1, layer, rows, :], STRIP + 2 * STRIP * k, 1)
            packed = jnp.where(lane // (2 * STRIP) == k, moved, packed)
        out[3] = packed


def get_faces(plan, msgs, coefs):
    ib = lax.axis_index("body")
    lane = lane_iota(plan.face)
    strips = jnp.logical_or(lane < STRIP, lane >= LANES - STRIP)
    sides = []
    for up, coef in zip((True, False), coefs):
        total = [jnp.zeros((plan.face, LANES), F32)] * 2
        for kind, msg in zip(plan.sb, msgs):
            use = jnp.logical_and(swap_up(kind, ib) == up, swap_valid(kind, ib, plan.nb))
            own = sum(coef[k] * msg[k] for k in range(3))
            strip = sum(coef[k] * pltpu.roll(msg[3], (LANES - STRIP - 2 * STRIP * k) % LANES, 1) for k in range(3))
            total[0] = jnp.where(use, own, total[0])
            total[1] = jnp.where(jnp.logical_and(use, strips), strip, total[1])
        sides.append(total)
    return sides


def krylov_kernel(plan, load, stiff, code, weight, *refs):
    refs = list(refs)
    take = lambda n: [refs.pop(0) for _ in range(n)]
    row_msgs, lane_msgs = take(len(plan.sx)), take(len(plan.sy))
    corner_msgs = take(len(plan.sx) * len(plan.sy))
    moments, = take(1)
    faces = take(len(plan.sb))
    basis = take(4)
    diag, inside, tables = take(3)
    pairing, = take(1)
    ix, iy = lax.axis_index("gx"), lax.axis_index("gy")
    rows, layers, buf = plan.rows, plan.layers, plan.buf
    own = pl.ds(PAD, rows)
    b0 = basis[0]

    def cell(which, k, t, where):
        if which == 0:
            return b0.at[t, k + 1, where, :]
        if which == 1:
            return diag.at[t, k, where, :]
        return pairing.at[which - 2, k, t, where, :]

    clear_frame(plan, b0)
    clear_frame(plan, basis[1])
    clear_frame(plan, basis[2])
    for edge in (0, layers + 1):
        for t in (0, 1):
            basis[3][t, edge] = jnp.zeros((buf, LANES), F32)
    fill_inside(plan, inside)

    zero = jnp.zeros((PAD, LANES), F32)
    sources = (load, stiff, code, weight)
    for which, k in plan.strips:
        cell(which, k, 0, own)[...] = sources[which][k].astype(F32)
        for t in (0, 1):
            cell(which, k, t, pl.ds(0, PAD))[...] = zero
            cell(which, k, t, pl.ds(buf - PAD, PAD))[...] = zero

    for kind, msg in zip(plan.sx, row_msgs):
        up, ok = swap_up(kind, ix), swap_valid(kind, ix, plan.nx)
        near = aligned(jnp.where(up, PAD + rows, PAD - 8))
        far = aligned(jnp.where(up, PAD + rows + 8, PAD - 16))
        for u, (which, k, is_far) in enumerate(plan.units):
            cell(which, k, 0, pl.ds(far if is_far else near, 8))[...] = jnp.where(ok, msg[u], 0.0)

    def place(kind):
        up, ok = swap_up(kind, iy), swap_valid(kind, iy, plan.ny)
        return up, ok

    def unpack(size, pieces):
        lane = lane_iota(size)
        total = jnp.zeros((size, LANES), F32)
        for kind, value, slot in pieces:
            up, ok = place(kind)
            turn = jnp.where(up, (LANES - STRIP * slot) % LANES, (2 * LANES - STRIP - STRIP * slot) % LANES)
            lo = jnp.where(up, 0, LANES - STRIP)
            use = jnp.logical_and(jnp.logical_and(lane >= lo, lane < lo + STRIP), ok)
            total = jnp.where(use, pltpu.roll(value, turn, 1), total)
        return total

    for j, (which, k) in enumerate(plan.strips):
        pieces = [(kind, msg[j // SLOTS], j % SLOTS) for kind, msg in zip(plan.sy, lane_msgs)]
        cell(which, k, 1, own)[...] = unpack(rows, pieces)
    for i, row_kind in enumerate(plan.sx):
        up, ok = swap_up(row_kind, ix), swap_valid(row_kind, ix, plan.nx)
        near = aligned(jnp.where(up, PAD + rows, PAD - 8))
        far = aligned(jnp.where(up, PAD + rows + 8, PAD - 16))
        msgs = corner_msgs[i * len(plan.sy) : (i + 1) * len(plan.sy)]
        for u, (which, k, is_far) in enumerate(plan.units):
            pieces = [(kind, msg[u // SLOTS], u % SLOTS) for kind, msg in zip(plan.sy, msgs)]
            value = jnp.where(ok, unpack(8, pieces), 0.0)
            cell(which, k, 1, pl.ds(far if is_far else near, 8))[...] = value

    def scale(layer, carry):
        for t in (0, 1):
            diag[t, layer] = (diag[t, layer] + (6.0 - CENTRE)) * (1.0 / SCALE)
        return carry

    lax.fori_loop(0, layers, scale, 0)

    for step, wide in ((0, (0, layers - 2, layers - 1)), (1, (layers - 1,))):
        src, dst = basis[step], basis[step + 1]

        def one(layer, carry):
            for first, size in chunks(PAD - 8, plan.face, 40):
                for t, value in enumerate(operate(src, diag, inside, layer, first, size)):
                    dst[t, layer + 1, pl.ds(first, size), :] = value
            return carry

        lax.fori_loop(0, layers, one, 0)
        for layer in wide:
            for first in (PAD - 16, PAD + rows + 8):
                for t, value in enumerate(operate(src, diag, inside, layer, first, 8)):
                    dst[t, layer + 1, pl.ds(first, 8), :] = value

    put_faces(plan, basis, faces)
    row = last_step(plan, basis[:3], diag, inside, basis[3])
    moments[...] = jnp.broadcast_to(row.reshape(1, 1, LANES), moments.shape)

    for t in (0, 1):
        for first, size in chunks(PAD - 8, plan.face, 40):
            span = pl.ds(first, size)
            codes = [pairing[0, k, t, span, :] for k in range(plan.pairs)]
            weights = [pairing[1, k, t, span, :] for k in range(plan.pairs)]
            for offset in range(SPAN * SPAN):
                total = jnp.where(codes[0] == offset, weights[0], 0.0)
                for k in range(1, plan.pairs):
                    total = total + jnp.where(codes[k] == offset, weights[k], 0.0)
                tables[offset, t, span, :] = total
        for offset in range(SPAN * SPAN):
            tables[offset, t, pl.ds(PAD - 16, 8), :] = jnp.zeros((8, LANES), F32)
            tables[offset, t, pl.ds(PAD + rows + 8, 8), :] = jnp.zeros((8, LANES), F32)


def solve(plan, moments):
    per = plan.nx * plan.ny
    body = lax.broadcasted_iota(jnp.int32, (plan.nb, LANES), 0)
    table = jnp.zeros((plan.nb, LANES), F32)
    for b in range(plan.nb):
        row = moments[b * per]
        for i in range(1, per):
            row = row + moments[b * per + i]
        table = jnp.where(body == b, row, table)
    lane = lax.broadcasted_iota(jnp.int32, (plan.nb, LANES), 1)
    m = [
        jnp.broadcast_to(jnp.sum(jnp.where(lane == k, table, 0.0), axis=1, keepdims=True), table.shape)
        for k in range(6)
    ]
    h = [SCALE * m[n + 1] + CENTRE * m[n] for n in range(5)]
    f1, f2 = h[1] / h[0], h[2] / h[0]
    d1 = h[2] - f1 * h[1]
    e = h[3] - f1 * h[2]
    d2 = h[4] - f2 * h[2]
    f3 = e / d1
    d2 = d2 - f3 * e
    g1 = m[1] - f1 * m[0]
    g2 = m[2] - f2 * m[0] - f3 * g1
    c2 = g2 / d2
    c1 = (g1 - e * c2) / d1
    c0 = (m[0] - h[1] * c1 - h[2] * c2) / h[0]

    def pick(index):
        return [jnp.sum(jnp.where(body == index, c, 0.0), axis=0, keepdims=True) for c in (c0, c1, c2)]

    ib = lax.axis_index("body")
    return pick(ib), pick(ib + 1), pick(ib - 1)


def lane_shift(first, second, by, lane):
    if by == 0:
        return first, second
    a, b = pltpu.roll(first, (-by) % LANES, 1), pltpu.roll(second, (-by) % LANES, 1)
    keep = lane < LANES - by if by > 0 else lane >= -by
    return jnp.where(keep, a, b), jnp.where(keep, b, a)


def put_shifted(shifted, first, size, planes):
    lane = lane_iota(size)
    for i in range(SPAN):
        for t, value in enumerate(lane_shift(planes[0], planes[1], i - REACH, lane)):
            shifted[i, t, pl.ds(first, size), :] = value


def pull(tables, shifted, t, first, size):
    total = jnp.zeros((size, LANES), F32)
    for offset in range(SPAN * SPAN):
        window = shifted[offset % SPAN, t, pl.ds(first + offset // SPAN - REACH, size), :]
        total = total + tables[offset, t, pl.ds(first, size), :] * window
    return total


def push(tables, face, first, size):
    lane = lane_iota(size)
    total = [jnp.zeros((size, LANES), F32)] * 2
    for i in range(SPAN):
        column = [jnp.zeros((size, LANES), F32)] * 2
        for j in range(SPAN):
            window = pl.ds(first - (j - REACH), size)
            for t in (0, 1):
                column[t] = column[t] + tables[j * SPAN + i, t, window, :] * face[t, window, :]
        moved = lane_shift(column[0], column[1], REACH - i, lane)
        total = [total[t] + moved[t] for t in (0, 1)]
    return total


def middle_kernel(plan, moments_in, *refs):
    refs = list(refs)
    take = lambda n: [refs.pop(0) for _ in range(n)]
    msgs = take(len(plan.sb))
    basis = take(4)
    diag, inside, tables = take(3)
    moments, = take(1)
    faces = take(len(plan.sb))
    vecs = take(3)
    solution, planes, multiplier = take(3)
    shifted, = take(1)
    ib = lax.axis_index("body")
    rows, layers, buf = plan.rows, plan.layers, plan.buf
    has_above, has_below = ib < plan.nb - 1, ib > 0
    own_coef, above_coef, below_coef = solve(plan, moments_in)
    c0, c1, c2 = own_coef
    rest = (
        1.0 - CENTRE * c0,
        -(SCALE * c0 + CENTRE * c1),
        -(SCALE * c1 + CENTRE * c2),
        -(SCALE * c2),
    )
    face = pl.ds(PAD - 8, plan.face)
    wide = pl.ds(PAD - 16, plan.face + 16)
    own = pl.ds(PAD, rows)

    for i in range(3):
        clear_frame(plan, vecs[i])

    def combine(layer, carry):
        solution[layer] = sum(c * v[0, layer + 1, own, :] for c, v in zip(own_coef, basis))
        for t in (0, 1):
            for first, size in chunks(PAD - 8, plan.face, 40):
                span = pl.ds(first, size)
                vecs[0][t, layer + 1, span, :] = sum(d * v[t, layer + 1, span, :] for d, v in zip(rest, basis))
        return carry

    lax.fori_loop(0, layers, combine, 0)

    top = [sum(c * v[t, layers, wide, :] for c, v in zip(own_coef, basis)) for t in (0, 1)]
    for t in (0, 1):
        planes[0, t, wide, :] = top[t]
    put_shifted(shifted, PAD - 16, plan.face + 16, top)
    above, below = get_faces(plan, msgs, (above_coef, below_coef))
    edge = jnp.zeros((8, LANES), F32)
    for t in (0, 1):
        planes[1, t, face, :] = above[t]
        multiplier[0, t, pl.ds(PAD - 16, 8), :] = edge
        multiplier[0, t, pl.ds(PAD + rows + 8, 8), :] = edge
        for first, size in chunks(PAD - 8, plan.face, 40):
            gap = planes[1, t, pl.ds(first, size), :] - pull(tables, shifted, t, first, size)
            multiplier[0, t, pl.ds(first, size), :] = jnp.where(has_above, RATE * gap, 0.0)

    for t in (0, 1):
        planes[2, t, face, :] = sum(c * v[t, 1, face, :] for c, v in zip(own_coef, basis))
        planes[3, t, face, :] = below[t]
        for i in range(SPAN):
            shifted[i, t, pl.ds(PAD - 16, 8), :] = edge
            shifted[i, t, pl.ds(PAD + rows + 8, 8), :] = edge
    put_shifted(shifted, PAD - 8, plan.face, below)
    for t in (0, 1):
        for first, size in chunks(PAD - 8, plan.face, 40):
            span = pl.ds(first, size)
            gap = planes[2, t, span, :] - pull(tables, shifted, t, first, size)
            gap = jnp.where(has_below, RATE * gap, 0.0)
            multiplier[1, t, span, :] = gap
            vecs[0][t, 1, span, :] = vecs[0][t, 1, span, :] - gap
    for first, size in chunks(PAD - 8, plan.face, 40):
        force = push(tables, multiplier.at[0], first, size)
        for t in (0, 1):
            span = pl.ds(first, size)
            pushed = force[t] * (SCALE * inside[t, span, :])
            vecs[0][t, layers, span, :] = vecs[0][t, layers, span, :] + pushed

    for step in range(2):
        src, dst = vecs[step], vecs[step + 1]

        def one(layer, carry):
            for first, size in chunks(PAD - 8, plan.face, 40):
                for t, value in enumerate(operate(src, diag, inside, layer, first, size)):
                    dst[t, layer + 1, pl.ds(first, size), :] = value
            return carry

        lax.fori_loop(0, layers, one, 0)

    put_faces(plan, vecs, faces)
    row = last_step(plan, vecs, diag, inside, None)
    moments[...] = jnp.broadcast_to(row.reshape(1, 1, LANES), moments.shape)


def final_kernel(plan, moments_in, *refs):
    refs = list(refs)
    take = lambda n: [refs.pop(0) for _ in range(n)]
    msgs = take(len(plan.sb))
    vecs = take(3)
    first_solution, planes, multiplier, tables = take(4)
    solution, interface = take(2)
    shifted, lifted = take(2)
    ib = lax.axis_index("body")
    rows, layers = plan.rows, plan.layers
    has_above, has_below = ib < plan.nb - 1, ib > 0
    own_coef, above_coef, below_coef = solve(plan, moments_in)
    own = pl.ds(PAD, rows)
    face = pl.ds(PAD - 8, plan.face)

    def combine(layer, carry):
        solution[layer] = first_solution[layer] + sum(c * v[0, layer + 1, own, :] for c, v in zip(own_coef, vecs))
        interface[layer] = jnp.zeros((rows, LANES), F32)
        return carry

    lax.fori_loop(0, layers, combine, 0)
    above, below = get_faces(plan, msgs, (above_coef, below_coef))
    edge = jnp.zeros((8, LANES), F32)
    for t in (0, 1):
        lifted[t, pl.ds(PAD - 16, 8), :] = edge
        lifted[t, pl.ds(PAD + rows + 8, 8), :] = edge
        for i in range(SPAN):
            shifted[i, t, pl.ds(PAD - 16, 8), :] = edge
            shifted[i, t, pl.ds(PAD + rows + 8, 8), :] = edge
    top = [
        planes[0, t, face, :] + sum(c * v[t, layers, face, :] for c, v in zip(own_coef, vecs)) for t in (0, 1)
    ]
    put_shifted(shifted, PAD - 8, plan.face, top)
    for t in (0, 1):
        lifted[t, face, :] = planes[1, t, face, :] + above[t]
        for first, size in chunks(PAD - 8, plan.face, 40):
            span = pl.ds(first, size)
            gap = lifted[t, span, :] - pull(tables, shifted, t, first, size)
            lifted[t, span, :] = multiplier[0, t, span, :] + jnp.where(has_above, RATE * gap, 0.0)
    interface[layers - 1] = push(tables, lifted, PAD, rows)[0]
    put_shifted(shifted, PAD - 8, plan.face, [planes[3, t, face, :] + below[t] for t in (0, 1)])
    bottom = planes[2, 0, own, :] + sum(c * v[0, 1, own, :] for c, v in zip(own_coef, vecs))
    gap = bottom - pull(tables, shifted, 0, PAD, rows)
    interface[0] = -(multiplier[1, 0, own, :] + jnp.where(has_below, RATE * gap, 0.0))


def shaped(*shape):
    return jax.ShapeDtypeStruct(shape, F32)


def held(*shape):
    return pltpu.VMEM(shape, F32)


def call(kernel, args, outs, scratch, name):
    vmem = pl.BlockSpec(memory_space=pltpu.VMEM)
    return pl.pallas_call(
        kernel,
        out_shape=tuple(outs),
        in_specs=[vmem] * len(args),
        out_specs=(vmem,) * len(outs),
        scratch_shapes=scratch,
        compiler_params=pltpu.CompilerParams(vmem_limit_bytes=20 * 1024 * 1024),
        name=name,
    )(*args)


def per_device(mesh, load, stiffness, pair_code, pair_weight):
    layers, rows, lanes = load.shape
    pairs = pair_code.shape[0]
    assert lanes == LANES and rows % 8 == 0 and rows >= 16
    plan = Plan(mesh, layers, rows, pairs)
    nb, nx, ny = plan.nb, plan.nx, plan.ny
    count = nb * nx * ny
    inputs = (load, stiffness, pair_code, pair_weight)

    def lateral(row_kind, lane_kind, array):
        a, b = swap_perm(row_kind, nx), swap_perm(lane_kind, ny)
        return lax.ppermute(array, G, [(i * ny + j, a[i][1] * ny + b[j][1]) for i in range(nx) for j in range(ny)])

    kinds = [(k, "") for k in plan.sx] + [("", k) for k in plan.sy] + [(a, b) for a in plan.sx for b in plan.sy]
    tiles = -(-len(plan.units) // SLOTS)
    shapes = [shaped(len(plan.units), 8, LANES) for _ in plan.sx]
    shapes += [shaped(-(-len(plan.strips) // SLOTS), rows, LANES) for _ in plan.sy]
    shapes += [shaped(tiles, 8, LANES) for _ in plan.sx for _ in plan.sy]
    packed = call(functools.partial(pack_kernel, plan), inputs, shapes, [], "pack")
    halos = [lateral(a, b, m) for (a, b), m in zip(kinds, packed)]

    def spread(moments, faces):
        faces = [lax.ppermute(f, "body", swap_perm(k, nb)) for k, f in zip(plan.sb, faces)]
        return lax.all_to_all(moments, ALL, 0, 0, tiled=True), faces

    nf = len(plan.sb)
    messages = [shaped(count, 1, LANES)] + [shaped(4, plan.face, LANES)] * nf
    vec = held(*plan.vec)
    tables = held(SPAN * SPAN, 2, plan.buf, LANES)
    first = call(
        functools.partial(krylov_kernel, plan),
        (*inputs, *halos),
        messages + [vec] * 4 + [held(2, layers, plan.buf, LANES), held(2, plan.buf, LANES), tables],
        [pltpu.VMEM((2, pairs, 2, plan.buf, LANES), F32)],
        "krylov",
    )
    moments, faces, basis = first[0], first[1 : 1 + nf], first[1 + nf : 5 + nf]
    diag, inside, table = first[5 + nf :]
    moments, faces = spread(moments, faces)
    planes = held(4, 2, plan.buf, LANES)
    second = call(
        functools.partial(middle_kernel, plan),
        (moments, *faces, *basis, diag, inside, table),
        messages + [vec] * 3 + [held(layers, rows, LANES), planes, held(2, 2, plan.buf, LANES)],
        [pltpu.VMEM((SPAN, 2, plan.buf, LANES), F32)],
        "middle",
    )
    moments, faces, vecs = second[0], second[1 : 1 + nf], second[1 + nf : 4 + nf]
    sol, kept, multiplier = second[4 + nf :]
    moments, faces = spread(moments, faces)
    return call(
        functools.partial(final_kernel, plan),
        (moments, *faces, *vecs, sol, kept, multiplier, table),
        [shaped(layers, rows, LANES)] * 2,
        [pltpu.VMEM((SPAN, 2, plan.buf, LANES), F32), pltpu.VMEM((2, plan.buf, LANES), F32)],
        "final",
    )


def solution(mesh):
    return jax.shard_map(
        functools.partial(per_device, mesh),
        mesh=mesh,
        in_specs=(P("body", "gx", "gy"), P("body", "gx", "gy"), P(None, "gx", "gy"), P(None, "gx", "gy")),
        out_specs=(P("body", "gx", "gy"), P("body", "gx", "gy")),
        check_vma=False,
    )
```

```python
import functools

import jax
import jax.numpy as jnp
from jax import lax
from jax.experimental import pallas as pl
from jax.experimental.pallas import tpu as pltpu
from jax.sharding import PartitionSpec as P


REACH = 2
SPAN = 2 * REACH + 1
RATE = 2.0
CENTRE = 7.5
LANES = 128
STRIP = 16
SLOTS = LANES // STRIP
PAD = 24
ORDER = 3
F32 = jnp.float32
G = ("gx", "gy")
ALL = ("body", "gx", "gy")


def swaps_of(count):
    return () if count < 2 else (("A",) if count == 2 else ("A", "B"))


def swap_perm(kind, count):
    if kind == "":
        return [(i, i) for i in range(count)]
    step = 1 if kind == "A" else -1
    return [(i, (i + (step if i % 2 == 0 else -step)) % count) for i in range(count)]


def swap_up(kind, index):
    even = lax.rem(index, 2) == 0
    return even if kind == "A" else jnp.logical_not(even)


def swap_valid(kind, index, count):
    if kind == "A":
        return index >= 0
    return jnp.where(swap_up(kind, index), index < count - 1, index > 0)


def row_units(layers, pairs):
    wide_load = (0, 1, layers - 3, layers - 2, layers - 1)
    wide_stiff = (0, layers - 3, layers - 2, layers - 1)
    units = []
    for which, wide in ((0, wide_load), (1, wide_stiff)):
        for layer in range(layers):
            units.append((which, layer, False))
            if layer in wide:
                units.append((which, layer, True))
    for which in (2, 3):
        units += [(which, k, False) for k in range(pairs)]
    return units


def strip_list(layers, pairs):
    return [(w, k) for w in (0, 1) for k in range(layers)] + [(w, k) for w in (2, 3) for k in range(pairs)]


def lane_iota(rows):
    return lax.broadcasted_iota(jnp.int32, (rows, LANES), 1)


def aligned(start):
    return pl.multiple_of(start, 8)


def chunks(first, size, step):
    return [(at, min(step, first + size - at)) for at in range(first, first + size, step)]


class Plan:
    def __init__(self, mesh, layers, rows, pairs):
        self.nb, self.nx, self.ny = (mesh.shape[a] for a in ALL)
        self.layers, self.rows, self.pairs = layers, rows, pairs
        self.buf = rows + 2 * PAD
        self.units = row_units(layers, pairs)
        self.strips = strip_list(layers, pairs)
        self.sx, self.sy, self.sb = swaps_of(self.nx), swaps_of(self.ny), swaps_of(self.nb)
        self.face = rows + 16
        self.vec = (2, layers + 2, self.buf, LANES)
        self.own = pl.ds(PAD, rows)
        self.near = pl.ds(PAD - 8, self.face)
        self.unit_tiles = -(-len(self.units) // SLOTS)
        self.strip_tiles = -(-len(self.strips) // SLOTS)


class Args:
    def __init__(self, refs):
        self.refs = list(refs)

    def take(self, count):
        got, self.refs = self.refs[:count], self.refs[count:]
        return got

    def one(self):
        return self.refs.pop(0)


def pack_kernel(plan, load, stiff, code, weight, *refs):
    args = Args(refs)
    b0, diag, codes, weights = args.take(4)
    row_out, lane_out = args.take(len(plan.sx)), args.take(len(plan.sy))
    corner_out = args.take(len(plan.sx) * len(plan.sy))
    sems = args.one()
    ix, iy = lax.axis_index("gx"), lax.axis_index("gy")
    rows, layers = plan.rows, plan.layers
    places = (b0.at[0, pl.ds(1, layers), plan.own, :], diag.at[0, :, plan.own, :], codes, weights)
    copies = [
        pltpu.make_async_copy(src, dst, sems.at[i]) for i, (src, dst) in enumerate(zip((load, stiff, code, weight), places))
    ]
    for copy in copies:
        copy.start()
    arrived = set()

    def take(which, k, start, size):
        if which not in arrived:
            copies[which].wait()
            arrived.add(which)
        if which == 0:
            return b0[0, k + 1, pl.ds(PAD + start, size), :]
        if which == 1:
            return diag[0, k, pl.ds(PAD + start, size), :]
        return (codes, weights)[which - 2][k, pl.ds(start, size), :].astype(F32)

    def starts(kind):
        up = swap_up(kind, ix)
        return aligned(jnp.where(up, rows - 8, 0)), aligned(jnp.where(up, rows - 16, 8))

    def gather(pieces, size, tile, outs):
        slot_of = lane_iota(size) // STRIP
        last, first = jnp.zeros((size, LANES), F32), jnp.zeros((size, LANES), F32)
        for slot, value in enumerate(pieces):
            moved = pltpu.roll(value, STRIP * (slot + 1) % LANES, 1) if slot + 1 < SLOTS else value
            last = jnp.where(slot_of == slot, moved, last)
            first = jnp.where(slot_of == (slot + 1) % SLOTS, moved, first)
        for kind, out in zip(plan.sy, outs):
            out[tile] = jnp.where(swap_up(kind, iy), last, first)

    for kind, out in zip(plan.sx, row_out):
        near, far = starts(kind)
        for u, (which, k, is_far) in enumerate(plan.units):
            out[u] = take(which, k, far if is_far else near, 8)
    for tile in range(plan.strip_tiles):
        members = plan.strips[tile * SLOTS : (tile + 1) * SLOTS]
        gather([take(which, k, 0, rows) for which, k in members], rows, tile, lane_out)
    for i, row_kind in enumerate(plan.sx):
        near, far = starts(row_kind)
        outs = corner_out[i * len(plan.sy) : (i + 1) * len(plan.sy)]
        for tile in range(plan.unit_tiles):
            members = plan.units[tile * SLOTS : (tile + 1) * SLOTS]
            gather([take(which, k, far if is_far else near, 8) for which, k, is_far in members], 8, tile, outs)


def clear_frame(plan, vec):
    zero = jnp.zeros((16, LANES), F32)
    for t in (0, 1):
        for edge in (0, plan.layers + 1):
            vec[t, edge] = jnp.zeros((plan.buf, LANES), F32)
        for layer in range(1, plan.layers + 1):
            vec[t, layer, pl.ds(0, 16), :] = zero
            vec[t, layer, pl.ds(plan.buf - 16, 16), :] = zero


def table_rows(plan, pairing, t, first, size, place):
    span = pl.ds(first, size)
    codes = [pairing[0, k, t, span, :] for k in range(plan.pairs)]
    weights = [pairing[1, k, t, span, :] for k in range(plan.pairs)]
    for offset in range(SPAN * SPAN):
        total = jnp.where(codes[0] == offset, weights[0], 0.0)
        for k in range(1, plan.pairs):
            total = total + jnp.where(codes[k] == offset, weights[k], 0.0)
        place(offset)[...] = total


def fill_inside(plan, inside):
    ix, iy = lax.axis_index("gx"), lax.axis_index("gy")
    rows, buf = plan.rows, plan.buf
    row = lax.broadcasted_iota(jnp.int32, (buf, LANES), 0) + ix * rows - PAD
    lane = lane_iota(buf)
    in_rows = jnp.logical_and(row >= 0, row < plan.nx * rows)
    right = jnp.logical_and(lane < STRIP, iy < plan.ny - 1)
    left = jnp.logical_and(lane >= LANES - STRIP, iy > 0)
    inside[0] = jnp.where(in_rows, 1.0, 0.0)
    inside[1] = jnp.where(jnp.logical_and(in_rows, jnp.logical_or(right, left)), 1.0, 0.0)


def prepare_kernel(plan, b0_in, diag_in, codes, weights, b0, diag, pairing, inside, b1, b2, tables_out, tables, sem):
    del b0_in, diag_in
    rows, layers, buf = plan.rows, plan.layers, plan.buf
    for k in range(plan.pairs):
        pairing[0, k, 0, plan.own, :] = codes[k].astype(F32)
        pairing[1, k, 0, plan.own, :] = weights[k]
    for first, size in chunks(PAD, rows, 32):
        table_rows(plan, pairing, 0, first, size, lambda o: tables.at[o, pl.ds(first - PAD, size), :])
    copy = pltpu.make_async_copy(tables, tables_out, sem)
    copy.start()
    fill_inside(plan, inside)
    zero = jnp.zeros((PAD, LANES), F32)
    for t in (0, 1):
        for span in (pl.ds(0, PAD), pl.ds(buf - PAD, PAD)):
            for layer in range(layers):
                b0[t, layer + 1, span, :] = zero
                diag[t, layer, span, :] = zero
            for k in range(plan.pairs):
                for i in (0, 1):
                    pairing[i, k, t, span, :] = zero
        for edge in (0, layers + 1):
            b0[t, edge] = jnp.zeros((buf, LANES), F32)
    clear_frame(plan, b1)
    clear_frame(plan, b2)
    for layer in range(layers):
        diag[0, layer, plan.own, :] = diag[0, layer, plan.own, :] + (6.0 - CENTRE)
    copy.wait()


def operate(src, at, diag, layer, inside, first, size, tiles=(0, 1), masked=True):
    lane = lane_iota(size)
    start, end = lane == 0, lane == LANES - 1
    rows = pl.ds(first, size)
    middle = [src[t, at, rows, :] for t in (0, 1)]
    before = [pltpu.roll(m, 1, 1) for m in middle]
    after = [pltpu.roll(m, LANES - 1, 1) for m in middle]
    done = []
    for t in tiles:
        total = jnp.where(start, before[1 - t], before[t]) + jnp.where(end, after[1 - t], after[t])
        total = total + src[t, at, pl.ds(first - 1, size), :]
        total = total + src[t, at, pl.ds(first + 1, size), :]
        total = total + (src[t, at - 1, rows, :] + src[t, at + 1, rows, :])
        if masked or t == 1:
            total = total * inside[t, rows, :]
        done.append(diag[t, layer, rows, :] * middle[t] - total)
    return done


def apply_near(plan, src, dst, at, diag, layer, inside):
    parts = [(PAD - 8, 8, True), (PAD + plan.rows, 8, True)]
    parts += [(first, size, False) for first, size in chunks(PAD, plan.rows, 32)]
    values = [
        (first, size, operate(src, at, diag, layer, inside, first, size, masked=masked)) for first, size, masked in parts
    ]
    for first, size, pair in values:
        for t in (0, 1):
            dst[t, at, pl.ds(first, size), :] = pair[t]


def apply_all(plan, src, dst, diag, inside):
    def one(layer, carry):
        apply_near(plan, src, dst, layer + 1, diag, layer, inside)
        return carry

    lax.fori_loop(0, plan.layers, one, 0)


def apply_own(plan, src, at, diag, layer, inside):
    parts = [
        operate(src, at, diag, layer, inside, first, size, (0,), False)[0] for first, size in chunks(PAD, plan.rows, 32)
    ]
    return jnp.concatenate(parts, axis=0)


def six_sums(parts):
    lane = lax.broadcasted_iota(jnp.int32, (1, LANES), 1)
    row = jnp.zeros((1, LANES), F32)
    for k, part in enumerate(parts):
        row = jnp.where(lane == k, jnp.sum(part), row)
    return row


def fold(value):
    return jnp.sum(value.reshape(-1, 8, LANES), axis=0)


def add_products(sums, v):
    pairs = ((v[0], v[0]), (v[0], v[1]), (v[1], v[1]), (v[1], v[2]), (v[2], v[2]), (v[2], v[3]))
    return tuple(s + fold(a * b) for s, (a, b) in zip(sums, pairs))


def put_moments(moments, sums):
    moments[...] = jnp.broadcast_to(six_sums(sums).reshape(1, 1, LANES), moments.shape)


def no_sums():
    return (jnp.zeros((8, LANES), F32),) * 6


def krylov_kernel(plan, *refs):
    args = Args(refs)
    row_msgs, lane_msgs = args.take(len(plan.sx)), args.take(len(plan.sy))
    corner_msgs = args.take(len(plan.sx) * len(plan.sy))
    inside = args.one()
    args.take(5)
    moments, b0, diag, b1, b2, pairing = args.take(6)
    kept = args.take(5)
    sems = args.one()
    copies = [
        pltpu.make_async_copy(src, dst, sems.at[i]) for i, (src, dst) in enumerate(zip((b0, diag, pairing, b1, b2), kept))
    ]
    ix, iy = lax.axis_index("gx"), lax.axis_index("gy")
    rows, layers = plan.rows, plan.layers

    def put(which, k, t, where, value):
        if which == 0:
            b0[t, k + 1, where, :] = value
        elif which == 1:
            diag[t, k, where, :] = value + (6.0 - CENTRE)
        else:
            pairing[which - 2, k, t, where, :] = value

    def spots(kind):
        up = swap_up(kind, ix)
        near = aligned(jnp.where(up, PAD + rows, PAD - 8))
        far = aligned(jnp.where(up, PAD + rows + 8, PAD - 16))
        return near, far, swap_valid(kind, ix, plan.nx)

    for kind, msg in zip(plan.sx, row_msgs):
        near, far, ok = spots(kind)
        for u, (which, k, is_far) in enumerate(plan.units):
            put(which, k, 0, pl.ds(far if is_far else near, 8), jnp.where(ok, msg[u], 0.0))

    def unpack(msgs, tile, size):
        sides = []
        for right in (True, False):
            total = jnp.zeros((size, LANES), F32)
            for kind, msg in zip(plan.sy, msgs):
                use = jnp.logical_and(swap_up(kind, iy) == right, swap_valid(kind, iy, plan.ny))
                total = jnp.where(use, msg[tile], total)
            sides.append(total)
        even = lax.rem(lane_iota(size) // STRIP, 2) == 0
        return jnp.where(even, sides[1], sides[0]), jnp.where(even, sides[0], sides[1])

    def piece(both, slot):
        turn = STRIP * (SLOTS - 1 - slot)
        return pltpu.roll(both[slot % 2], turn, 1) if turn else both[slot % 2]

    for tile in range(plan.strip_tiles):
        both = unpack(lane_msgs, tile, rows)
        for slot, (which, k) in enumerate(plan.strips[tile * SLOTS : (tile + 1) * SLOTS]):
            put(which, k, 1, plan.own, piece(both, slot))
    for i, row_kind in enumerate(plan.sx):
        near, far, ok = spots(row_kind)
        for tile in range(plan.unit_tiles):
            both = unpack(corner_msgs[i * len(plan.sy) : (i + 1) * len(plan.sy)], tile, 8)
            both = [jnp.where(ok, b, 0.0) for b in both]
            for slot, (which, k, is_far) in enumerate(plan.units[tile * SLOTS : (tile + 1) * SLOTS]):
                put(which, k, 1, pl.ds(far if is_far else near, 8), piece(both, slot))

    for copy in copies[:3]:
        copy.start()
    steps = ((b0, b1, (0, layers - 2, layers - 1), copies[3]), (b1, b2, (layers - 1,), copies[4]))
    for src, dst, wide, copy in steps:
        apply_all(plan, src, dst, diag, inside)
        for layer in wide:
            for first in (PAD - 16, PAD + rows + 8):
                for t, value in enumerate(operate(src, layer + 1, diag, layer, inside, first, 8)):
                    dst[t, layer + 1, pl.ds(first, 8), :] = value
        copy.start()

    def one(layer, sums):
        last = apply_own(plan, b2, layer + 1, diag, layer, inside)
        return add_products(sums, [v[0, layer + 1, plan.own, :] for v in (b0, b1, b2)] + [last])

    put_moments(moments, lax.fori_loop(0, layers, one, no_sums()))
    for copy in copies:
        copy.wait()


def lane_shift(first, second, by, lane):
    if by == 0:
        return first, second
    a, b = pltpu.roll(first, (-by) % LANES, 1), pltpu.roll(second, (-by) % LANES, 1)
    keep = lane < LANES - by if by > 0 else lane >= -by
    return jnp.where(keep, a, b), jnp.where(keep, b, a)


def put_shifted(shifted, n, first, size, planes):
    lane = lane_iota(size)
    for i in range(SPAN):
        for t, value in enumerate(lane_shift(planes[0], planes[1], i - REACH, lane)):
            shifted[n, i, t, pl.ds(first, size), :] = value


def pull(tables, shifted, count, t, first, size):
    total = [jnp.zeros((size, LANES), F32)] * count
    for offset in range(SPAN * SPAN):
        table = tables[offset, t, pl.ds(first, size), :]
        window = pl.ds(first + offset // SPAN - REACH, size)
        for n in range(count):
            total[n] = total[n] + table * shifted[n, offset % SPAN, t, window, :]
    return total


def push(tables, face, first, size, tiles=(0, 1)):
    lane = lane_iota(size)
    total = [jnp.zeros((size, LANES), F32)] * 2
    for i in range(SPAN):
        column = [jnp.zeros((size, LANES), F32)] * 2
        for j in range(SPAN):
            window = pl.ds(first - (j - REACH), size)
            for t in (0, 1):
                column[t] = column[t] + tables[j * SPAN + i, t, window, :] * face[t, window, :]
        moved = lane_shift(column[0], column[1], REACH - i, lane)
        total = [total[t] + moved[t] for t in (0, 1)]
    return [total[t] for t in tiles]


def put_faces(plan, tops, bottoms, outs):
    ib = lax.axis_index("body")
    lane = lane_iota(plan.face)
    for kind, out in zip(plan.sb, outs):
        up = swap_up(kind, ib)
        packed = jnp.zeros((plan.face, LANES), F32)
        for k in range(ORDER):
            out[k] = jnp.where(up, tops(k, 0), bottoms(k, 0))
            strips = pltpu.roll(jnp.where(up, tops(k, 1), bottoms(k, 1)), STRIP + 2 * STRIP * k, 1)
            packed = jnp.where(lane // (2 * STRIP) == k, strips, packed)
        out[ORDER] = packed


def get_face(plan, msgs, coef, up, tiles=(0, 1)):
    ib = lax.axis_index("body")
    total = [jnp.zeros((plan.face, LANES), F32)] * 2
    for kind, msg in zip(plan.sb, msgs):
        use = jnp.logical_and(swap_up(kind, ib) == up, swap_valid(kind, ib, plan.nb))
        for t in tiles:
            if t == 0:
                value = sum(coef[k] * msg[k] for k in range(ORDER))
            else:
                value = sum(
                    coef[k] * pltpu.roll(msg[ORDER], (LANES - STRIP - 2 * STRIP * k) % LANES, 1) for k in range(ORDER)
                )
            total[t] = jnp.where(use, value, total[t])
    return [total[t] for t in tiles]


def mortar_kernel(plan, b0, b1, b2, pairing_in, tables_in, *refs):
    args = Args(refs)
    faces = args.take(len(plan.sb))
    pulled, tables, shifted, ends, pairing, sems = args.take(6)
    rows, layers = plan.rows, plan.layers
    pair_copy = pltpu.make_async_copy(pairing_in, pairing, sems.at[0])
    table_copy = pltpu.make_async_copy(tables_in, tables.at[:, 0, plan.own, :], sems.at[1])
    end_copies = [
        pltpu.make_async_copy(b.at[:, layer], ends.at[side, k], sems.at[2 + 2 * k + side])
        for k, b in enumerate((b0, b1, b2))
        for side, layer in enumerate((1, layers))
    ]
    for copy in [pair_copy] + end_copies + [table_copy]:
        copy.start()
    zero = jnp.zeros((8, LANES), F32)
    for offset in range(SPAN * SPAN):
        for t in (0, 1):
            tables[offset, t, pl.ds(PAD - 16, 8), :] = zero
            tables[offset, t, pl.ds(PAD + rows + 8, 8), :] = zero
    pair_copy.wait()
    for t, first, size in [(0, PAD - 8, 8), (0, PAD + rows, 8)] + [(1, *c) for c in chunks(PAD - 8, plan.face, 40)]:
        table_rows(plan, pairing, t, first, size, lambda o: tables.at[o, t, pl.ds(first, size), :])
    for copy in end_copies:
        copy.wait()
    wide = pl.ds(PAD - 16, plan.face + 16)
    for k in range(ORDER):
        put_shifted(shifted, k, PAD - 16, plan.face + 16, [ends[1, k, t, wide, :] for t in (0, 1)])
    table_copy.wait()
    for t in (0, 1):
        for first, size in chunks(PAD - 8, plan.face, 40):
            for k, value in enumerate(pull(tables, shifted, ORDER, t, first, size)):
                pulled[k, t, pl.ds(first, size), :] = value
    put_faces(plan, lambda k, t: pulled[k, t, plan.near, :], lambda k, t: ends[0, k, t, plan.near, :], faces)


def powers_kernel(plan, tables, pulled, b0_in, b1_in, b2_in, diag_in, *refs):
    del pulled
    args = Args(refs)
    b0, b1, b2, b3, b4, b5, b6, diag, inside = args.take(9)
    tables_out, later, sems = args.take(3)
    pairs = ((b2_in, b2), (diag_in, diag), (b0_in, b0), (b1_in, b1), (tables, tables_out))
    copies = [pltpu.make_async_copy(src, dst, sems.at[i]) for i, (src, dst) in enumerate(pairs)]
    for copy in copies:
        copy.start()
    fill_inside(plan, inside)
    for vec in (b3, b4, b5):
        clear_frame(plan, vec)
    for copy in copies[:2]:
        copy.wait()
    for i, (src, dst) in enumerate(((b2, b3), (b3, b4), (b4, b5))):
        apply_all(plan, src, dst, diag, inside)
        copies.append(
            pltpu.make_async_copy(dst.at[0, pl.ds(1, plan.layers), plan.own, :], later.at[i], sems.at[len(pairs) + i])
        )
        copies[-1].start()

    def one(layer, carry):
        b6[layer] = apply_own(plan, b5, layer + 1, diag, layer, inside)
        return carry

    lax.fori_loop(0, plan.layers, one, 0)
    for copy in copies[2:]:
        copy.wait()


def solve(plan, moments):
    per = plan.nx * plan.ny
    body = lax.broadcasted_iota(jnp.int32, (plan.nb, LANES), 0)
    table = jnp.zeros((plan.nb, LANES), F32)
    for b in range(plan.nb):
        row = [moments[b * per + i] for i in range(per)]
        while len(row) > 1:
            row = [x + y for x, y in zip(row[::2], row[1::2])] + row[len(row) // 2 * 2 :]
        table = jnp.where(body == b, row[0], table)
    lane = lax.broadcasted_iota(jnp.int32, (plan.nb, LANES), 1)
    m = [
        jnp.broadcast_to(jnp.sum(jnp.where(lane == k, table, 0.0), axis=1, keepdims=True), table.shape)
        for k in range(6)
    ]
    h = [m[n + 1] + CENTRE * m[n] for n in range(5)]
    f1, f2 = h[1] / h[0], h[2] / h[0]
    d1 = h[2] - f1 * h[1]
    e = h[3] - f1 * h[2]
    f3 = e / d1
    d2 = h[4] - f2 * h[2] - f3 * e
    g1 = m[1] - f1 * m[0]
    g2 = m[2] - f2 * m[0] - f3 * g1
    c2 = g2 / d2
    c1 = (g1 - e * c2) / d1
    c0 = (m[0] - h[1] * c1 - h[2] * c2) / h[0]

    def pick(index):
        return [jnp.sum(jnp.where(body == index, c, 0.0), axis=0, keepdims=True) for c in (c0, c1, c2)]

    ib = lax.axis_index("body")
    return pick(ib), pick(ib + 1), pick(ib - 1)


def residual_coefs(c):
    return 1.0 - CENTRE * c[0], -(c[0] + CENTRE * c[1]), -(c[1] + CENTRE * c[2]), -c[2]


def middle_kernel(plan, moments_in, *refs):
    args = Args(refs)
    msgs = args.take(len(plan.sb))
    basis = args.take(6)
    b6, diag, inside, tables, pulled = args.take(5)
    moments, carry_out, forces_out, carry, stacks, sems = args.take(6)
    above_lambda = carry.at[pl.ds(4 * ORDER, 2)]
    ib = lax.axis_index("body")
    rows, layers = plan.rows, plan.layers
    has_above, has_below = ib < plan.nb - 1, ib > 0
    c, above_c, below_c = solve(plan, moments_in)
    d = residual_coefs(c)
    for i, row in enumerate(tuple(c) + d):
        carry[4 * ORDER + 3, pl.ds(i, 1), :] = row
    near = plan.near
    depth = ORDER + 1

    zero = jnp.zeros((8, LANES), F32)
    for side in (0, 1):
        for k in range(ORDER):
            for t in (0, 1):
                for at in range(depth + 2):
                    if at != 1 + k and (at == 0 or at > k):
                        stacks[side, k, t, at] = jnp.zeros((plan.buf, LANES), F32)
                    else:
                        stacks[side, k, t, at, pl.ds(PAD - 16, 8), :] = zero
                        stacks[side, k, t, at, pl.ds(PAD + rows + 8, 8), :] = zero

    slave = get_face(plan, msgs, above_c, True)
    master = get_face(plan, msgs, below_c, False)
    for t in (0, 1):
        above_lambda[t, pl.ds(PAD - 16, 8), :] = zero
        above_lambda[t, pl.ds(PAD + rows + 8, 8), :] = zero
        gap = slave[t] - sum(x * pulled[k, t, near, :] for k, x in enumerate(c))
        above_lambda[t, near, :] = jnp.where(has_above, RATE * gap, 0.0)
        gap = sum(x * basis[k][t, 1, near, :] for k, x in enumerate(c)) - master[t]
        gap = jnp.where(has_below, RATE * gap, 0.0)
        if t == 0:
            carry[4 * ORDER + 2, near, :] = gap
        stacks[0, 0, t, 1, near, :] = -gap
    for first, size in chunks(PAD - 8, plan.face, 40):
        for t, value in enumerate(push(tables, above_lambda, first, size)):
            stacks[1, 0, t, 1, pl.ds(first, size), :] = value * inside[t, pl.ds(first, size), :]

    for side in (0, 1):
        for k in range(ORDER - 1):
            for at in range(k + 2):
                layer = layers - 1 - at if side else at
                apply_near(plan, stacks.at[side, k], stacks.at[side, k + 1], at + 1, diag, layer, inside)
        at = layers if side else 1
        for k in range(ORDER):
            for t in (0, 1):
                made = sum(x * basis[k + n][t, at, near, :] for n, x in enumerate(d))
                carry[(side * ORDER + k) * 2 + t, near, :] = made + stacks[side, k, t, 1, near, :]
    copies = (
        pltpu.make_async_copy(carry, carry_out, sems.at[0]),
        pltpu.make_async_copy(stacks.at[:, :, 0, pl.ds(1, ORDER)], forces_out, sems.at[1]),
    )
    for copy in copies:
        copy.start()

    def cells(layer, first, size, side, at):
        span = pl.ds(first, size)
        b = [v[0, layer + 1, span, :] for v in basis] + [b6[layer, pl.ds(first - PAD, size), :]]
        made = [sum(x * b[k + j] for k, x in enumerate(d)) for j in range(depth)]
        if side is not None:
            for k in range(min(at, ORDER), ORDER):
                made[k] = made[k] + stacks[side, k, 0, at + 1, span, :]
            tail = operate(stacks.at[side, ORDER - 1], at + 1, diag, layer, inside, first, size, (0,), False)[0]
            made[ORDER] = made[ORDER] + tail
        return made

    def one(layer, sums):
        for first, size in chunks(PAD, rows, 32):
            sums = add_products(sums, cells(layer, first, size, None, 0))
        return sums

    sums = lax.fori_loop(depth, layers - depth, one, no_sums())
    for side in (0, 1):
        for at in range(depth):
            for first, size in chunks(PAD, rows, 32):
                sums = add_products(sums, cells(layers - 1 - at if side else at, first, size, side, at))
    put_moments(moments, sums)
    for copy in copies:
        copy.wait()


def second_mortar_kernel(plan, carry_in, tables_in, *refs):
    args = Args(refs)
    faces = args.take(len(plan.sb))
    pulled, carry, tables, shifted, sems = args.take(5)
    rows = plan.rows
    carry_copy = pltpu.make_async_copy(carry_in, carry, sems.at[0])
    table_copy = pltpu.make_async_copy(tables_in, tables, sems.at[1])
    carry_copy.start()
    table_copy.start()
    zero = jnp.zeros((8, LANES), F32)
    for k in range(ORDER):
        for t in (0, 1):
            for i in range(SPAN):
                shifted[k, i, t, pl.ds(PAD - 16, 8), :] = zero
                shifted[k, i, t, pl.ds(PAD + rows + 8, 8), :] = zero
    carry_copy.wait()
    plane = lambda side, k, t: carry[(side * ORDER + k) * 2 + t, plan.near, :]
    for k in range(ORDER):
        put_shifted(shifted, k, PAD - 8, plan.face, [plane(1, k, t) for t in (0, 1)])
    table_copy.wait()
    for t in (0, 1):
        for first, size in chunks(PAD - 8, plan.face, 40):
            for k, value in enumerate(pull(tables, shifted, ORDER, t, first, size)):
                pulled[k, t, pl.ds(first, size), :] = value
    put_faces(plan, lambda k, t: pulled[k, t, plan.near, :], lambda k, t: plane(0, k, t), faces)


def recall_kernel(plan, b0, b1, b2, later, forces_in, basis, forces, sems):
    own = plan.own
    pairs = [(b.at[0, pl.ds(1, plan.layers), own, :], basis.at[i]) for i, b in enumerate((b0, b1, b2))]
    pairs += [(later, basis.at[pl.ds(ORDER, ORDER)]), (forces_in.at[:, :, :, own, :], forces)]
    copies = [pltpu.make_async_copy(src, dst, sems.at[i]) for i, (src, dst) in enumerate(pairs)]
    for copy in copies:
        copy.start()
    for copy in copies:
        copy.wait()


def final_kernel(plan, moments_in, *refs):
    args = Args(refs)
    msgs = args.take(len(plan.sb))
    basis, forces, pulled, carry, tables = args.take(5)
    solution, interface, lifted = args.take(3)
    ib = lax.axis_index("body")
    rows, layers = plan.rows, plan.layers
    has_above, has_below = ib < plan.nb - 1, ib > 0
    c, above_c, below_c = solve(plan, moments_in)
    near, own = plan.near, plan.own
    base = 4 * ORDER
    past = [carry[base + 3, pl.ds(i, 1), :] for i in range(2 * ORDER + 1)]
    weights = []
    for j in range(2 * ORDER):
        terms = [c[k] * past[ORDER + j - k] for k in range(ORDER) if 0 <= j - k <= ORDER]
        weights.append(sum(terms[1:], terms[0]) + (past[j] if j < ORDER else 0.0))

    zero = jnp.zeros((8, LANES), F32)
    slave = get_face(plan, msgs, above_c, True)
    for t in (0, 1):
        lifted[t, pl.ds(PAD - 16, 8), :] = zero
        lifted[t, pl.ds(PAD + rows + 8, 8), :] = zero
        gap = slave[t] - sum(x * pulled[k, t, near, :] for k, x in enumerate(c))
        lifted[t, near, :] = 2.0 * carry[base + t, near, :] + jnp.where(has_above, RATE * gap, 0.0)
    interface[layers - 1] = push(tables, lifted, PAD, rows, (0,))[0]
    master = get_face(plan, msgs, below_c, False, (0,))[0][8 : 8 + rows]
    gap = sum(x * carry[2 * k, own, :] for k, x in enumerate(c)) - master
    interface[0] = -(2.0 * carry[base + 2, own, :] + jnp.where(has_below, RATE * gap, 0.0))

    def mixed(layer):
        return sum(x * basis[j, layer] for j, x in enumerate(weights))

    def combine(layer, state):
        solution[layer] = mixed(layer)
        return state

    lax.fori_loop(ORDER, layers - ORDER, combine, 0)
    for side in (0, 1):
        for at in range(ORDER):
            layer = layers - 1 - at if side else at
            extra = sum(c[k] * forces[side, k, at] for k in range(at, ORDER))
            solution[layer] = mixed(layer) + extra
    for layer in range(1, layers - 1):
        interface[layer] = jnp.zeros((rows, LANES), F32)


def shaped(*shape):
    return jax.ShapeDtypeStruct(shape, F32)


def held(*shape, dtype=F32):
    return pltpu.VMEM(shape, dtype)


def kept(*shape):
    return pltpu.HBM(shape, F32)


def call(kernel, args, outs, scratch=(), aliases=None, hbm_args=()):
    vmem = pl.BlockSpec(memory_space=pltpu.VMEM)
    hbm = pl.BlockSpec(memory_space=pltpu.HBM)
    in_hbm = lambda out: getattr(out, "memory_space", None) == pltpu.HBM
    return pl.pallas_call(
        kernel,
        out_shape=tuple(outs),
        in_specs=[vmem] * len(args) + [hbm] * len(hbm_args),
        out_specs=tuple(hbm if in_hbm(out) else vmem for out in outs),
        scratch_shapes=list(scratch),
        input_output_aliases=aliases or {},
        compiler_params=pltpu.CompilerParams(vmem_limit_bytes=8 * 1024 * 1024),
    )(*args, *[pltpu.with_memory_space_constraint(x, pltpu.HBM) for x in hbm_args])


def per_device(mesh, load, stiffness, pair_code, pair_weight):
    layers, rows, lanes = load.shape
    pairs = pair_code.shape[0]
    assert lanes == LANES and rows % 8 == 0 and rows >= 16 and layers >= 8
    plan = Plan(mesh, layers, rows, pairs)
    nb, nx, ny = plan.nb, plan.nx, plan.ny
    count = nb * nx * ny
    nf = len(plan.sb)
    buf = plan.buf
    bind = lambda kernel: functools.partial(kernel, plan)
    sems = lambda n: pltpu.SemaphoreType.DMA((n,))

    def lateral(row_kind, lane_kind, array):
        a, b = swap_perm(row_kind, nx), swap_perm(lane_kind, ny)
        return lax.ppermute(array, G, [(i * ny + j, a[i][1] * ny + b[j][1]) for i in range(nx) for j in range(ny)])

    def across(faces):
        return [lax.ppermute(f, "body", swap_perm(k, nb)) for k, f in zip(plan.sb, faces)]

    kinds = [(k, "") for k in plan.sx] + [("", k) for k in plan.sy] + [(a, b) for a in plan.sx for b in plan.sy]
    vec_shape, stack_shape = plan.vec, (2, layers, buf, LANES)
    pair_shape, table_shape = (2, pairs, 2, buf, LANES), (SPAN * SPAN, 2, buf, LANES)
    vec, stack = held(*vec_shape), held(*stack_shape)
    face = shaped(ORDER + 1, plan.face, LANES)
    message = shaped(count, 1, LANES)
    planes, mask = held(ORDER, 2, buf, LANES), held(2, buf, LANES)
    pairing, tables = held(*pair_shape), held(*table_shape)
    cells = (layers, rows, LANES)
    carry_shape = (4 * ORDER + 4, buf, LANES)
    shifted = pltpu.VMEM((ORDER, SPAN, 2, buf, LANES), F32)

    shapes = [shaped(len(plan.units), 8, LANES) for _ in plan.sx]
    shapes += [shaped(plan.strip_tiles, rows, LANES) for _ in plan.sy]
    shapes += [shaped(plan.unit_tiles, 8, LANES) for _ in plan.sx for _ in plan.sy]
    b0, diag, codes, weights, *packed = call(
        bind(pack_kernel),
        (),
        [vec, stack, held(pairs, rows, LANES, dtype=jnp.int32), held(pairs, rows, LANES)] + shapes,
        [sems(4)],
        hbm_args=(load, stiffness, pair_code, pair_weight),
    )
    halos = [lateral(a, b, m) for (a, b), m in zip(kinds, packed)]
    own_tables = (SPAN * SPAN, rows, LANES)
    b0, diag, pair, inside, b1, b2, table_own = call(
        bind(prepare_kernel),
        (b0, diag, codes, weights),
        [vec, stack, pairing, mask, vec, vec, kept(*own_tables)],
        [pltpu.VMEM(own_tables, F32), pltpu.SemaphoreType.DMA],
        {0: 0, 1: 1},
    )
    at = len(halos) + 1
    moments, _, _, _, _, _, b0, diag, pair, b1, b2 = call(
        bind(krylov_kernel),
        (*halos, inside, b0, diag, b1, b2, pair),
        [message, vec, stack, vec, vec, pairing]
        + [kept(*vec_shape), kept(*stack_shape), kept(*pair_shape), kept(*vec_shape), kept(*vec_shape)],
        [sems(5)],
        {at + i: 1 + i for i in range(5)},
    )
    moments = lax.all_to_all(moments, ALL, 0, 0, tiled=True)
    *faces, pulled, table = call(
        bind(mortar_kernel),
        (),
        [face] * nf + [planes, tables],
        [shifted, pltpu.VMEM((2, ORDER, 2, buf, LANES), F32), pltpu.VMEM(pair_shape, F32), sems(2 + 2 * ORDER)],
        hbm_args=(b0, b1, b2, pair, table_own),
    )
    faces = across(faces)
    *basis, b6, diag, inside, table_kept, later = call(
        bind(powers_kernel),
        (table, pulled),
        [vec] * 6 + [held(*cells), stack, mask, kept(*table_shape), kept(ORDER, *cells)],
        [sems(5 + ORDER)],
        hbm_args=(b0, b1, b2, diag),
    )
    forces_shape = (2, ORDER, ORDER, buf, LANES)
    moments, carry, forces = call(
        bind(middle_kernel),
        (moments, *faces, *basis, b6, diag, inside, table, pulled),
        [message, kept(*carry_shape), kept(*forces_shape)],
        [pltpu.VMEM(carry_shape, F32), pltpu.VMEM((2, ORDER, 2, ORDER + 3, buf, LANES), F32), sems(2)],
    )
    moments = lax.all_to_all(moments, ALL, 0, 0, tiled=True)
    *faces, pulled, carry, table = call(
        bind(second_mortar_kernel),
        (),
        [face] * nf + [planes, held(*carry_shape), tables],
        [shifted, sems(2)],
        hbm_args=(carry, table_kept),
    )
    faces = across(faces)
    own_basis, forces = call(
        bind(recall_kernel),
        (),
        [held(2 * ORDER, *cells), held(2, ORDER, ORDER, rows, LANES)],
        [sems(5)],
        hbm_args=(b0, b1, b2, later, forces),
    )
    return call(
        bind(final_kernel),
        (moments, *faces, own_basis, forces, pulled, carry, table),
        [shaped(*cells)] * 2,
        [pltpu.VMEM((2, buf, LANES), F32)],
    )


def solution(mesh):
    def whole(*args):
        return per_device(mesh, *args)

    return jax.shard_map(
        whole,
        mesh=mesh,
        in_specs=(P("body", "gx", "gy"), P("body", "gx", "gy"), P(None, "gx", "gy"), P(None, "gx", "gy")),
        out_specs=(P("body", "gx", "gy"), P("body", "gx", "gy")),
        check_vma=False,
    )
```

```python
import functools

import jax
import jax.numpy as jnp
from jax import lax
from jax.experimental import pallas as pl
from jax.experimental.pallas import tpu as pltpu
from jax.sharding import PartitionSpec as P

REACH = 2
SPAN = 2 * REACH + 1
RATE = 2.0
CENTRE = 7.5
LANES = 128
STRIP = 16
SLOTS = LANES // STRIP
PAD = 24
ORDER = 3
UNROLL = 2
F32 = jnp.float32
G = ("gx", "gy")
ALL = ("body", "gx", "gy")


def swaps_of(count):
    return () if count < 2 else (("A",) if count == 2 else ("A", "B"))


def swap_perm(kind, count):
    if kind == "":
        return [(i, i) for i in range(count)]
    step = 1 if kind == "A" else -1
    return [(i, (i + (step if i % 2 == 0 else -step)) % count) for i in range(count)]


def swap_up(kind, index):
    even = lax.rem(index, 2) == 0
    return even if kind == "A" else jnp.logical_not(even)


def swap_valid(kind, index, count):
    if kind == "A":
        return index >= 0
    return jnp.where(swap_up(kind, index), index < count - 1, index > 0)


def row_units(layers, pairs):
    wide_load = (0, 1, layers - 3, layers - 2, layers - 1)
    wide_stiff = (0, layers - 3, layers - 2, layers - 1)
    units = []
    for which, wide in ((0, wide_load), (1, wide_stiff)):
        for layer in range(layers):
            units.append((which, layer, False))
            if layer in wide:
                units.append((which, layer, True))
    for which in (2, 3):
        units += [(which, k, False) for k in range(pairs)]
    return units


def strip_list(layers, pairs):
    return [(w, k) for w in (0, 1) for k in range(layers)] + [(w, k) for w in (2, 3) for k in range(pairs)]


def lane_iota(rows):
    return lax.broadcasted_iota(jnp.int32, (rows, LANES), 1)


def aligned(start):
    return pl.multiple_of(start, 8)


def chunks(first, size, step):
    return [(at, min(step, first + size - at)) for at in range(first, first + size, step)]


class Plan:
    def __init__(self, mesh, layers, rows, pairs):
        self.nb, self.nx, self.ny = (mesh.shape[a] for a in ALL)
        self.layers, self.rows, self.pairs = layers, rows, pairs
        self.buf = rows + 2 * PAD
        self.units = row_units(layers, pairs)
        self.strips = strip_list(layers, pairs)
        self.sx, self.sy, self.sb = swaps_of(self.nx), swaps_of(self.ny), swaps_of(self.nb)
        self.face = rows + 16
        self.vec = (2, layers + 2, self.buf, LANES)
        self.own = pl.ds(PAD, rows)
        self.near = pl.ds(PAD - 8, self.face)
        self.unit_tiles = -(-len(self.units) // SLOTS)
        self.strip_tiles = -(-len(self.strips) // SLOTS)


class Args:
    def __init__(self, refs):
        self.refs = list(refs)

    def take(self, count):
        got, self.refs = self.refs[:count], self.refs[count:]
        return got

    def one(self):
        return self.refs.pop(0)


def pack_kernel(plan, load, stiff, code, weight, *refs):
    args = Args(refs)
    b0, diag, codes, weights = args.take(4)
    row_out, lane_out = args.take(len(plan.sx)), args.take(len(plan.sy))
    corner_out = args.take(len(plan.sx) * len(plan.sy))
    sems = args.one()
    ix, iy = lax.axis_index("gx"), lax.axis_index("gy")
    rows, layers = plan.rows, plan.layers
    places = (b0.at[0, pl.ds(1, layers), plan.own, :], diag.at[0, :, plan.own, :], codes, weights)
    copies = [
        pltpu.make_async_copy(src, dst, sems.at[i]) for i, (src, dst) in enumerate(zip((load, stiff, code, weight), places))
    ]
    for copy in copies:
        copy.start()
    arrived = set()

    def take(which, k, start, size):
        if which not in arrived:
            copies[which].wait()
            arrived.add(which)
        if which == 0:
            return b0[0, k + 1, pl.ds(PAD + start, size), :]
        if which == 1:
            return diag[0, k, pl.ds(PAD + start, size), :]
        return (codes, weights)[which - 2][k, pl.ds(start, size), :].astype(F32)

    def starts(kind):
        up = swap_up(kind, ix)
        return aligned(jnp.where(up, rows - 8, 0)), aligned(jnp.where(up, rows - 16, 8))

    def gather(pieces, size, tile, outs):
        slot_of = lane_iota(size) // STRIP
        last, first = jnp.zeros((size, LANES), F32), jnp.zeros((size, LANES), F32)
        for slot, value in enumerate(pieces):
            moved = pltpu.roll(value, STRIP * (slot + 1) % LANES, 1) if slot + 1 < SLOTS else value
            last = jnp.where(slot_of == slot, moved, last)
            first = jnp.where(slot_of == (slot + 1) % SLOTS, moved, first)
        for kind, out in zip(plan.sy, outs):
            out[tile] = jnp.where(swap_up(kind, iy), last, first)

    for kind, out in zip(plan.sx, row_out):
        near, far = starts(kind)
        for u, (which, k, is_far) in enumerate(plan.units):
            out[u] = take(which, k, far if is_far else near, 8)
    for tile in range(plan.strip_tiles):
        members = plan.strips[tile * SLOTS : (tile + 1) * SLOTS]
        gather([take(which, k, 0, rows) for which, k in members], rows, tile, lane_out)
    for i, row_kind in enumerate(plan.sx):
        near, far = starts(row_kind)
        outs = corner_out[i * len(plan.sy) : (i + 1) * len(plan.sy)]
        for tile in range(plan.unit_tiles):
            members = plan.units[tile * SLOTS : (tile + 1) * SLOTS]
            gather([take(which, k, far if is_far else near, 8) for which, k, is_far in members], 8, tile, outs)


def clear_frame(plan, vec):
    zero = jnp.zeros((16, LANES), F32)
    for t in (0, 1):
        for edge in (0, plan.layers + 1):
            vec[t, edge] = jnp.zeros((plan.buf, LANES), F32)
        for layer in range(1, plan.layers + 1):
            vec[t, layer, pl.ds(0, 16), :] = zero
            vec[t, layer, pl.ds(plan.buf - 16, 16), :] = zero


def table_rows(plan, pairing, tables, t, first, size):
    span = pl.ds(first, size)
    codes = [pairing[0, k, t, span, :] for k in range(plan.pairs)]
    weights = [pairing[1, k, t, span, :] for k in range(plan.pairs)]
    for offset in range(SPAN * SPAN):
        total = jnp.where(codes[0] == offset, weights[0], 0.0)
        for k in range(1, plan.pairs):
            total = total + jnp.where(codes[k] == offset, weights[k], 0.0)
        tables[offset, t, span, :] = total


def prepare_kernel(plan, b0_in, diag_in, codes, weights, b0, diag, pairing, inside, tables, *vecs):
    del b0_in, diag_in
    ix, iy = lax.axis_index("gx"), lax.axis_index("gy")
    rows, layers, buf = plan.rows, plan.layers, plan.buf
    row = lax.broadcasted_iota(jnp.int32, (buf, LANES), 0) + ix * rows - PAD
    lane = lane_iota(buf)
    in_rows = jnp.logical_and(row >= 0, row < plan.nx * rows)
    right = jnp.logical_and(lane < STRIP, iy < plan.ny - 1)
    left = jnp.logical_and(lane >= LANES - STRIP, iy > 0)
    inside[0] = jnp.where(in_rows, 1.0, 0.0)
    inside[1] = jnp.where(jnp.logical_and(in_rows, jnp.logical_or(right, left)), 1.0, 0.0)
    zero = jnp.zeros((PAD, LANES), F32)
    for t in (0, 1):
        for span in (pl.ds(0, PAD), pl.ds(buf - PAD, PAD)):
            for layer in range(layers):
                b0[t, layer + 1, span, :] = zero
                diag[t, layer, span, :] = zero
            for k in range(plan.pairs):
                for i in (0, 1):
                    pairing[i, k, t, span, :] = zero
        for edge in (0, layers + 1):
            b0[t, edge] = jnp.zeros((buf, LANES), F32)
        for offset in range(SPAN * SPAN):
            tables[offset, t, pl.ds(PAD - 16, 8), :] = jnp.zeros((8, LANES), F32)
            tables[offset, t, pl.ds(PAD + rows + 8, 8), :] = jnp.zeros((8, LANES), F32)
    for vec in vecs:
        clear_frame(plan, vec)
    for layer in range(layers):
        diag[0, layer, plan.own, :] = diag[0, layer, plan.own, :] + (6.0 - CENTRE)
    for k in range(plan.pairs):
        pairing[0, k, 0, plan.own, :] = codes[k].astype(F32)
        pairing[1, k, 0, plan.own, :] = weights[k]
    for first, size in chunks(PAD, rows, 32):
        table_rows(plan, pairing, tables, 0, first, size)


def operate(src, at, diag, layer, inside, first, size, tiles=(0, 1), masked=True):
    lane = lane_iota(size)
    start, end = lane == 0, lane == LANES - 1
    rows = pl.ds(first, size)
    middle = [src[t, at, rows, :] for t in (0, 1)]
    before = [pltpu.roll(m, 1, 1) for m in middle]
    after = [pltpu.roll(m, LANES - 1, 1) for m in middle]
    done = []
    for t in tiles:
        total = jnp.where(start, before[1 - t], before[t]) + jnp.where(end, after[1 - t], after[t])
        total = total + src[t, at, pl.ds(first - 1, size), :]
        total = total + src[t, at, pl.ds(first + 1, size), :]
        total = total + (src[t, at - 1, rows, :] + src[t, at + 1, rows, :])
        if masked or t == 1:
            total = total * inside[t, rows, :]
        done.append(diag[t, layer, rows, :] * middle[t] - total)
    return done


def apply_near(plan, src, dst, at, diag, layer, inside):
    parts = [(PAD - 8, 8, True), (PAD + plan.rows, 8, True)]
    parts += [(first, size, False) for first, size in chunks(PAD, plan.rows, 32)]
    values = [
        (first, size, operate(src, at, diag, layer, inside, first, size, masked=masked)) for first, size, masked in parts
    ]
    for first, size, pair in values:
        for t in (0, 1):
            dst[t, at, pl.ds(first, size), :] = pair[t]
    return jnp.concatenate([pair[0] for _, _, pair in values[2:]], axis=0)


def apply_all(plan, src, dst, diag, inside):
    def one(layer, carry):
        apply_near(plan, src, dst, layer + 1, diag, layer, inside)
        return carry

    lax.fori_loop(0, plan.layers, one, 0, unroll=UNROLL)


def apply_own(plan, src, at, diag, layer, inside):
    parts = [
        operate(src, at, diag, layer, inside, first, size, (0,), False)[0] for first, size in chunks(PAD, plan.rows, 32)
    ]
    return jnp.concatenate(parts, axis=0)


def six_sums(parts):
    lane = lax.broadcasted_iota(jnp.int32, (1, LANES), 1)
    row = jnp.zeros((1, LANES), F32)
    for k, part in enumerate(parts):
        row = jnp.where(lane == k, jnp.sum(part), row)
    return row


def fold(value):
    return jnp.sum(value.reshape(-1, 8, LANES), axis=0)


def add_products(sums, v):
    pairs = ((v[0], v[0]), (v[0], v[1]), (v[1], v[1]), (v[1], v[2]), (v[2], v[2]), (v[2], v[3]))
    return tuple(s + fold(a * b) for s, (a, b) in zip(sums, pairs))


def put_moments(moments, sums):
    moments[...] = jnp.broadcast_to(six_sums(sums).reshape(1, 1, LANES), moments.shape)


def no_sums():
    return (jnp.zeros((8, LANES), F32),) * 6


def krylov_kernel(plan, *refs):
    args = Args(refs)
    row_msgs, lane_msgs = args.take(len(plan.sx)), args.take(len(plan.sy))
    corner_msgs = args.take(len(plan.sx) * len(plan.sy))
    inside = args.one()
    args.take(6)
    moments, = args.take(1)
    faces = args.take(len(plan.sb))
    pulled, b0, diag, b1, b2, b3, pairing, tables, shifted = args.take(9)
    ix, iy = lax.axis_index("gx"), lax.axis_index("gy")
    rows, layers = plan.rows, plan.layers

    def put(which, k, t, where, value):
        if which == 0:
            b0[t, k + 1, where, :] = value
        elif which == 1:
            diag[t, k, where, :] = value + (6.0 - CENTRE)
        else:
            pairing[which - 2, k, t, where, :] = value

    def spots(kind):
        up = swap_up(kind, ix)
        near = aligned(jnp.where(up, PAD + rows, PAD - 8))
        far = aligned(jnp.where(up, PAD + rows + 8, PAD - 16))
        return near, far, swap_valid(kind, ix, plan.nx)

    for kind, msg in zip(plan.sx, row_msgs):
        near, far, ok = spots(kind)
        for u, (which, k, is_far) in enumerate(plan.units):
            put(which, k, 0, pl.ds(far if is_far else near, 8), jnp.where(ok, msg[u], 0.0))

    def unpack(msgs, tile, size):
        sides = []
        for right in (True, False):
            total = jnp.zeros((size, LANES), F32)
            for kind, msg in zip(plan.sy, msgs):
                use = jnp.logical_and(swap_up(kind, iy) == right, swap_valid(kind, iy, plan.ny))
                total = jnp.where(use, msg[tile], total)
            sides.append(total)
        even = lax.rem(lane_iota(size) // STRIP, 2) == 0
        return jnp.where(even, sides[1], sides[0]), jnp.where(even, sides[0], sides[1])

    def piece(both, slot):
        turn = STRIP * (SLOTS - 1 - slot)
        return pltpu.roll(both[slot % 2], turn, 1) if turn else both[slot % 2]

    for tile in range(plan.strip_tiles):
        both = unpack(lane_msgs, tile, rows)
        for slot, (which, k) in enumerate(plan.strips[tile * SLOTS : (tile + 1) * SLOTS]):
            put(which, k, 1, plan.own, piece(both, slot))
    for i, row_kind in enumerate(plan.sx):
        near, far, ok = spots(row_kind)
        for tile in range(plan.unit_tiles):
            both = unpack(corner_msgs[i * len(plan.sy) : (i + 1) * len(plan.sy)], tile, 8)
            both = [jnp.where(ok, b, 0.0) for b in both]
            for slot, (which, k, is_far) in enumerate(plan.units[tile * SLOTS : (tile + 1) * SLOTS]):
                put(which, k, 1, pl.ds(far if is_far else near, 8), piece(both, slot))

    for src, dst, wide in ((b0, b1, (0, layers - 2, layers - 1)), (b1, b2, (layers - 1,))):
        apply_all(plan, src, dst, diag, inside)
        for layer in wide:
            for first in (PAD - 16, PAD + rows + 8):
                for t, value in enumerate(operate(src, layer + 1, diag, layer, inside, first, 8)):
                    dst[t, layer + 1, pl.ds(first, 8), :] = value

    def one(layer, sums):
        last = apply_near(plan, b2, b3, layer + 1, diag, layer, inside)
        return add_products(sums, [v[0, layer + 1, plan.own, :] for v in (b0, b1, b2)] + [last])

    put_moments(moments, lax.fori_loop(0, layers, one, no_sums(), unroll=UNROLL))

    for t, first, size in [(0, PAD - 8, 8), (0, PAD + rows, 8)] + [(1, *c) for c in chunks(PAD - 8, plan.face, 40)]:
        table_rows(plan, pairing, tables, t, first, size)
    vecs = (b0, b1, b2)
    wide = pl.ds(PAD - 16, plan.face + 16)
    for k, vec in enumerate(vecs):
        put_shifted(shifted, k, PAD - 16, plan.face + 16, [vec[t, layers, wide, :] for t in (0, 1)])
    send_planes(plan, tables, shifted, pulled, lambda k, t: vecs[k][t, 1, plan.near, :], faces)


def lane_shift(first, second, by, lane):
    if by == 0:
        return first, second
    a, b = pltpu.roll(first, (-by) % LANES, 1), pltpu.roll(second, (-by) % LANES, 1)
    keep = lane < LANES - by if by > 0 else lane >= -by
    return jnp.where(keep, a, b), jnp.where(keep, b, a)


def put_shifted(shifted, n, first, size, planes):
    lane = lane_iota(size)
    for i in range(SPAN):
        for t, value in enumerate(lane_shift(planes[0], planes[1], i - REACH, lane)):
            shifted[n, i, t, pl.ds(first, size), :] = value


def pull(tables, shifted, count, t, first, size):
    total = [jnp.zeros((size, LANES), F32)] * count
    for offset in range(SPAN * SPAN):
        table = tables[offset, t, pl.ds(first, size), :]
        window = pl.ds(first + offset // SPAN - REACH, size)
        for n in range(count):
            total[n] = total[n] + table * shifted[n, offset % SPAN, t, window, :]
    return total


def push(tables, face, first, size, tiles=(0, 1)):
    lane = lane_iota(size)
    total = [jnp.zeros((size, LANES), F32)] * 2
    for i in range(SPAN):
        column = [jnp.zeros((size, LANES), F32)] * 2
        for j in range(SPAN):
            window = pl.ds(first - (j - REACH), size)
            for t in (0, 1):
                column[t] = column[t] + tables[j * SPAN + i, t, window, :] * face[t, window, :]
        moved = lane_shift(column[0], column[1], REACH - i, lane)
        total = [total[t] + moved[t] for t in (0, 1)]
    return [total[t] for t in tiles]


def put_faces(plan, tops, bottoms, outs):
    ib = lax.axis_index("body")
    lane = lane_iota(plan.face)
    for kind, out in zip(plan.sb, outs):
        up = swap_up(kind, ib)
        packed = jnp.zeros((plan.face, LANES), F32)
        for k in range(ORDER):
            out[k] = jnp.where(up, tops(k, 0), bottoms(k, 0))
            strips = pltpu.roll(jnp.where(up, tops(k, 1), bottoms(k, 1)), STRIP + 2 * STRIP * k, 1)
            packed = jnp.where(lane // (2 * STRIP) == k, strips, packed)
        out[ORDER] = packed


def get_face(plan, msgs, coef, up, tiles=(0, 1)):
    ib = lax.axis_index("body")
    total = [jnp.zeros((plan.face, LANES), F32)] * 2
    for kind, msg in zip(plan.sb, msgs):
        use = jnp.logical_and(swap_up(kind, ib) == up, swap_valid(kind, ib, plan.nb))
        for t in tiles:
            if t == 0:
                value = sum(coef[k] * msg[k] for k in range(ORDER))
            else:
                value = sum(
                    coef[k] * pltpu.roll(msg[ORDER], (LANES - STRIP - 2 * STRIP * k) % LANES, 1) for k in range(ORDER)
                )
            total[t] = jnp.where(use, value, total[t])
    return [total[t] for t in tiles]


def send_planes(plan, tables, shifted, pulled, bottoms, faces):
    for t in (0, 1):
        for first, size in chunks(PAD - 8, plan.face, 40):
            for k, value in enumerate(pull(tables, shifted, ORDER, t, first, size)):
                pulled[k, t, pl.ds(first, size), :] = value
    put_faces(plan, lambda k, t: pulled[k, t, plan.near, :], bottoms, faces)


def solve(plan, moments):
    per = plan.nx * plan.ny
    body = lax.broadcasted_iota(jnp.int32, (plan.nb, LANES), 0)
    table = jnp.zeros((plan.nb, LANES), F32)
    for b in range(plan.nb):
        row = [moments[b * per + i] for i in range(per)]
        while len(row) > 1:
            row = [x + y for x, y in zip(row[::2], row[1::2])] + row[len(row) // 2 * 2 :]
        table = jnp.where(body == b, row[0], table)
    lane = lax.broadcasted_iota(jnp.int32, (plan.nb, LANES), 1)
    m = [
        jnp.broadcast_to(jnp.sum(jnp.where(lane == k, table, 0.0), axis=1, keepdims=True), table.shape)
        for k in range(6)
    ]
    h = [m[n + 1] + CENTRE * m[n] for n in range(5)]
    f1, f2 = h[1] / h[0], h[2] / h[0]
    d1 = h[2] - f1 * h[1]
    e = h[3] - f1 * h[2]
    f3 = e / d1
    d2 = h[4] - f2 * h[2] - f3 * e
    g1 = m[1] - f1 * m[0]
    g2 = m[2] - f2 * m[0] - f3 * g1
    c2 = g2 / d2
    c1 = (g1 - e * c2) / d1
    c0 = (m[0] - h[1] * c1 - h[2] * c2) / h[0]

    def pick(index):
        return [jnp.sum(jnp.where(body == index, c, 0.0), axis=0, keepdims=True) for c in (c0, c1, c2)]

    ib = lax.axis_index("body")
    return pick(ib), pick(ib + 1), pick(ib - 1)


def residual_coefs(c):
    return 1.0 - CENTRE * c[0], -(c[0] + CENTRE * c[1]), -(c[1] + CENTRE * c[2]), -c[2]


def middle_kernel(plan, moments_in, *refs):
    args = Args(refs)
    msgs = args.take(len(plan.sb))
    basis = args.take(4)
    diag, inside, tables, pulled_in = args.take(4)
    moments, = args.take(1)
    faces = args.take(len(plan.sb))
    vecs = args.take(3)
    base, above_lambda, below_lambda, pulled, shifted = args.take(5)
    ib = lax.axis_index("body")
    rows, layers = plan.rows, plan.layers
    has_above, has_below = ib < plan.nb - 1, ib > 0
    c, above_c, below_c = solve(plan, moments_in)
    d = residual_coefs(c)
    near, own = plan.near, plan.own
    for vec in vecs:
        clear_frame(plan, vec)

    def combine(layer, carry):
        for first, size in chunks(PAD - 8, plan.face, 40):
            for t in (0, 1):
                span = pl.ds(first, size)
                vecs[0][t, layer + 1, span, :] = sum(x * v[t, layer + 1, span, :] for x, v in zip(d, basis))
        base[layer] = sum(x * v[0, layer + 1, own, :] for x, v in zip(c, basis))
        return carry

    lax.fori_loop(0, layers, combine, 0)

    zero = jnp.zeros((8, LANES), F32)
    slave = get_face(plan, msgs, above_c, True)
    master = get_face(plan, msgs, below_c, False)
    for t in (0, 1):
        above_lambda[t, pl.ds(PAD - 16, 8), :] = zero
        above_lambda[t, pl.ds(PAD + rows + 8, 8), :] = zero
        gap = slave[t] - sum(x * pulled_in[k, t, near, :] for k, x in enumerate(c))
        above_lambda[t, near, :] = jnp.where(has_above, RATE * gap, 0.0)
        gap = sum(x * basis[k][t, 1, near, :] for k, x in enumerate(c)) - master[t]
        gap = jnp.where(has_below, RATE * gap, 0.0)
        if t == 0:
            below_lambda[...] = gap[8 : 8 + rows]
        vecs[0][t, 1, near, :] = vecs[0][t, 1, near, :] - gap
    for first, size in chunks(PAD - 8, plan.face, 40):
        span = pl.ds(first, size)
        for t, value in enumerate(push(tables, above_lambda, first, size)):
            vecs[0][t, layers, span, :] = vecs[0][t, layers, span, :] + value * inside[t, span, :]

    for step in range(2):
        apply_all(plan, vecs[step], vecs[step + 1], diag, inside)

    def one(layer, sums):
        last = apply_own(plan, vecs[2], layer + 1, diag, layer, inside)
        return add_products(sums, [v[0, layer + 1, own, :] for v in vecs] + [last])

    put_moments(moments, lax.fori_loop(0, layers, one, no_sums(), unroll=UNROLL))

    for k, vec in enumerate(vecs):
        for t in (0, 1):
            for i in range(SPAN):
                shifted[k, i, t, pl.ds(PAD - 16, 8), :] = zero
                shifted[k, i, t, pl.ds(PAD + rows + 8, 8), :] = zero
        put_shifted(shifted, k, PAD - 8, plan.face, [vec[t, layers, near, :] for t in (0, 1)])
    send_planes(plan, tables, shifted, pulled, lambda k, t: vecs[k][t, 1, near, :], faces)


def final_kernel(plan, moments_in, *refs):
    args = Args(refs)
    msgs = args.take(len(plan.sb))
    vecs = args.take(3)
    base, above_lambda, below_lambda, pulled, tables = args.take(5)
    solution_out, interface_out, solution, interface, lifted, sems = args.take(6)
    ib = lax.axis_index("body")
    rows, layers = plan.rows, plan.layers
    has_above, has_below = ib < plan.nb - 1, ib > 0
    inner = pl.ds(1, layers - 2)
    copies = [pltpu.make_async_copy(interface.at[inner], interface_out.at[inner], sems.at[0])]
    for layer in range(1, layers - 1):
        interface[layer] = jnp.zeros((rows, LANES), F32)
    copies[0].start()
    c, above_c, below_c = solve(plan, moments_in)
    near, own = plan.near, plan.own
    half = layers // 2
    for i, (low, high) in enumerate(((0, half), (half, layers))):

        def combine(layer, carry):
            solution[layer] = base[layer] + sum(x * v[0, layer + 1, own, :] for x, v in zip(c, vecs))
            return carry

        lax.fori_loop(low, high, combine, 0, unroll=UNROLL)
        part = pl.ds(low, high - low)
        copies.append(pltpu.make_async_copy(solution.at[part], solution_out.at[part], sems.at[1 + i]))
        copies[-1].start()

    zero = jnp.zeros((8, LANES), F32)
    master = get_face(plan, msgs, below_c, False, (0,))[0][8 : 8 + rows]
    gap = sum(x * v[0, 1, own, :] for x, v in zip(c, vecs)) - master
    interface[0] = -(2.0 * below_lambda[...] + jnp.where(has_below, RATE * gap, 0.0))
    copies.append(pltpu.make_async_copy(interface.at[0], interface_out.at[0], sems.at[3]))
    copies[-1].start()
    slave = get_face(plan, msgs, above_c, True)
    for t in (0, 1):
        lifted[t, pl.ds(PAD - 16, 8), :] = zero
        lifted[t, pl.ds(PAD + rows + 8, 8), :] = zero
        gap = slave[t] - sum(x * pulled[k, t, near, :] for k, x in enumerate(c))
        lifted[t, near, :] = 2.0 * above_lambda[t, near, :] + jnp.where(has_above, RATE * gap, 0.0)
    interface[layers - 1] = push(tables, lifted, PAD, rows, (0,))[0]
    copies.append(pltpu.make_async_copy(interface.at[layers - 1], interface_out.at[layers - 1], sems.at[4]))
    copies[-1].start()
    for copy in copies:
        copy.wait()


def shaped(*shape):
    return jax.ShapeDtypeStruct(shape, F32)


def held(*shape, dtype=F32):
    return pltpu.VMEM(shape, dtype)


def kept(*shape):
    return pltpu.HBM(shape, F32)


def call(kernel, args, outs, name, scratch=(), aliases=None, hbm_args=()):
    vmem = pl.BlockSpec(memory_space=pltpu.VMEM)
    hbm = pl.BlockSpec(memory_space=pltpu.HBM)
    in_hbm = lambda out: getattr(out, "memory_space", None) == pltpu.HBM
    return pl.pallas_call(
        kernel,
        out_shape=tuple(outs),
        in_specs=[vmem] * len(args) + [hbm] * len(hbm_args),
        out_specs=tuple(hbm if in_hbm(out) else vmem for out in outs),
        scratch_shapes=list(scratch),
        input_output_aliases=aliases or {},
        compiler_params=pltpu.CompilerParams(vmem_limit_bytes=8 * 1024 * 1024),
        name=name,
    )(*args, *[pltpu.with_memory_space_constraint(x, pltpu.HBM) for x in hbm_args])


def per_device(mesh, load, stiffness, pair_code, pair_weight):
    layers, rows, lanes = load.shape
    pairs = pair_code.shape[0]
    assert lanes == LANES and rows % 8 == 0 and rows >= 16 and layers % 4 == 0
    plan = Plan(mesh, layers, rows, pairs)
    nb, nx, ny = plan.nb, plan.nx, plan.ny
    count = nb * nx * ny
    nf = len(plan.sb)
    buf = plan.buf
    bind = lambda kernel: functools.partial(kernel, plan)
    sems = lambda n: pltpu.SemaphoreType.DMA((n,))

    def lateral(row_kind, lane_kind, array):
        a, b = swap_perm(row_kind, nx), swap_perm(lane_kind, ny)
        return lax.ppermute(array, G, [(i * ny + j, a[i][1] * ny + b[j][1]) for i in range(nx) for j in range(ny)])

    def across(kind, array):
        side = nx * ny
        pairs = []
        for b, to in swap_perm(kind, nb):
            for i in range(side):
                pairs.append((b * side + i, to * side + i) if abs(to - b) == 1 else (b * side + i, b * side + (i ^ 1)))
        return lax.ppermute(array, ALL, pairs)

    def spread(moments, faces):
        return lax.all_to_all(moments, ALL, 0, 0, tiled=True), [across(k, f) for k, f in zip(plan.sb, faces)]

    kinds = [(k, "") for k in plan.sx] + [("", k) for k in plan.sy] + [(a, b) for a in plan.sx for b in plan.sy]
    vec, stack = held(*plan.vec), held(2, layers, buf, LANES)
    face = shaped(ORDER + 1, plan.face, LANES)
    message = shaped(count, 1, LANES)
    planes, mask = held(ORDER, 2, buf, LANES), held(2, buf, LANES)
    pairing, tables = held(2, pairs, 2, buf, LANES), held(SPAN * SPAN, 2, buf, LANES)
    cells = (layers, rows, LANES)
    shifted = pltpu.VMEM((ORDER, SPAN, 2, buf, LANES), F32)

    shapes = [shaped(len(plan.units), 8, LANES) for _ in plan.sx]
    shapes += [shaped(plan.strip_tiles, rows, LANES) for _ in plan.sy]
    shapes += [shaped(plan.unit_tiles, 8, LANES) for _ in plan.sx for _ in plan.sy]
    b0, diag, codes, weights, *packed = call(
        bind(pack_kernel),
        (),
        [vec, stack, held(pairs, rows, LANES, dtype=jnp.int32), held(pairs, rows, LANES)] + shapes,
        "pack",
        [sems(4)],
        hbm_args=(load, stiffness, pair_code, pair_weight),
    )
    halos = [lateral(a, b, m) for (a, b), m in zip(kinds, packed)]
    b0, diag, pair, inside, table, b1, b2 = call(
        bind(prepare_kernel),
        (b0, diag, codes, weights),
        [vec, stack, pairing, mask, tables, vec, vec],
        "prepare",
        aliases={0: 0, 1: 1},
    )
    at = len(halos) + 1
    out_at = 2 + nf
    moments, *rest = call(
        bind(krylov_kernel),
        (*halos, inside, b0, diag, b1, b2, pair, table),
        [message] + [face] * nf + [planes, vec, stack, vec, vec, vec, pairing, tables],
        "krylov",
        [shifted],
        {at: out_at, at + 1: out_at + 1, at + 2: out_at + 2, at + 3: out_at + 3, at + 4: out_at + 5, at + 5: out_at + 6},
    )
    faces, (pulled, b0, diag, b1, b2, b3, _, table) = rest[:nf], rest[nf:]
    moments, faces = spread(moments, faces)
    moments, *rest = call(
        bind(middle_kernel),
        (moments, *faces, b0, b1, b2, b3, diag, inside, table, pulled),
        [message] + [face] * nf + [vec] * 3 + [held(*cells), mask, held(rows, LANES), planes],
        "middle",
        [shifted],
    )
    faces, kept_arrays = rest[:nf], rest[nf:]
    moments, faces = spread(moments, faces)
    return call(
        bind(final_kernel),
        (moments, *faces, *kept_arrays, table),
        [kept(*cells)] * 2,
        "final",
        [pltpu.VMEM(cells, F32), pltpu.VMEM(cells, F32), pltpu.VMEM((2, buf, LANES), F32), sems(5)],
    )


def solution(mesh):
    return jax.shard_map(
        functools.partial(per_device, mesh),
        mesh=mesh,
        in_specs=(P("body", "gx", "gy"), P("body", "gx", "gy"), P(None, "gx", "gy"), P(None, "gx", "gy")),
        out_specs=(P("body", "gx", "gy"), P("body", "gx", "gy")),
        check_vma=False,
    )
```

```python
import functools

import jax
import jax.numpy as jnp
from jax import lax
from jax.experimental import pallas as pl
from jax.experimental.pallas import tpu as pltpu
from jax.sharding import PartitionSpec as P

REACH = 2
SPAN = 2 * REACH + 1
RATE = 2.0
CENTRE = 7.5
LANES = 128
STRIP = 16
SLOTS = LANES // STRIP
PAD = 24
ORDER = 3
UNROLL = 4
UPDATES = 2
STEADY = 0.05
F32 = jnp.float32
G = ("gx", "gy")
ALL = ("body", "gx", "gy")


def swaps_of(count):
    return () if count < 2 else (("A",) if count == 2 else ("A", "B"))


def swap_perm(kind, count):
    if kind == "":
        return [(i, i) for i in range(count)]
    step = 1 if kind == "A" else -1
    return [(i, (i + (step if i % 2 == 0 else -step)) % count) for i in range(count)]


def swap_up(kind, index):
    even = lax.rem(index, 2) == 0
    return even if kind == "A" else jnp.logical_not(even)


def swap_valid(kind, index, count):
    if kind == "A":
        return index >= 0
    return jnp.where(swap_up(kind, index), index < count - 1, index > 0)


def row_units(layers, pairs):
    wide_load = (0, 1, layers - 3, layers - 2, layers - 1)
    wide_stiff = (0, layers - 3, layers - 2, layers - 1)
    units = []
    for which, wide in ((0, wide_load), (1, wide_stiff)):
        for layer in range(layers):
            units.append((which, layer, False))
            if layer in wide:
                units.append((which, layer, True))
    for which in (2, 3):
        units += [(which, k, False) for k in range(pairs)]
    return units


def strip_list(layers, pairs):
    return [(w, k) for w in (0, 1) for k in range(layers)] + [(w, k) for w in (2, 3) for k in range(pairs)]


def lane_iota(rows):
    return lax.broadcasted_iota(jnp.int32, (rows, LANES), 1)


def aligned(start):
    return pl.multiple_of(start, 8)


def chunks(first, size, step):
    return [(at, min(step, first + size - at)) for at in range(first, first + size, step)]


class Plan:
    def __init__(self, mesh, layers, rows, pairs):
        self.nb, self.nx, self.ny = (mesh.shape[a] for a in ALL)
        self.layers, self.rows, self.pairs = layers, rows, pairs
        self.buf = rows + 2 * PAD
        self.units = row_units(layers, pairs)
        self.strips = strip_list(layers, pairs)
        self.sx, self.sy, self.sb = swaps_of(self.nx), swaps_of(self.ny), swaps_of(self.nb)
        self.face = rows + 16
        self.vec = (2, layers + 2, self.buf, LANES)
        self.own = pl.ds(PAD, rows)
        self.near = pl.ds(PAD - 8, self.face)
        self.unit_tiles = -(-len(self.units) // SLOTS)
        self.strip_tiles = -(-len(self.strips) // SLOTS)


class Args:
    def __init__(self, refs):
        self.refs = list(refs)

    def take(self, count):
        got, self.refs = self.refs[:count], self.refs[count:]
        return got

    def one(self):
        return self.refs.pop(0)


def pack_kernel(plan, load, stiff, code, weight, *refs):
    args = Args(refs)
    b0, diag, codes, weights = args.take(4)
    row_out, lane_out = args.take(len(plan.sx)), args.take(len(plan.sy))
    corner_out = args.take(len(plan.sx) * len(plan.sy))
    sems = args.one()
    ix, iy = lax.axis_index("gx"), lax.axis_index("gy")
    rows, layers = plan.rows, plan.layers
    places = (b0.at[0, pl.ds(1, layers), plan.own, :], diag.at[0, :, plan.own, :], codes, weights)
    copies = [
        pltpu.make_async_copy(src, dst, sems.at[i]) for i, (src, dst) in enumerate(zip((load, stiff, code, weight), places))
    ]
    for copy in copies:
        copy.start()
    arrived = set()

    def take(which, k, start, size):
        if which not in arrived:
            copies[which].wait()
            arrived.add(which)
        if which == 0:
            return b0[0, k + 1, pl.ds(PAD + start, size), :]
        if which == 1:
            return diag[0, k, pl.ds(PAD + start, size), :]
        return (codes, weights)[which - 2][k, pl.ds(start, size), :].astype(F32)

    def starts(kind):
        up = swap_up(kind, ix)
        return aligned(jnp.where(up, rows - 8, 0)), aligned(jnp.where(up, rows - 16, 8))

    def gather(pieces, size, tile, outs):
        slot_of = lane_iota(size) // STRIP
        last, first = jnp.zeros((size, LANES), F32), jnp.zeros((size, LANES), F32)
        for slot, value in enumerate(pieces):
            moved = pltpu.roll(value, STRIP * (slot + 1) % LANES, 1) if slot + 1 < SLOTS else value
            last = jnp.where(slot_of == slot, moved, last)
            first = jnp.where(slot_of == (slot + 1) % SLOTS, moved, first)
        for kind, out in zip(plan.sy, outs):
            out[tile] = jnp.where(swap_up(kind, iy), last, first)

    for kind, out in zip(plan.sx, row_out):
        near, far = starts(kind)
        for u, (which, k, is_far) in enumerate(plan.units):
            out[u] = take(which, k, far if is_far else near, 8)
    for tile in range(plan.strip_tiles):
        members = plan.strips[tile * SLOTS : (tile + 1) * SLOTS]
        gather([take(which, k, 0, rows) for which, k in members], rows, tile, lane_out)
    for i, row_kind in enumerate(plan.sx):
        near, far = starts(row_kind)
        outs = corner_out[i * len(plan.sy) : (i + 1) * len(plan.sy)]
        for tile in range(plan.unit_tiles):
            members = plan.units[tile * SLOTS : (tile + 1) * SLOTS]
            gather([take(which, k, far if is_far else near, 8) for which, k, is_far in members], 8, tile, outs)


def clear_frame(plan, vec):
    zero = jnp.zeros((16, LANES), F32)
    for t in (0, 1):
        for edge in (0, plan.layers + 1):
            vec[t, edge] = jnp.zeros((plan.buf, LANES), F32)
        for layer in range(1, plan.layers + 1):
            vec[t, layer, pl.ds(0, 16), :] = zero
            vec[t, layer, pl.ds(plan.buf - 16, 16), :] = zero


def table_rows(plan, pairing, tables, t, first, size):
    span = pl.ds(first, size)
    codes = [pairing[0, k, t, span, :] for k in range(plan.pairs)]
    weights = [pairing[1, k, t, span, :] for k in range(plan.pairs)]
    for offset in range(SPAN * SPAN):
        total = jnp.where(codes[0] == offset, weights[0], 0.0)
        for k in range(1, plan.pairs):
            total = total + jnp.where(codes[k] == offset, weights[k], 0.0)
        tables[offset, t, span, :] = total


def prepare_kernel(plan, b0_in, diag_in, codes, weights, b0, diag, pairing, inside, tables, *vecs):
    del b0_in, diag_in
    ix, iy = lax.axis_index("gx"), lax.axis_index("gy")
    rows, layers, buf = plan.rows, plan.layers, plan.buf
    row = lax.broadcasted_iota(jnp.int32, (buf, LANES), 0) + ix * rows - PAD
    lane = lane_iota(buf)
    in_rows = jnp.logical_and(row >= 0, row < plan.nx * rows)
    right = jnp.logical_and(lane < STRIP, iy < plan.ny - 1)
    left = jnp.logical_and(lane >= LANES - STRIP, iy > 0)
    inside[0] = jnp.where(in_rows, 1.0, 0.0)
    inside[1] = jnp.where(jnp.logical_and(in_rows, jnp.logical_or(right, left)), 1.0, 0.0)
    zero = jnp.zeros((PAD, LANES), F32)
    for t in (0, 1):
        for span in (pl.ds(0, PAD), pl.ds(buf - PAD, PAD)):
            for layer in range(layers):
                b0[t, layer + 1, span, :] = zero
                diag[t, layer, span, :] = zero
            for k in range(plan.pairs):
                for i in (0, 1):
                    pairing[i, k, t, span, :] = zero
        for edge in (0, layers + 1):
            b0[t, edge] = jnp.zeros((buf, LANES), F32)
        for offset in range(SPAN * SPAN):
            tables[offset, t, pl.ds(PAD - 16, 8), :] = jnp.zeros((8, LANES), F32)
            tables[offset, t, pl.ds(PAD + rows + 8, 8), :] = jnp.zeros((8, LANES), F32)
    for vec in vecs:
        clear_frame(plan, vec)
    for layer in range(layers):
        diag[0, layer, plan.own, :] = diag[0, layer, plan.own, :] + (6.0 - CENTRE)
    for k in range(plan.pairs):
        pairing[0, k, 0, plan.own, :] = codes[k].astype(F32)
        pairing[1, k, 0, plan.own, :] = weights[k]
    for first, size in chunks(PAD, rows, 32):
        table_rows(plan, pairing, tables, 0, first, size)


def operate(src, at, diag, layer, inside, first, size, tiles=(0, 1), masked=True):
    lane = lane_iota(size)
    start, end = lane == 0, lane == LANES - 1
    rows = pl.ds(first, size)
    middle = [src[t, at, rows, :] for t in (0, 1)]
    before = [pltpu.roll(m, 1, 1) for m in middle]
    after = [pltpu.roll(m, LANES - 1, 1) for m in middle]
    done = []
    for t in tiles:
        total = jnp.where(start, before[1 - t], before[t]) + jnp.where(end, after[1 - t], after[t])
        total = total + src[t, at, pl.ds(first - 1, size), :]
        total = total + src[t, at, pl.ds(first + 1, size), :]
        total = total + (src[t, at - 1, rows, :] + src[t, at + 1, rows, :])
        if masked or t == 1:
            total = total * inside[t, rows, :]
        done.append(diag[t, layer, rows, :] * middle[t] - total)
    return done


def apply_near(plan, src, dst, at, diag, layer, inside):
    parts = [(PAD - 8, 8, True), (PAD + plan.rows, 8, True)]
    parts += [(first, size, False) for first, size in chunks(PAD, plan.rows, 32)]
    values = [
        (first, size, operate(src, at, diag, layer, inside, first, size, masked=masked)) for first, size, masked in parts
    ]
    for first, size, pair in values:
        for t in (0, 1):
            dst[t, at, pl.ds(first, size), :] = pair[t]
    return jnp.concatenate([pair[0] for _, _, pair in values[2:]], axis=0)


def apply_all(plan, src, dst, diag, inside):
    def one(layer, carry):
        apply_near(plan, src, dst, layer + 1, diag, layer, inside)
        return carry

    lax.fori_loop(0, plan.layers, one, 0, unroll=UNROLL)


def apply_own(plan, src, at, diag, layer, inside):
    parts = [
        operate(src, at, diag, layer, inside, first, size, (0,), False)[0] for first, size in chunks(PAD, plan.rows, 32)
    ]
    return jnp.concatenate(parts, axis=0)


def six_sums(parts):
    lane = lax.broadcasted_iota(jnp.int32, (1, LANES), 1)
    row = jnp.zeros((1, LANES), F32)
    for k, part in enumerate(parts):
        row = jnp.where(lane == k, jnp.sum(part), row)
    return row


def fold(value):
    return jnp.sum(value.reshape(-1, 8, LANES), axis=0)


def add_products(sums, v):
    pairs = ((v[0], v[0]), (v[0], v[1]), (v[1], v[1]), (v[1], v[2]), (v[2], v[2]), (v[2], v[3]))
    return tuple(s + fold(a * b) for s, (a, b) in zip(sums, pairs))


def put_moments(moments, sums):
    moments[...] = jnp.broadcast_to(six_sums(sums).reshape(1, 1, LANES), moments.shape)


def no_sums():
    return (jnp.zeros((8, LANES), F32),) * 6


def krylov_kernel(plan, *refs):
    args = Args(refs)
    row_msgs, lane_msgs = args.take(len(plan.sx)), args.take(len(plan.sy))
    corner_msgs = args.take(len(plan.sx) * len(plan.sy))
    inside = args.one()
    args.take(6)
    moments, = args.take(1)
    faces = args.take(len(plan.sb))
    pulled, b0, diag, b1, b2, b3, pairing, tables, shifted = args.take(9)
    ix, iy = lax.axis_index("gx"), lax.axis_index("gy")
    rows, layers = plan.rows, plan.layers

    def put(which, k, t, where, value):
        if which == 0:
            b0[t, k + 1, where, :] = value
        elif which == 1:
            diag[t, k, where, :] = value + (6.0 - CENTRE)
        else:
            pairing[which - 2, k, t, where, :] = value

    def spots(kind):
        up = swap_up(kind, ix)
        near = aligned(jnp.where(up, PAD + rows, PAD - 8))
        far = aligned(jnp.where(up, PAD + rows + 8, PAD - 16))
        return near, far, swap_valid(kind, ix, plan.nx)

    for kind, msg in zip(plan.sx, row_msgs):
        near, far, ok = spots(kind)
        for u, (which, k, is_far) in enumerate(plan.units):
            put(which, k, 0, pl.ds(far if is_far else near, 8), jnp.where(ok, msg[u], 0.0))

    def unpack(msgs, tile, size):
        sides = []
        for right in (True, False):
            total = jnp.zeros((size, LANES), F32)
            for kind, msg in zip(plan.sy, msgs):
                use = jnp.logical_and(swap_up(kind, iy) == right, swap_valid(kind, iy, plan.ny))
                total = jnp.where(use, msg[tile], total)
            sides.append(total)
        even = lax.rem(lane_iota(size) // STRIP, 2) == 0
        return jnp.where(even, sides[1], sides[0]), jnp.where(even, sides[0], sides[1])

    def piece(both, slot):
        turn = STRIP * (SLOTS - 1 - slot)
        return pltpu.roll(both[slot % 2], turn, 1) if turn else both[slot % 2]

    for tile in range(plan.strip_tiles):
        both = unpack(lane_msgs, tile, rows)
        for slot, (which, k) in enumerate(plan.strips[tile * SLOTS : (tile + 1) * SLOTS]):
            put(which, k, 1, plan.own, piece(both, slot))
    for i, row_kind in enumerate(plan.sx):
        near, far, ok = spots(row_kind)
        for tile in range(plan.unit_tiles):
            both = unpack(corner_msgs[i * len(plan.sy) : (i + 1) * len(plan.sy)], tile, 8)
            both = [jnp.where(ok, b, 0.0) for b in both]
            for slot, (which, k, is_far) in enumerate(plan.units[tile * SLOTS : (tile + 1) * SLOTS]):
                put(which, k, 1, pl.ds(far if is_far else near, 8), piece(both, slot))

    for src, dst, wide in ((b0, b1, (0, layers - 2, layers - 1)), (b1, b2, (layers - 1,))):
        apply_all(plan, src, dst, diag, inside)
        for layer in wide:
            for first in (PAD - 16, PAD + rows + 8):
                for t, value in enumerate(operate(src, layer + 1, diag, layer, inside, first, 8)):
                    dst[t, layer + 1, pl.ds(first, 8), :] = value

    def one(layer, sums):
        last = apply_near(plan, b2, b3, layer + 1, diag, layer, inside)
        return add_products(sums, [v[0, layer + 1, plan.own, :] for v in (b0, b1, b2)] + [last])

    put_moments(moments, lax.fori_loop(0, layers, one, no_sums(), unroll=UNROLL))

    for t, first, size in [(0, PAD - 8, 8), (0, PAD + rows, 8)] + [(1, *c) for c in chunks(PAD - 8, plan.face, 40)]:
        table_rows(plan, pairing, tables, t, first, size)
    vecs = (b0, b1, b2)
    wide = pl.ds(PAD - 16, plan.face + 16)
    for k, vec in enumerate(vecs):
        put_shifted(shifted, k, PAD - 16, plan.face + 16, [vec[t, layers, wide, :] for t in (0, 1)])
    send_planes(plan, tables, shifted, pulled, lambda k, t: vecs[k][t, 1, plan.near, :], faces)


def lane_shift(first, second, by, lane):
    if by == 0:
        return first, second
    a, b = pltpu.roll(first, (-by) % LANES, 1), pltpu.roll(second, (-by) % LANES, 1)
    keep = lane < LANES - by if by > 0 else lane >= -by
    return jnp.where(keep, a, b), jnp.where(keep, b, a)


def put_shifted(shifted, n, first, size, planes):
    lane = lane_iota(size)
    for i in range(SPAN):
        for t, value in enumerate(lane_shift(planes[0], planes[1], i - REACH, lane)):
            shifted[n, i, t, pl.ds(first, size), :] = value


def pull(tables, shifted, count, t, first, size):
    total = [jnp.zeros((size, LANES), F32)] * count
    for offset in range(SPAN * SPAN):
        table = tables[offset, t, pl.ds(first, size), :]
        window = pl.ds(first + offset // SPAN - REACH, size)
        for n in range(count):
            total[n] = total[n] + table * shifted[n, offset % SPAN, t, window, :]
    return total


def push(tables, face, first, size, tiles=(0, 1)):
    lane = lane_iota(size)
    total = [jnp.zeros((size, LANES), F32)] * 2
    for i in range(SPAN):
        column = [jnp.zeros((size, LANES), F32)] * 2
        for j in range(SPAN):
            window = pl.ds(first - (j - REACH), size)
            for t in (0, 1):
                column[t] = column[t] + tables[j * SPAN + i, t, window, :] * face[t, window, :]
        moved = lane_shift(column[0], column[1], REACH - i, lane)
        total = [total[t] + moved[t] for t in (0, 1)]
    return [total[t] for t in tiles]


def put_faces(plan, tops, bottoms, outs):
    ib = lax.axis_index("body")
    lane = lane_iota(plan.face)
    for kind, out in zip(plan.sb, outs):
        up = swap_up(kind, ib)
        packed = jnp.zeros((plan.face, LANES), F32)
        for k in range(ORDER):
            out[k] = jnp.where(up, tops(k, 0), bottoms(k, 0))
            strips = pltpu.roll(jnp.where(up, tops(k, 1), bottoms(k, 1)), STRIP + 2 * STRIP * k, 1)
            packed = jnp.where(lane // (2 * STRIP) == k, strips, packed)
        out[ORDER] = packed


def get_face(plan, msgs, coef, up, tiles=(0, 1)):
    ib = lax.axis_index("body")
    total = [jnp.zeros((plan.face, LANES), F32)] * 2
    for kind, msg in zip(plan.sb, msgs):
        use = jnp.logical_and(swap_up(kind, ib) == up, swap_valid(kind, ib, plan.nb))
        for t in tiles:
            if t == 0:
                value = sum(coef[k] * msg[k] for k in range(ORDER))
            else:
                value = sum(
                    coef[k] * pltpu.roll(msg[ORDER], (LANES - STRIP - 2 * STRIP * k) % LANES, 1) for k in range(ORDER)
                )
            total[t] = jnp.where(use, value, total[t])
    return [total[t] for t in tiles]


def send_planes(plan, tables, shifted, pulled, bottoms, faces):
    for t in (0, 1):
        for first, size in chunks(PAD - 8, plan.face, 40):
            for k, value in enumerate(pull(tables, shifted, ORDER, t, first, size)):
                pulled[k, t, pl.ds(first, size), :] = value
    put_faces(plan, lambda k, t: pulled[k, t, plan.near, :], bottoms, faces)


def solve(plan, moments):
    per = plan.nx * plan.ny
    body = lax.broadcasted_iota(jnp.int32, (plan.nb, LANES), 0)
    table = jnp.zeros((plan.nb, LANES), F32)
    for b in range(plan.nb):
        row = [moments[b * per + i] for i in range(per)]
        while len(row) > 1:
            row = [x + y for x, y in zip(row[::2], row[1::2])] + row[len(row) // 2 * 2 :]
        table = jnp.where(body == b, row[0], table)
    lane = lax.broadcasted_iota(jnp.int32, (plan.nb, LANES), 1)
    m = [
        jnp.broadcast_to(jnp.sum(jnp.where(lane == k, table, 0.0), axis=1, keepdims=True), table.shape)
        for k in range(6)
    ]
    h = [m[n + 1] + CENTRE * m[n] for n in range(5)]
    f1, f2 = h[1] / h[0], h[2] / h[0]
    d1 = h[2] - f1 * h[1]
    e = h[3] - f1 * h[2]
    f3 = e / d1
    d2 = h[4] - f2 * h[2] - f3 * e
    g1 = m[1] - f1 * m[0]
    g2 = m[2] - f2 * m[0] - f3 * g1
    c2 = g2 / d2
    c1 = (g1 - e * c2) / d1
    c0 = (m[0] - h[1] * c1 - h[2] * c2) / h[0]

    steady = jnp.minimum(d1 / h[2], d2 / h[4])

    def pick(index):
        return [jnp.sum(jnp.where(body == index, c, 0.0), axis=0, keepdims=True) for c in (c0, c1, c2)]

    ib = lax.axis_index("body")
    return pick(ib), pick(ib + 1), pick(ib - 1), jnp.where(steady > STEADY, 0.0, 1.0)


def residual_coefs(c):
    return 1.0 - CENTRE * c[0], -(c[0] + CENTRE * c[1]), -(c[1] + CENTRE * c[2]), -c[2]


def middle_kernel(plan, moments_in, *refs):
    args = Args(refs)
    msgs = args.take(len(plan.sb))
    basis = args.take(4)
    diag, inside, tables, pulled_in = args.take(4)
    moments, = args.take(1)
    faces = args.take(len(plan.sb))
    vecs = args.take(3)
    base, above_lambda, below_lambda, pulled, doubt, shifted = args.take(6)
    ib = lax.axis_index("body")
    rows, layers = plan.rows, plan.layers
    has_above, has_below = ib < plan.nb - 1, ib > 0
    c, above_c, below_c, doubt[...] = solve(plan, moments_in)
    d = residual_coefs(c)
    near, own = plan.near, plan.own
    for vec in vecs:
        clear_frame(plan, vec)

    def combine(layer, carry):
        for first, size in chunks(PAD - 8, plan.face, 40):
            for t in (0, 1):
                span = pl.ds(first, size)
                vecs[0][t, layer + 1, span, :] = sum(x * v[t, layer + 1, span, :] for x, v in zip(d, basis))
        base[layer] = sum(x * v[0, layer + 1, own, :] for x, v in zip(c, basis))
        return carry

    lax.fori_loop(0, layers, combine, 0)

    zero = jnp.zeros((8, LANES), F32)
    slave = get_face(plan, msgs, above_c, True)
    master = get_face(plan, msgs, below_c, False)
    for t in (0, 1):
        above_lambda[t, pl.ds(PAD - 16, 8), :] = zero
        above_lambda[t, pl.ds(PAD + rows + 8, 8), :] = zero
        gap = slave[t] - sum(x * pulled_in[k, t, near, :] for k, x in enumerate(c))
        above_lambda[t, near, :] = jnp.where(has_above, RATE * gap, 0.0)
        gap = sum(x * basis[k][t, 1, near, :] for k, x in enumerate(c)) - master[t]
        gap = jnp.where(has_below, RATE * gap, 0.0)
        if t == 0:
            below_lambda[...] = gap[8 : 8 + rows]
        vecs[0][t, 1, near, :] = vecs[0][t, 1, near, :] - gap
    for first, size in chunks(PAD - 8, plan.face, 40):
        span = pl.ds(first, size)
        for t, value in enumerate(push(tables, above_lambda, first, size)):
            vecs[0][t, layers, span, :] = vecs[0][t, layers, span, :] + value * inside[t, span, :]

    for step in range(2):
        apply_all(plan, vecs[step], vecs[step + 1], diag, inside)

    def one(layer, sums):
        last = apply_own(plan, vecs[2], layer + 1, diag, layer, inside)
        return add_products(sums, [v[0, layer + 1, own, :] for v in vecs] + [last])

    put_moments(moments, lax.fori_loop(0, layers, one, no_sums(), unroll=UNROLL))

    for k, vec in enumerate(vecs):
        for t in (0, 1):
            for i in range(SPAN):
                shifted[k, i, t, pl.ds(PAD - 16, 8), :] = zero
                shifted[k, i, t, pl.ds(PAD + rows + 8, 8), :] = zero
        put_shifted(shifted, k, PAD - 8, plan.face, [vec[t, layers, near, :] for t in (0, 1)])
    send_planes(plan, tables, shifted, pulled, lambda k, t: vecs[k][t, 1, near, :], faces)


def final_kernel(plan, moments_in, *refs):
    args = Args(refs)
    msgs = args.take(len(plan.sb))
    vecs = args.take(3)
    base, above_lambda, below_lambda, pulled, doubt, tables = args.take(6)
    solution_out, interface_out, again, solution, interface, lifted, sems = args.take(7)
    ib = lax.axis_index("body")
    rows, layers = plan.rows, plan.layers
    has_above, has_below = ib < plan.nb - 1, ib > 0
    inner = pl.ds(1, layers - 2)
    copies = [pltpu.make_async_copy(interface.at[inner], interface_out.at[inner], sems.at[0])]
    for layer in range(1, layers - 1):
        interface[layer] = jnp.zeros((rows, LANES), F32)
    copies[0].start()
    c, above_c, below_c, doubt_now = solve(plan, moments_in)
    again[0, 0] = jnp.where(jnp.max(jnp.maximum(doubt[...], doubt_now)) > 0.5, 1, 0)
    near, own = plan.near, plan.own
    half = layers // 2
    for i, (low, high) in enumerate(((0, half), (half, layers))):

        def combine(layer, carry):
            solution[layer] = base[layer] + sum(x * v[0, layer + 1, own, :] for x, v in zip(c, vecs))
            return carry

        lax.fori_loop(low, high, combine, 0, unroll=UNROLL)
        part = pl.ds(low, high - low)
        copies.append(pltpu.make_async_copy(solution.at[part], solution_out.at[part], sems.at[1 + i]))
        copies[-1].start()

    zero = jnp.zeros((8, LANES), F32)
    master = get_face(plan, msgs, below_c, False, (0,))[0][8 : 8 + rows]
    gap = sum(x * v[0, 1, own, :] for x, v in zip(c, vecs)) - master
    interface[0] = -(2.0 * below_lambda[...] + jnp.where(has_below, RATE * gap, 0.0))
    copies.append(pltpu.make_async_copy(interface.at[0], interface_out.at[0], sems.at[3]))
    copies[-1].start()
    slave = get_face(plan, msgs, above_c, True)
    for t in (0, 1):
        lifted[t, pl.ds(PAD - 16, 8), :] = zero
        lifted[t, pl.ds(PAD + rows + 8, 8), :] = zero
        gap = slave[t] - sum(x * pulled[k, t, near, :] for k, x in enumerate(c))
        lifted[t, near, :] = 2.0 * above_lambda[t, near, :] + jnp.where(has_above, RATE * gap, 0.0)
    interface[layers - 1] = push(tables, lifted, PAD, rows, (0,))[0]
    copies.append(pltpu.make_async_copy(interface.at[layers - 1], interface_out.at[layers - 1], sems.at[4]))
    copies[-1].start()
    for copy in copies:
        copy.wait()


def with_halo(cells, sides, width):
    for axis, dim in sides:
        count = lax.axis_size(axis)
        head = lax.slice_in_dim(cells, 0, width, axis=dim)
        tail = lax.slice_in_dim(cells, cells.shape[dim] - width, cells.shape[dim], axis=dim)
        left = lax.ppermute(tail, axis, [(i, i + 1) for i in range(count - 1)])
        right = lax.ppermute(head, axis, [(i + 1, i) for i in range(count - 1)])
        cells = jnp.concatenate([left, cells, right], axis=dim)
    return cells


def passed_along(array, axis, by):
    count = lax.axis_size(axis)
    return lax.ppermute(array, axis, [(i, i + by) for i in range(count) if 0 <= i + by < count])


def copy_refs(flag, *refs):
    del flag
    half = len(refs) // 2
    for src, dst in zip(refs[:half], refs[half:]):
        dst[...] = src[...]


def step_by_step(load, stiffness, pair_code, pair_weight):
    layers, rows, cols = load.shape
    position = lax.axis_index("body")
    has_above = position < lax.axis_size("body") - 1
    layer_index = lax.broadcasted_iota(jnp.int32, load.shape, 0)
    lateral = (("gx", 0), ("gy", 1))

    def apply_a(vector):
        padded = with_halo(vector, (("gx", 1), ("gy", 2)), 1)
        stacked = jnp.pad(vector, ((1, 1), (0, 0), (0, 0)))
        beside_it = stacked[2:] + stacked[:-2] + padded[:, 2:, 1:-1] + padded[:, :-2, 1:-1]
        beside_it = beside_it + padded[:, 1:-1, 2:] + padded[:, 1:-1, :-2]
        return (6.0 + stiffness) * vector - beside_it

    def body_sum(first, second):
        return lax.psum(jnp.sum(first * second), G)

    offsets = jnp.arange(SPAN * SPAN, dtype=jnp.int32)[:, None, None, None]
    tables = jnp.sum(jnp.where(pair_code[None] == offsets, pair_weight[None], 0.0), axis=1)
    tables_grown = with_halo(tables, (("gx", 1), ("gy", 2)), REACH)

    def update(_, state):
        solution, multiplier, interface_load = state
        residual = load + interface_load - apply_a(solution)

        def inner(_, state):
            solution, residual, direction, norm = state
            image = apply_a(direction)
            alpha = norm / body_sum(direction, image)
            solution = solution + alpha * direction
            residual = residual - alpha * image
            new = body_sum(residual, residual)
            return solution, residual, residual + (new / norm) * direction, new

        start = (solution, residual, residual, body_sum(residual, residual))
        solution = lax.fori_loop(0, ORDER, inner, start)[0]
        master = with_halo(solution[layers - 1], lateral, REACH)
        slave = passed_along(solution[0], "body", -1)

        def pull_one(offset, total):
            window = lax.dynamic_slice(master, (offset // SPAN, offset % SPAN), (rows, cols))
            return total + tables[offset] * window

        pulled = lax.fori_loop(0, SPAN * SPAN, pull_one, jnp.zeros((rows, cols), F32))
        multiplier = jnp.where(has_above, multiplier + RATE * (slave - pulled), 0.0)
        grown = with_halo(multiplier, lateral, REACH)

        def push_one(offset, total):
            at = (2 * REACH - offset // SPAN, 2 * REACH - offset % SPAN)
            return total + lax.dynamic_slice(tables_grown[offset] * grown, at, (rows, cols))

        force = lax.fori_loop(0, SPAN * SPAN, push_one, jnp.zeros((rows, cols), F32))
        lifted = passed_along(multiplier, "body", 1)
        interface_load = jnp.where(layer_index == layers - 1, force[None], 0.0)
        interface_load = interface_load + jnp.where(layer_index == 0, -lifted[None], 0.0)
        return solution, multiplier, interface_load

    state = (jnp.zeros_like(load), jnp.zeros((rows, cols), F32), jnp.zeros_like(load))
    solution, _, interface_load = lax.fori_loop(0, UPDATES, update, state)
    return solution, interface_load


def shaped(*shape):
    return jax.ShapeDtypeStruct(shape, F32)


def held(*shape, dtype=F32):
    return pltpu.VMEM(shape, dtype)


def kept(*shape):
    return pltpu.HBM(shape, F32)


def call(kernel, args, outs, name, scratch=(), aliases=None, hbm_args=()):
    vmem = pl.BlockSpec(memory_space=pltpu.VMEM)
    hbm = pl.BlockSpec(memory_space=pltpu.HBM)
    smem = pl.BlockSpec(memory_space=pltpu.SMEM)
    in_hbm = lambda out: getattr(out, "memory_space", None) == pltpu.HBM
    return pl.pallas_call(
        kernel,
        out_shape=tuple(outs),
        in_specs=[vmem] * len(args) + [hbm] * len(hbm_args),
        out_specs=tuple(hbm if in_hbm(out) else (smem if out.dtype == jnp.int32 and out.shape == (1, 1) else vmem) for out in outs),
        scratch_shapes=list(scratch),
        input_output_aliases=aliases or {},
        compiler_params=pltpu.CompilerParams(vmem_limit_bytes=8 * 1024 * 1024),
        name=name,
    )(*args, *[pltpu.with_memory_space_constraint(x, pltpu.HBM) for x in hbm_args])


def per_device(mesh, load, stiffness, pair_code, pair_weight):
    layers, rows, lanes = load.shape
    pairs = pair_code.shape[0]
    assert lanes == LANES and rows % 8 == 0 and rows >= 16 and layers % 4 == 0
    plan = Plan(mesh, layers, rows, pairs)
    nb, nx, ny = plan.nb, plan.nx, plan.ny
    count = nb * nx * ny
    nf = len(plan.sb)
    buf = plan.buf
    bind = lambda kernel: functools.partial(kernel, plan)
    sems = lambda n: pltpu.SemaphoreType.DMA((n,))

    def lateral(row_kind, lane_kind, array):
        a, b = swap_perm(row_kind, nx), swap_perm(lane_kind, ny)
        return lax.ppermute(array, G, [(i * ny + j, a[i][1] * ny + b[j][1]) for i in range(nx) for j in range(ny)])

    def across(kind, array):
        side = nx * ny
        pairs = []
        for b, to in swap_perm(kind, nb):
            for i in range(side):
                pairs.append((b * side + i, to * side + i) if abs(to - b) == 1 else (b * side + i, b * side + (i ^ 1)))
        return lax.ppermute(array, ALL, pairs)

    def spread(moments, faces):
        return lax.all_to_all(moments, ALL, 0, 0, tiled=True), [across(k, f) for k, f in zip(plan.sb, faces)]

    kinds = [(k, "") for k in plan.sx] + [("", k) for k in plan.sy] + [(a, b) for a in plan.sx for b in plan.sy]
    vec, stack = held(*plan.vec), held(2, layers, buf, LANES)
    face = shaped(ORDER + 1, plan.face, LANES)
    message = shaped(count, 1, LANES)
    planes, mask = held(ORDER, 2, buf, LANES), held(2, buf, LANES)
    pairing, tables = held(2, pairs, 2, buf, LANES), held(SPAN * SPAN, 2, buf, LANES)
    cells = (layers, rows, LANES)
    shifted = pltpu.VMEM((ORDER, SPAN, 2, buf, LANES), F32)

    shapes = [shaped(len(plan.units), 8, LANES) for _ in plan.sx]
    shapes += [shaped(plan.strip_tiles, rows, LANES) for _ in plan.sy]
    shapes += [shaped(plan.unit_tiles, 8, LANES) for _ in plan.sx for _ in plan.sy]
    b0, diag, codes, weights, *packed = call(
        bind(pack_kernel),
        (),
        [vec, stack, held(pairs, rows, LANES, dtype=jnp.int32), held(pairs, rows, LANES)] + shapes,
        "pack",
        [sems(4)],
        hbm_args=(load, stiffness, pair_code, pair_weight),
    )
    halos = [lateral(a, b, m) for (a, b), m in zip(kinds, packed)]
    b0, diag, pair, inside, table, b1, b2 = call(
        bind(prepare_kernel),
        (b0, diag, codes, weights),
        [vec, stack, pairing, mask, tables, vec, vec],
        "prepare",
        aliases={0: 0, 1: 1},
    )
    at = len(halos) + 1
    out_at = 2 + nf
    moments, *rest = call(
        bind(krylov_kernel),
        (*halos, inside, b0, diag, b1, b2, pair, table),
        [message] + [face] * nf + [planes, vec, stack, vec, vec, vec, pairing, tables],
        "krylov",
        [shifted],
        {at: out_at, at + 1: out_at + 1, at + 2: out_at + 2, at + 3: out_at + 3, at + 4: out_at + 5, at + 5: out_at + 6},
    )
    faces, (pulled, b0, diag, b1, b2, b3, _, table) = rest[:nf], rest[nf:]
    moments, faces = spread(moments, faces)
    moments, *rest = call(
        bind(middle_kernel),
        (moments, *faces, b0, b1, b2, b3, diag, inside, table, pulled),
        [message] + [face] * nf + [vec] * 3 + [held(*cells), mask, held(rows, LANES), planes, held(nb, LANES)],
        "middle",
        [shifted],
    )
    faces, kept_arrays = rest[:nf], rest[nf:]
    moments, faces = spread(moments, faces)
    found, lifted, again = call(
        bind(final_kernel),
        (moments, *faces, *kept_arrays, table),
        [kept(*cells)] * 2 + [jax.ShapeDtypeStruct((1, 1), jnp.int32)],
        "final",
        [pltpu.VMEM(cells, F32), pltpu.VMEM(cells, F32), pltpu.VMEM((2, buf, LANES), F32), sems(5)],
    )

    def same(arrays, flag):
        vmem = pl.BlockSpec(memory_space=pltpu.VMEM)
        return pl.pallas_call(
copy_refs,
            out_shape=[jax.ShapeDtypeStruct(a.shape, a.dtype) for a in arrays],
            in_specs=[pl.BlockSpec(memory_space=pltpu.SMEM)] + [vmem] * len(arrays),
            out_specs=[vmem] * len(arrays),
            name="same",
        )(flag, *arrays)

    def redo(state):
        inputs = same((load, stiffness, pair_code, pair_weight), state[2])
        return (*same(step_by_step(*inputs), state[2]), jnp.zeros_like(state[2]))

    found, lifted, _ = lax.while_loop(lambda state: state[2][0, 0] > 0, redo, (found, lifted, again))
    return found, lifted


def solution(mesh):
    return jax.shard_map(
        functools.partial(per_device, mesh),
        mesh=mesh,
        in_specs=(P("body", "gx", "gy"), P("body", "gx", "gy"), P(None, "gx", "gy"), P(None, "gx", "gy")),
        out_specs=(P("body", "gx", "gy"), P("body", "gx", "gy")),
        check_vma=False,
    )
```

```python
import functools

import jax
import jax.numpy as jnp
from jax import lax
from jax.experimental import pallas as pl
from jax.experimental.pallas import tpu as pltpu
from jax.sharding import PartitionSpec as P

REACH = 2
SPAN = 2 * REACH + 1
RATE = 2.0
CENTRE = 7.5
LANES = 128
STRIP = 16
SLOTS = LANES // STRIP
PAD = 24
ORDER = 3
UNROLL = 4
UPDATES = 2
STEADY = 0.05
F32 = jnp.float32
G = ("gx", "gy")
ALL = ("body", "gx", "gy")


def swaps_of(count):
    return () if count < 2 else (("A",) if count == 2 else ("A", "B"))


def swap_perm(kind, count):
    if kind == "":
        return [(i, i) for i in range(count)]
    step = 1 if kind == "A" else -1
    return [(i, (i + (step if i % 2 == 0 else -step)) % count) for i in range(count)]


def swap_up(kind, index):
    even = lax.rem(index, 2) == 0
    return even if kind == "A" else jnp.logical_not(even)


def swap_valid(kind, index, count):
    if kind == "A":
        return index >= 0
    return jnp.where(swap_up(kind, index), index < count - 1, index > 0)


def row_units(layers, pairs):
    wide_load = (0, 1, layers - 3, layers - 2, layers - 1)
    wide_stiff = (0, layers - 3, layers - 2, layers - 1)
    units = []
    for which, wide in ((0, wide_load), (1, wide_stiff)):
        for layer in range(layers):
            units.append((which, layer, False))
            if layer in wide:
                units.append((which, layer, True))
    for which in (2, 3):
        units += [(which, k, False) for k in range(pairs)]
    return units


def strip_list(layers, pairs):
    return [(w, k) for w in (0, 1) for k in range(layers)] + [(w, k) for w in (2, 3) for k in range(pairs)]


def lane_iota(rows):
    return lax.broadcasted_iota(jnp.int32, (rows, LANES), 1)


def aligned(start):
    return pl.multiple_of(start, 8)


def chunks(first, size, step):
    return [(at, min(step, first + size - at)) for at in range(first, first + size, step)]


class Plan:
    def __init__(self, mesh, layers, rows, pairs):
        self.nb, self.nx, self.ny = (mesh.shape[a] for a in ALL)
        self.layers, self.rows, self.pairs = layers, rows, pairs
        self.buf = rows + 2 * PAD
        self.units = row_units(layers, pairs)
        self.strips = strip_list(layers, pairs)
        self.sx, self.sy, self.sb = swaps_of(self.nx), swaps_of(self.ny), swaps_of(self.nb)
        self.face = rows + 16
        self.vec = (2, layers + 2, self.buf, LANES)
        self.own = pl.ds(PAD, rows)
        self.near = pl.ds(PAD - 8, self.face)
        self.unit_tiles = -(-len(self.units) // SLOTS)
        self.strip_tiles = -(-len(self.strips) // SLOTS)


class Args:
    def __init__(self, refs):
        self.refs = list(refs)

    def take(self, count):
        got, self.refs = self.refs[:count], self.refs[count:]
        return got

    def one(self):
        return self.refs.pop(0)


def pack_kernel(plan, load, stiff, code, weight, *refs):
    args = Args(refs)
    b0, diag, codes, weights = args.take(4)
    row_out, lane_out = args.take(len(plan.sx)), args.take(len(plan.sy))
    corner_out = args.take(len(plan.sx) * len(plan.sy))
    sems = args.one()
    ix, iy = lax.axis_index("gx"), lax.axis_index("gy")
    rows, layers = plan.rows, plan.layers
    places = (b0.at[0, pl.ds(1, layers), plan.own, :], diag.at[0, :, plan.own, :], codes, weights)
    copies = [
        pltpu.make_async_copy(src, dst, sems.at[i]) for i, (src, dst) in enumerate(zip((load, stiff, code, weight), places))
    ]
    for copy in copies:
        copy.start()
    arrived = set()

    def take(which, k, start, size):
        if which not in arrived:
            copies[which].wait()
            arrived.add(which)
        if which == 0:
            return b0[0, k + 1, pl.ds(PAD + start, size), :]
        if which == 1:
            return diag[0, k, pl.ds(PAD + start, size), :]
        return (codes, weights)[which - 2][k, pl.ds(start, size), :].astype(F32)

    def starts(kind):
        up = swap_up(kind, ix)
        return aligned(jnp.where(up, rows - 8, 0)), aligned(jnp.where(up, rows - 16, 8))

    def gather(pieces, size, tile, outs):
        slot_of = lane_iota(size) // STRIP
        last, first = jnp.zeros((size, LANES), F32), jnp.zeros((size, LANES), F32)
        for slot, value in enumerate(pieces):
            moved = pltpu.roll(value, STRIP * (slot + 1) % LANES, 1) if slot + 1 < SLOTS else value
            last = jnp.where(slot_of == slot, moved, last)
            first = jnp.where(slot_of == (slot + 1) % SLOTS, moved, first)
        for kind, out in zip(plan.sy, outs):
            out[tile] = jnp.where(swap_up(kind, iy), last, first)

    for kind, out in zip(plan.sx, row_out):
        near, far = starts(kind)
        for u, (which, k, is_far) in enumerate(plan.units):
            out[u] = take(which, k, far if is_far else near, 8)
    for tile in range(plan.strip_tiles):
        members = plan.strips[tile * SLOTS : (tile + 1) * SLOTS]
        gather([take(which, k, 0, rows) for which, k in members], rows, tile, lane_out)
    for i, row_kind in enumerate(plan.sx):
        near, far = starts(row_kind)
        outs = corner_out[i * len(plan.sy) : (i + 1) * len(plan.sy)]
        for tile in range(plan.unit_tiles):
            members = plan.units[tile * SLOTS : (tile + 1) * SLOTS]
            gather([take(which, k, far if is_far else near, 8) for which, k, is_far in members], 8, tile, outs)


def clear_frame(plan, vec):
    zero = jnp.zeros((16, LANES), F32)
    for t in (0, 1):
        for edge in (0, plan.layers + 1):
            vec[t, edge] = jnp.zeros((plan.buf, LANES), F32)
        for layer in range(1, plan.layers + 1):
            vec[t, layer, pl.ds(0, 16), :] = zero
            vec[t, layer, pl.ds(plan.buf - 16, 16), :] = zero


def table_rows(plan, pairing, tables, t, first, size):
    span = pl.ds(first, size)
    codes = [pairing[0, k, t, span, :] for k in range(plan.pairs)]
    weights = [pairing[1, k, t, span, :] for k in range(plan.pairs)]
    for offset in range(SPAN * SPAN):
        total = jnp.where(codes[0] == offset, weights[0], 0.0)
        for k in range(1, plan.pairs):
            total = total + jnp.where(codes[k] == offset, weights[k], 0.0)
        tables[offset, t, span, :] = total


def prepare_kernel(plan, b0_in, diag_in, codes, weights, b0, diag, pairing, inside, tables, *vecs):
    del b0_in, diag_in
    ix, iy = lax.axis_index("gx"), lax.axis_index("gy")
    rows, layers, buf = plan.rows, plan.layers, plan.buf
    row = lax.broadcasted_iota(jnp.int32, (buf, LANES), 0) + ix * rows - PAD
    lane = lane_iota(buf)
    in_rows = jnp.logical_and(row >= 0, row < plan.nx * rows)
    right = jnp.logical_and(lane < STRIP, iy < plan.ny - 1)
    left = jnp.logical_and(lane >= LANES - STRIP, iy > 0)
    inside[0] = jnp.where(in_rows, 1.0, 0.0)
    inside[1] = jnp.where(jnp.logical_and(in_rows, jnp.logical_or(right, left)), 1.0, 0.0)
    zero = jnp.zeros((PAD, LANES), F32)
    for t in (0, 1):
        for span in (pl.ds(0, PAD), pl.ds(buf - PAD, PAD)):
            for layer in range(layers):
                b0[t, layer + 1, span, :] = zero
                diag[t, layer, span, :] = zero
            for k in range(plan.pairs):
                for i in (0, 1):
                    pairing[i, k, t, span, :] = zero
        for edge in (0, layers + 1):
            b0[t, edge] = jnp.zeros((buf, LANES), F32)
        for offset in range(SPAN * SPAN):
            tables[offset, t, pl.ds(PAD - 16, 8), :] = jnp.zeros((8, LANES), F32)
            tables[offset, t, pl.ds(PAD + rows + 8, 8), :] = jnp.zeros((8, LANES), F32)
    for vec in vecs:
        clear_frame(plan, vec)
    for layer in range(layers):
        diag[0, layer, plan.own, :] = diag[0, layer, plan.own, :] + (6.0 - CENTRE)
    for k in range(plan.pairs):
        pairing[0, k, 0, plan.own, :] = codes[k].astype(F32)
        pairing[1, k, 0, plan.own, :] = weights[k]
    for first, size in chunks(PAD, rows, 32):
        table_rows(plan, pairing, tables, 0, first, size)


def operate(src, at, diag, layer, inside, first, size, tiles=(0, 1), masked=True):
    lane = lane_iota(size)
    start, end = lane == 0, lane == LANES - 1
    rows = pl.ds(first, size)
    middle = [src[t, at, rows, :] for t in (0, 1)]
    before = [pltpu.roll(m, 1, 1) for m in middle]
    after = [pltpu.roll(m, LANES - 1, 1) for m in middle]
    done = []
    for t in tiles:
        total = jnp.where(start, before[1 - t], before[t]) + jnp.where(end, after[1 - t], after[t])
        total = total + src[t, at, pl.ds(first - 1, size), :]
        total = total + src[t, at, pl.ds(first + 1, size), :]
        total = total + (src[t, at - 1, rows, :] + src[t, at + 1, rows, :])
        if masked or t == 1:
            total = total * inside[t, rows, :]
        done.append(diag[t, layer, rows, :] * middle[t] - total)
    return done


def apply_rows(src, dst, at, diag, layer, inside, parts):
    values = [operate(src, at, diag, layer, inside, first, size, masked=masked) for first, size, masked in parts]
    for (first, size, _), pair in zip(parts, values):
        for t in (0, 1):
            dst[t, at, pl.ds(first, size), :] = pair[t]
    return [pair[0] for pair in values]


def near_rows(plan):
    outer = [(PAD - 8, 8, True), (PAD + plan.rows, 8, True)]
    return outer + [(first, size, False) for first, size in chunks(PAD, plan.rows, 32)]


def inner_rows(plan, step):
    return [(first, size, False) for first, size in chunks(PAD + 8 * step, plan.rows - 16 * step, 32)]


def outer_rows(plan, step):
    wide = 8 * step
    outer = [(PAD - 8, 8, True), (PAD + plan.rows, 8, True)]
    return outer + [(PAD, wide, False), (PAD + plan.rows - wide, wide, False)]


def apply_all(plan, src, dst, diag, inside, parts):
    def one(layer, carry):
        apply_rows(src, dst, layer + 1, diag, layer, inside, parts)
        return carry

    lax.fori_loop(0, plan.layers, one, 0, unroll=UNROLL)


def apply_own(plan, src, at, diag, layer, inside):
    parts = [
        operate(src, at, diag, layer, inside, first, size, (0,), False)[0] for first, size in chunks(PAD, plan.rows, 32)
    ]
    return jnp.concatenate(parts, axis=0)


def six_sums(parts):
    lane = lax.broadcasted_iota(jnp.int32, (1, LANES), 1)
    row = jnp.zeros((1, LANES), F32)
    for k, part in enumerate(parts):
        row = jnp.where(lane == k, jnp.sum(part), row)
    return row


def fold(value):
    return jnp.sum(value.reshape(-1, 8, LANES), axis=0)


def add_products(sums, v):
    pairs = ((v[0], v[0]), (v[0], v[1]), (v[1], v[1]), (v[1], v[2]), (v[2], v[2]), (v[2], v[3]))
    return tuple(s + fold(a * b) for s, (a, b) in zip(sums, pairs))


def put_moments(moments, sums):
    moments[...] = jnp.broadcast_to(six_sums(sums).reshape(1, 1, LANES), moments.shape)


def no_sums():
    return (jnp.zeros((8, LANES), F32),) * 6


def put_cells(arrays, which, k, t, where, value):
    b0, diag, pairing = arrays
    if which == 0:
        b0[t, k + 1, where, :] = value
    elif which == 1:
        diag[t, k, where, :] = value + (6.0 - CENTRE)
    else:
        pairing[which - 2, k, t, where, :] = value


def unpack(plan, msgs, tile, size):
    iy = lax.axis_index("gy")
    sides = []
    for right in (True, False):
        total = jnp.zeros((size, LANES), F32)
        for kind, msg in zip(plan.sy, msgs):
            use = jnp.logical_and(swap_up(kind, iy) == right, swap_valid(kind, iy, plan.ny))
            total = jnp.where(use, msg[tile], total)
        sides.append(total)
    even = lax.rem(lane_iota(size) // STRIP, 2) == 0
    return jnp.where(even, sides[1], sides[0]), jnp.where(even, sides[0], sides[1])


def piece(both, slot):
    turn = STRIP * (SLOTS - 1 - slot)
    return pltpu.roll(both[slot % 2], turn, 1) if turn else both[slot % 2]


def inner_kernel(plan, *refs):
    args = Args(refs)
    msgs = args.take(len(plan.sy))
    inside, _, _, _, _, _, _ = args.take(7)
    b0, diag, pairing, b1, b2, tables, b3 = args.take(7)
    for tile in range(plan.strip_tiles):
        both = unpack(plan, msgs, tile, plan.rows)
        for slot, (which, k) in enumerate(plan.strips[tile * SLOTS : (tile + 1) * SLOTS]):
            put_cells((b0, diag, pairing), which, k, 1, plan.own, piece(both, slot))
    for step, (src, dst) in enumerate(((b0, b1), (b1, b2), (b2, b3))):
        apply_all(plan, src, dst, diag, inside, inner_rows(plan, step + 1))
    for first, size in chunks(PAD, plan.rows, 32):
        table_rows(plan, pairing, tables, 1, first, size)


def krylov_kernel(plan, *refs):
    args = Args(refs)
    row_msgs = args.take(len(plan.sx))
    corner_msgs = args.take(len(plan.sx) * len(plan.sy))
    inside = args.one()
    args.take(7)
    moments, = args.take(1)
    faces = args.take(len(plan.sb))
    pulled, b0, diag, pairing, b1, b2, tables, b3, shifted = args.take(9)
    ix = lax.axis_index("gx")
    rows, layers = plan.rows, plan.layers
    arrays = (b0, diag, pairing)

    def spots(kind):
        up = swap_up(kind, ix)
        near = aligned(jnp.where(up, PAD + rows, PAD - 8))
        far = aligned(jnp.where(up, PAD + rows + 8, PAD - 16))
        return near, far, swap_valid(kind, ix, plan.nx)

    for kind, msg in zip(plan.sx, row_msgs):
        near, far, ok = spots(kind)
        for u, (which, k, is_far) in enumerate(plan.units):
            put_cells(arrays, which, k, 0, pl.ds(far if is_far else near, 8), jnp.where(ok, msg[u], 0.0))
    for i, row_kind in enumerate(plan.sx):
        near, far, ok = spots(row_kind)
        for tile in range(plan.unit_tiles):
            both = unpack(plan, corner_msgs[i * len(plan.sy) : (i + 1) * len(plan.sy)], tile, 8)
            both = [jnp.where(ok, b, 0.0) for b in both]
            for slot, (which, k, is_far) in enumerate(plan.units[tile * SLOTS : (tile + 1) * SLOTS]):
                put_cells(arrays, which, k, 1, pl.ds(far if is_far else near, 8), piece(both, slot))

    for step, (src, dst, wide) in enumerate(((b0, b1, (0, layers - 2, layers - 1)), (b1, b2, (layers - 1,)))):
        apply_all(plan, src, dst, diag, inside, outer_rows(plan, step + 1))
        for layer in wide:
            for first in (PAD - 16, PAD + rows + 8):
                for t, value in enumerate(operate(src, layer + 1, diag, layer, inside, first, 8)):
                    dst[t, layer + 1, pl.ds(first, 8), :] = value

    middle = pl.ds(PAD + 8 * ORDER, rows - 16 * ORDER)

    def one(layer, sums):
        ends = apply_rows(b2, b3, layer + 1, diag, layer, inside, outer_rows(plan, ORDER))[2:]
        last = jnp.concatenate([ends[0], b3[0, layer + 1, middle, :], ends[1]], axis=0)
        return add_products(sums, [v[0, layer + 1, plan.own, :] for v in (b0, b1, b2)] + [last])

    put_moments(moments, lax.fori_loop(0, layers, one, no_sums(), unroll=UNROLL))

    for t in (0, 1):
        for first in (PAD - 8, PAD + rows):
            table_rows(plan, pairing, tables, t, first, 8)
    vecs = (b0, b1, b2)
    wide = pl.ds(PAD - 16, plan.face + 16)
    for k, vec in enumerate(vecs):
        put_shifted(shifted, k, PAD - 16, plan.face + 16, [vec[t, layers, wide, :] for t in (0, 1)])
    for t in (0, 1):
        for first, size in chunks(PAD - 8, plan.face, 40):
            for k, value in enumerate(pull(tables, shifted, ORDER, t, first, size)):
                pulled[k, t, pl.ds(first, size), :] = value
    put_faces(plan, lambda k, t: pulled[k, t, plan.near, :], lambda k, t: vecs[k][t, 1, plan.near, :], faces)


def lane_shift(first, second, by, lane):
    if by == 0:
        return first, second
    a, b = pltpu.roll(first, (-by) % LANES, 1), pltpu.roll(second, (-by) % LANES, 1)
    keep = lane < LANES - by if by > 0 else lane >= -by
    return jnp.where(keep, a, b), jnp.where(keep, b, a)


def put_shifted(shifted, n, first, size, planes):
    lane = lane_iota(size)
    for i in range(SPAN):
        for t, value in enumerate(lane_shift(planes[0], planes[1], i - REACH, lane)):
            shifted[n, i, t, pl.ds(first, size), :] = value


def pull(tables, shifted, count, t, first, size):
    total = [jnp.zeros((size, LANES), F32)] * count
    for offset in range(SPAN * SPAN):
        table = tables[offset, t, pl.ds(first, size), :]
        window = pl.ds(first + offset // SPAN - REACH, size)
        for n in range(count):
            total[n] = total[n] + table * shifted[n, offset % SPAN, t, window, :]
    return total


def push(tables, face, first, size, tiles=(0, 1)):
    lane = lane_iota(size)
    total = [jnp.zeros((size, LANES), F32)] * 2
    for i in range(SPAN):
        column = [jnp.zeros((size, LANES), F32)] * 2
        for j in range(SPAN):
            window = pl.ds(first - (j - REACH), size)
            for t in (0, 1):
                column[t] = column[t] + tables[j * SPAN + i, t, window, :] * face[t, window, :]
        moved = lane_shift(column[0], column[1], REACH - i, lane)
        total = [total[t] + moved[t] for t in (0, 1)]
    return [total[t] for t in tiles]


def put_faces(plan, tops, bottoms, outs):
    ib = lax.axis_index("body")
    lane = lane_iota(plan.face)
    for kind, out in zip(plan.sb, outs):
        up = swap_up(kind, ib)
        packed = jnp.zeros((plan.face, LANES), F32)
        for k in range(ORDER):
            out[k] = jnp.where(up, tops(k, 0), bottoms(k, 0))
            strips = pltpu.roll(jnp.where(up, tops(k, 1), bottoms(k, 1)), STRIP + 2 * STRIP * k, 1)
            packed = jnp.where(lane // (2 * STRIP) == k, strips, packed)
        out[ORDER] = packed


def get_face(plan, msgs, coef, up, tiles=(0, 1)):
    ib = lax.axis_index("body")
    total = [jnp.zeros((plan.face, LANES), F32)] * 2
    for kind, msg in zip(plan.sb, msgs):
        use = jnp.logical_and(swap_up(kind, ib) == up, swap_valid(kind, ib, plan.nb))
        for t in tiles:
            if t == 0:
                value = sum(coef[k] * msg[k] for k in range(ORDER))
            else:
                value = sum(
                    coef[k] * pltpu.roll(msg[ORDER], (LANES - STRIP - 2 * STRIP * k) % LANES, 1) for k in range(ORDER)
                )
            total[t] = jnp.where(use, value, total[t])
    return [total[t] for t in tiles]


def solve(plan, moments):
    per = plan.nx * plan.ny
    body = lax.broadcasted_iota(jnp.int32, (plan.nb, LANES), 0)
    table = jnp.zeros((plan.nb, LANES), F32)
    for b in range(plan.nb):
        row = [moments[b * per + i] for i in range(per)]
        while len(row) > 1:
            row = [x + y for x, y in zip(row[::2], row[1::2])] + row[len(row) // 2 * 2 :]
        table = jnp.where(body == b, row[0], table)
    lane = lax.broadcasted_iota(jnp.int32, (plan.nb, LANES), 1)
    m = [
        jnp.broadcast_to(jnp.sum(jnp.where(lane == k, table, 0.0), axis=1, keepdims=True), table.shape)
        for k in range(6)
    ]
    h = [m[n + 1] + CENTRE * m[n] for n in range(5)]
    f1, f2 = h[1] / h[0], h[2] / h[0]
    d1 = h[2] - f1 * h[1]
    e = h[3] - f1 * h[2]
    f3 = e / d1
    d2 = h[4] - f2 * h[2] - f3 * e
    g1 = m[1] - f1 * m[0]
    g2 = m[2] - f2 * m[0] - f3 * g1
    c2 = g2 / d2
    c1 = (g1 - e * c2) / d1
    c0 = (m[0] - h[1] * c1 - h[2] * c2) / h[0]

    steady = jnp.minimum(d1 / h[2], d2 / h[4])

    def pick(index):
        return [jnp.sum(jnp.where(body == index, c, 0.0), axis=0, keepdims=True) for c in (c0, c1, c2)]

    ib = lax.axis_index("body")
    return pick(ib), pick(ib + 1), pick(ib - 1), jnp.where(steady > STEADY, 0.0, 1.0)


def residual_coefs(c):
    return 1.0 - CENTRE * c[0], -(c[0] + CENTRE * c[1]), -(c[1] + CENTRE * c[2]), -c[2]


def middle_kernel(plan, moments_in, *refs):
    args = Args(refs)
    msgs = args.take(len(plan.sb))
    basis = args.take(4)
    diag, inside, tables, pulled_in = args.take(4)
    moments, = args.take(1)
    faces = args.take(len(plan.sb))
    vecs = args.take(3)
    base, above_lambda, below_lambda, doubt = args.take(4)
    ib = lax.axis_index("body")
    rows, layers = plan.rows, plan.layers
    has_above, has_below = ib < plan.nb - 1, ib > 0
    c, above_c, below_c, doubt[...] = solve(plan, moments_in)
    d = residual_coefs(c)
    near, own = plan.near, plan.own
    for vec in vecs:
        clear_frame(plan, vec)

    def combine(layer, carry):
        for first, size in chunks(PAD - 8, plan.face, 40):
            for t in (0, 1):
                span = pl.ds(first, size)
                vecs[0][t, layer + 1, span, :] = sum(x * v[t, layer + 1, span, :] for x, v in zip(d, basis))
        base[layer] = sum(x * v[0, layer + 1, own, :] for x, v in zip(c, basis))
        return carry

    lax.fori_loop(0, layers, combine, 0)

    zero = jnp.zeros((8, LANES), F32)
    slave = get_face(plan, msgs, above_c, True)
    master = get_face(plan, msgs, below_c, False)
    for t in (0, 1):
        above_lambda[t, pl.ds(PAD - 16, 8), :] = zero
        above_lambda[t, pl.ds(PAD + rows + 8, 8), :] = zero
        gap = slave[t] - sum(x * pulled_in[k, t, near, :] for k, x in enumerate(c))
        above_lambda[t, near, :] = jnp.where(has_above, RATE * gap, 0.0)
        gap = sum(x * basis[k][t, 1, near, :] for k, x in enumerate(c)) - master[t]
        gap = jnp.where(has_below, RATE * gap, 0.0)
        if t == 0:
            below_lambda[...] = gap[8 : 8 + rows]
        vecs[0][t, 1, near, :] = vecs[0][t, 1, near, :] - gap
    for first, size in chunks(PAD - 8, plan.face, 40):
        span = pl.ds(first, size)
        for t, value in enumerate(push(tables, above_lambda, first, size)):
            vecs[0][t, layers, span, :] = vecs[0][t, layers, span, :] + value * inside[t, span, :]

    for step in range(2):
        apply_all(plan, vecs[step], vecs[step + 1], diag, inside, near_rows(plan))

    def one(layer, sums):
        last = apply_own(plan, vecs[2], layer + 1, diag, layer, inside)
        return add_products(sums, [v[0, layer + 1, own, :] for v in vecs] + [last])

    put_moments(moments, lax.fori_loop(0, layers, one, no_sums(), unroll=UNROLL))

    put_faces(plan, lambda k, t: vecs[k][t, layers, near, :], lambda k, t: vecs[k][t, 1, near, :], faces)


def final_kernel(plan, moments_in, *refs):
    args = Args(refs)
    msgs = args.take(len(plan.sb))
    vecs = args.take(3)
    base, above_lambda, below_lambda, doubt, tables = args.take(5)
    solution_out, interface_out, again, solution, interface, lifted, shifted, sems = args.take(8)
    ib = lax.axis_index("body")
    rows, layers = plan.rows, plan.layers
    has_above, has_below = ib < plan.nb - 1, ib > 0
    inner = pl.ds(1, layers - 2)
    copies = [pltpu.make_async_copy(interface.at[inner], interface_out.at[inner], sems.at[0])]
    for layer in range(1, layers - 1):
        interface[layer] = jnp.zeros((rows, LANES), F32)
    copies[0].start()
    c, above_c, below_c, doubt_now = solve(plan, moments_in)
    again[0, 0] = jnp.where(jnp.max(jnp.maximum(doubt[...], doubt_now)) > 0.5, 1, 0)
    near, own = plan.near, plan.own
    half = layers // 2
    for i, (low, high) in enumerate(((0, half), (half, layers))):

        def combine(layer, carry):
            solution[layer] = base[layer] + sum(x * v[0, layer + 1, own, :] for x, v in zip(c, vecs))
            return carry

        lax.fori_loop(low, high, combine, 0, unroll=UNROLL)
        part = pl.ds(low, high - low)
        copies.append(pltpu.make_async_copy(solution.at[part], solution_out.at[part], sems.at[1 + i]))
        copies[-1].start()

    zero = jnp.zeros((8, LANES), F32)
    for n in (0, 1):
        for t in (0, 1):
            for i in range(SPAN):
                shifted[n, i, t, pl.ds(PAD - 16, 8), :] = zero
                shifted[n, i, t, pl.ds(PAD + rows + 8, 8), :] = zero
    put_shifted(shifted, 0, PAD - 8, plan.face, get_face(plan, msgs, below_c, False))
    top = [sum(x * v[t, layers, near, :] for x, v in zip(c, vecs)) for t in (0, 1)]
    put_shifted(shifted, 1, PAD - 8, plan.face, top)
    master = pull(tables, shifted, 1, 0, PAD, rows)[0]
    gap = sum(x * v[0, 1, own, :] for x, v in zip(c, vecs)) - master
    interface[0] = -(2.0 * below_lambda[...] + jnp.where(has_below, RATE * gap, 0.0))
    copies.append(pltpu.make_async_copy(interface.at[0], interface_out.at[0], sems.at[3]))
    copies[-1].start()
    slave = get_face(plan, msgs, above_c, True)
    for t in (0, 1):
        lifted[t, pl.ds(PAD - 16, 8), :] = zero
        lifted[t, pl.ds(PAD + rows + 8, 8), :] = zero
        for first, size in chunks(PAD - 8, plan.face, 40):
            span = pl.ds(first, size)
            gap = slave[t][first - PAD + 8 : first - PAD + 8 + size] - pull(tables, shifted.at[pl.ds(1, 1)], 1, t, first, size)[0]
            lifted[t, span, :] = 2.0 * above_lambda[t, span, :] + jnp.where(has_above, RATE * gap, 0.0)
    interface[layers - 1] = push(tables, lifted, PAD, rows, (0,))[0]
    copies.append(pltpu.make_async_copy(interface.at[layers - 1], interface_out.at[layers - 1], sems.at[4]))
    copies[-1].start()
    for copy in copies:
        copy.wait()


def with_halo(cells, sides, width):
    for axis, dim in sides:
        count = lax.axis_size(axis)
        head = lax.slice_in_dim(cells, 0, width, axis=dim)
        tail = lax.slice_in_dim(cells, cells.shape[dim] - width, cells.shape[dim], axis=dim)
        left = lax.ppermute(tail, axis, [(i, i + 1) for i in range(count - 1)])
        right = lax.ppermute(head, axis, [(i + 1, i) for i in range(count - 1)])
        cells = jnp.concatenate([left, cells, right], axis=dim)
    return cells


def passed_along(array, axis, by):
    count = lax.axis_size(axis)
    return lax.ppermute(array, axis, [(i, i + by) for i in range(count) if 0 <= i + by < count])


def copy_refs(flag, *refs):
    del flag
    half = len(refs) // 2
    for src, dst in zip(refs[:half], refs[half:]):
        dst[...] = src[...]


def step_by_step(load, stiffness, pair_code, pair_weight):
    layers, rows, cols = load.shape
    position = lax.axis_index("body")
    has_above = position < lax.axis_size("body") - 1
    layer_index = lax.broadcasted_iota(jnp.int32, load.shape, 0)
    lateral = (("gx", 0), ("gy", 1))

    def apply_a(vector):
        padded = with_halo(vector, (("gx", 1), ("gy", 2)), 1)
        stacked = jnp.pad(vector, ((1, 1), (0, 0), (0, 0)))
        beside_it = stacked[2:] + stacked[:-2] + padded[:, 2:, 1:-1] + padded[:, :-2, 1:-1]
        beside_it = beside_it + padded[:, 1:-1, 2:] + padded[:, 1:-1, :-2]
        return (6.0 + stiffness) * vector - beside_it

    def body_sum(first, second):
        return lax.psum(jnp.sum(first * second), G)

    offsets = jnp.arange(SPAN * SPAN, dtype=jnp.int32)[:, None, None, None]
    tables = jnp.sum(jnp.where(pair_code[None] == offsets, pair_weight[None], 0.0), axis=1)
    tables_grown = with_halo(tables, (("gx", 1), ("gy", 2)), REACH)

    def update(_, state):
        solution, multiplier, interface_load = state
        residual = load + interface_load - apply_a(solution)

        def inner(_, state):
            solution, residual, direction, norm = state
            image = apply_a(direction)
            alpha = norm / body_sum(direction, image)
            solution = solution + alpha * direction
            residual = residual - alpha * image
            new = body_sum(residual, residual)
            return solution, residual, residual + (new / norm) * direction, new

        start = (solution, residual, residual, body_sum(residual, residual))
        solution = lax.fori_loop(0, ORDER, inner, start)[0]
        master = with_halo(solution[layers - 1], lateral, REACH)
        slave = passed_along(solution[0], "body", -1)

        def pull_one(offset, total):
            window = lax.dynamic_slice(master, (offset // SPAN, offset % SPAN), (rows, cols))
            return total + tables[offset] * window

        pulled = lax.fori_loop(0, SPAN * SPAN, pull_one, jnp.zeros((rows, cols), F32))
        multiplier = jnp.where(has_above, multiplier + RATE * (slave - pulled), 0.0)
        grown = with_halo(multiplier, lateral, REACH)

        def push_one(offset, total):
            at = (2 * REACH - offset // SPAN, 2 * REACH - offset % SPAN)
            return total + lax.dynamic_slice(tables_grown[offset] * grown, at, (rows, cols))

        force = lax.fori_loop(0, SPAN * SPAN, push_one, jnp.zeros((rows, cols), F32))
        lifted = passed_along(multiplier, "body", 1)
        interface_load = jnp.where(layer_index == layers - 1, force[None], 0.0)
        interface_load = interface_load + jnp.where(layer_index == 0, -lifted[None], 0.0)
        return solution, multiplier, interface_load

    state = (jnp.zeros_like(load), jnp.zeros((rows, cols), F32), jnp.zeros_like(load))
    solution, _, interface_load = lax.fori_loop(0, UPDATES, update, state)
    return solution, interface_load


def shaped(*shape):
    return jax.ShapeDtypeStruct(shape, F32)


def held(*shape, dtype=F32):
    return pltpu.VMEM(shape, dtype)


def kept(*shape):
    return pltpu.HBM(shape, F32)


def call(kernel, args, outs, name, scratch=(), aliases=None, hbm_args=()):
    vmem = pl.BlockSpec(memory_space=pltpu.VMEM)
    hbm = pl.BlockSpec(memory_space=pltpu.HBM)
    smem = pl.BlockSpec(memory_space=pltpu.SMEM)
    in_hbm = lambda out: getattr(out, "memory_space", None) == pltpu.HBM
    return pl.pallas_call(
        kernel,
        out_shape=tuple(outs),
        in_specs=[vmem] * len(args) + [hbm] * len(hbm_args),
        out_specs=tuple(hbm if in_hbm(out) else (smem if out.dtype == jnp.int32 and out.shape == (1, 1) else vmem) for out in outs),
        scratch_shapes=list(scratch),
        input_output_aliases=aliases or {},
        compiler_params=pltpu.CompilerParams(vmem_limit_bytes=8 * 1024 * 1024),
        name=name,
    )(*args, *[pltpu.with_memory_space_constraint(x, pltpu.HBM) for x in hbm_args])


def per_device(mesh, load, stiffness, pair_code, pair_weight):
    layers, rows, lanes = load.shape
    pairs = pair_code.shape[0]
    assert lanes == LANES and rows % 8 == 0 and rows >= 16 * ORDER + 8 and layers % 4 == 0
    plan = Plan(mesh, layers, rows, pairs)
    nb, nx, ny = plan.nb, plan.nx, plan.ny
    count = nb * nx * ny
    nf = len(plan.sb)
    buf = plan.buf
    bind = lambda kernel: functools.partial(kernel, plan)
    sems = lambda n: pltpu.SemaphoreType.DMA((n,))

    def lateral(row_kind, lane_kind, array):
        a, b = swap_perm(row_kind, nx), swap_perm(lane_kind, ny)
        return lax.ppermute(array, G, [(i * ny + j, a[i][1] * ny + b[j][1]) for i in range(nx) for j in range(ny)])

    def across(kind, array):
        side = nx * ny
        pairs = []
        for b, to in swap_perm(kind, nb):
            for i in range(side):
                pairs.append((b * side + i, to * side + i) if abs(to - b) == 1 else (b * side + i, b * side + (i ^ 1)))
        return lax.ppermute(array, ALL, pairs)

    def spread(moments, faces):
        return lax.all_to_all(moments, ALL, 0, 0, tiled=True), [across(k, f) for k, f in zip(plan.sb, faces)]

    kinds = [(k, "") for k in plan.sx] + [("", k) for k in plan.sy] + [(a, b) for a in plan.sx for b in plan.sy]
    vec, stack = held(*plan.vec), held(2, layers, buf, LANES)
    face = shaped(ORDER + 1, plan.face, LANES)
    message = shaped(count, 1, LANES)
    planes, mask = held(ORDER, 2, buf, LANES), held(2, buf, LANES)
    pairing, tables = held(2, pairs, 2, buf, LANES), held(SPAN * SPAN, 2, buf, LANES)
    cells = (layers, rows, LANES)
    shifted = pltpu.VMEM((ORDER, SPAN, 2, buf, LANES), F32)

    shapes = [shaped(len(plan.units), 8, LANES) for _ in plan.sx]
    shapes += [shaped(plan.strip_tiles, rows, LANES) for _ in plan.sy]
    shapes += [shaped(plan.unit_tiles, 8, LANES) for _ in plan.sx for _ in plan.sy]
    b0, diag, codes, weights, *packed = call(
        bind(pack_kernel),
        (),
        [vec, stack, held(pairs, rows, LANES, dtype=jnp.int32), held(pairs, rows, LANES)] + shapes,
        "pack",
        [sems(4)],
        hbm_args=(load, stiffness, pair_code, pair_weight),
    )
    halos = [lateral(a, b, m) for (a, b), m in zip(kinds, packed)]
    b0, diag, pair, inside, table, b1, b2 = call(
        bind(prepare_kernel),
        (b0, diag, codes, weights),
        [vec, stack, pairing, mask, tables, vec, vec],
        "prepare",
        aliases={0: 0, 1: 1},
    )
    nx_msgs, ny_msgs = len(plan.sx), len(plan.sy)
    row_halos, lane_halos, corner_halos = halos[:nx_msgs], halos[nx_msgs : nx_msgs + ny_msgs], halos[nx_msgs + ny_msgs :]
    b0, diag, pair, b1, b2, table, b3 = call(
        bind(inner_kernel),
        (*lane_halos, inside, b0, diag, pair, b1, b2, table),
        [vec, stack, pairing, vec, vec, tables, vec],
        "inner",
        aliases={ny_msgs + 1 + i: i for i in range(6)},
    )
    at = len(row_halos) + len(corner_halos) + 1
    moments, *rest = call(
        bind(krylov_kernel),
        (*row_halos, *corner_halos, inside, b0, diag, pair, b1, b2, table, b3),
        [message] + [face] * nf + [planes, vec, stack, pairing, vec, vec, tables, vec],
        "krylov",
        [shifted],
        {at + i: 2 + nf + i for i in range(7)},
    )
    faces, (pulled, b0, diag, _, b1, b2, table, b3) = rest[:nf], rest[nf:]
    moments, faces = spread(moments, faces)
    moments, *rest = call(
        bind(middle_kernel),
        (moments, *faces, b0, b1, b2, b3, diag, inside, table, pulled),
        [message] + [face] * nf + [vec] * 3 + [held(*cells), mask, held(rows, LANES), held(nb, LANES)],
        "middle",
    )
    faces, kept_arrays = rest[:nf], rest[nf:]
    moments, faces = spread(moments, faces)
    found, lifted, again = call(
        bind(final_kernel),
        (moments, *faces, *kept_arrays, table),
        [kept(*cells)] * 2 + [jax.ShapeDtypeStruct((1, 1), jnp.int32)],
        "final",
        [pltpu.VMEM(cells, F32), pltpu.VMEM(cells, F32), pltpu.VMEM((2, buf, LANES), F32), shifted, sems(5)],
    )

    def same(arrays, flag):
        vmem = pl.BlockSpec(memory_space=pltpu.VMEM)
        return pl.pallas_call(
copy_refs,
            out_shape=[jax.ShapeDtypeStruct(a.shape, a.dtype) for a in arrays],
            in_specs=[pl.BlockSpec(memory_space=pltpu.SMEM)] + [vmem] * len(arrays),
            out_specs=[vmem] * len(arrays),
            name="same",
        )(flag, *arrays)

    def redo(state):
        inputs = same((load, stiffness, pair_code, pair_weight), state[2])
        return (*same(step_by_step(*inputs), state[2]), jnp.zeros_like(state[2]))

    found, lifted, _ = lax.while_loop(lambda state: state[2][0, 0] > 0, redo, (found, lifted, again))
    return found, lifted


def solution(mesh):
    return jax.shard_map(
        functools.partial(per_device, mesh),
        mesh=mesh,
        in_specs=(P("body", "gx", "gy"), P("body", "gx", "gy"), P(None, "gx", "gy"), P(None, "gx", "gy")),
        out_specs=(P("body", "gx", "gy"), P("body", "gx", "gy")),
        check_vma=False,
    )
```

```python
import functools
import itertools

import jax
import jax.numpy as jnp
from jax import lax
from jax.experimental import pallas as pl
from jax.experimental.pallas import tpu as pltpu
from jax.sharding import PartitionSpec as P

REACH = 2
SPAN = 2 * REACH + 1
RATE = 2.0
CENTRE = 7.5
LANES = 128
STRIP = 16
SLOTS = LANES // STRIP
PAD = 24
ORDER = 3
UNROLL = 4
UPDATES = 2
STEADY = 0.05
F32 = jnp.float32
G = ("gx", "gy")
ALL = ("body", "gx", "gy")


def swaps_of(count):
    return () if count < 2 else (("A",) if count == 2 else ("A", "B"))


def swap_perm(kind, count):
    if kind == "":
        return [(i, i) for i in range(count)]
    step = 1 if kind == "A" else -1
    return [(i, (i + (step if i % 2 == 0 else -step)) % count) for i in range(count)]


def swap_up(kind, index):
    even = lax.rem(index, 2) == 0
    return even if kind == "A" else jnp.logical_not(even)


def swap_valid(kind, index, count):
    if kind == "A":
        return index >= 0
    return jnp.where(swap_up(kind, index), index < count - 1, index > 0)


def row_units(layers, pairs):
    wide_load = (0, 1, layers - 3, layers - 2, layers - 1)
    wide_stiff = (0, layers - 3, layers - 2, layers - 1)
    units = []
    for which, wide in ((0, wide_load), (1, wide_stiff)):
        for layer in range(layers):
            units.append((which, layer, False))
            if layer in wide:
                units.append((which, layer, True))
    for which in (2, 3):
        units += [(which, k, False) for k in range(pairs)]
    return units


def strip_list(layers, pairs):
    return [(w, k) for w in (0, 1) for k in range(layers)] + [(w, k) for w in (2, 3) for k in range(pairs)]


def lane_iota(rows):
    return lax.broadcasted_iota(jnp.int32, (rows, LANES), 1)


def aligned(start):
    return pl.multiple_of(start, 8)


def chunks(first, size, step):
    return [(at, min(step, first + size - at)) for at in range(first, first + size, step)]


class Plan:
    def __init__(self, mesh, layers, rows, pairs):
        self.nb, self.nx, self.ny = (mesh.shape[a] for a in ALL)
        self.layers, self.rows, self.pairs = layers, rows, pairs
        self.buf = rows + 2 * PAD
        self.units = row_units(layers, pairs)
        self.strips = strip_list(layers, pairs)
        self.sx, self.sy, self.sb = swaps_of(self.nx), swaps_of(self.ny), swaps_of(self.nb)
        self.face = rows + 16
        self.vec = (2, layers + 2, self.buf, LANES)
        self.own = pl.ds(PAD, rows)
        self.near = pl.ds(PAD - 8, self.face)
        self.unit_tiles = -(-len(self.units) // SLOTS)
        self.strip_tiles = -(-len(self.strips) // SLOTS)


class Args:
    def __init__(self, refs):
        self.refs = list(refs)

    def take(self, count):
        got, self.refs = self.refs[:count], self.refs[count:]
        return got

    def one(self):
        return self.refs.pop(0)


def pack_kernel(plan, load, stiff, code, weight, *refs):
    args = Args(refs)
    b0, diag, codes, weights = args.take(4)
    row_out, lane_out = args.take(len(plan.sx)), args.take(len(plan.sy))
    corner_out = args.take(len(plan.sx) * len(plan.sy))
    sems = args.one()
    ix, iy = lax.axis_index("gx"), lax.axis_index("gy")
    rows, layers = plan.rows, plan.layers
    places = (b0.at[0, pl.ds(1, layers), plan.own, :], diag.at[0, :, plan.own, :], codes, weights)
    copies = [
        pltpu.make_async_copy(src, dst, sems.at[i]) for i, (src, dst) in enumerate(zip((load, stiff, code, weight), places))
    ]
    for copy in copies:
        copy.start()
    arrived = set()

    def take(which, k, start, size):
        if which not in arrived:
            copies[which].wait()
            arrived.add(which)
        if which == 0:
            return b0[0, k + 1, pl.ds(PAD + start, size), :]
        if which == 1:
            return diag[0, k, pl.ds(PAD + start, size), :]
        return (codes, weights)[which - 2][k, pl.ds(start, size), :].astype(F32)

    def starts(kind):
        up = swap_up(kind, ix)
        return aligned(jnp.where(up, rows - 8, 0)), aligned(jnp.where(up, rows - 16, 8))

    def gather(pieces, size, tile, outs):
        slot_of = lane_iota(size) // STRIP
        last, first = jnp.zeros((size, LANES), F32), jnp.zeros((size, LANES), F32)
        for slot, value in enumerate(pieces):
            moved = pltpu.roll(value, STRIP * (slot + 1) % LANES, 1) if slot + 1 < SLOTS else value
            last = jnp.where(slot_of == slot, moved, last)
            first = jnp.where(slot_of == (slot + 1) % SLOTS, moved, first)
        for kind, out in zip(plan.sy, outs):
            out[tile] = jnp.where(swap_up(kind, iy), last, first)

    for kind, out in zip(plan.sx, row_out):
        near, far = starts(kind)
        for u, (which, k, is_far) in enumerate(plan.units):
            out[u] = take(which, k, far if is_far else near, 8)
    for tile in range(plan.strip_tiles):
        members = plan.strips[tile * SLOTS : (tile + 1) * SLOTS]
        gather([take(which, k, 0, rows) for which, k in members], rows, tile, lane_out)
    for i, row_kind in enumerate(plan.sx):
        near, far = starts(row_kind)
        outs = corner_out[i * len(plan.sy) : (i + 1) * len(plan.sy)]
        for tile in range(plan.unit_tiles):
            members = plan.units[tile * SLOTS : (tile + 1) * SLOTS]
            gather([take(which, k, far if is_far else near, 8) for which, k, is_far in members], 8, tile, outs)


def clear_frame(plan, vec):
    zero = jnp.zeros((16, LANES), F32)
    for t in (0, 1):
        for edge in (0, plan.layers + 1):
            vec[t, edge] = jnp.zeros((plan.buf, LANES), F32)
        for layer in range(1, plan.layers + 1):
            vec[t, layer, pl.ds(0, 16), :] = zero
            vec[t, layer, pl.ds(plan.buf - 16, 16), :] = zero


def table_rows(plan, pairing, tables, t, first, size):
    span = pl.ds(first, size)
    codes = [pairing[0, k, t, span, :] for k in range(plan.pairs)]
    weights = [pairing[1, k, t, span, :] for k in range(plan.pairs)]
    for offset in range(SPAN * SPAN):
        total = jnp.where(codes[0] == offset, weights[0], 0.0)
        for k in range(1, plan.pairs):
            total = total + jnp.where(codes[k] == offset, weights[k], 0.0)
        tables[offset, t, span, :] = total


def prepare_kernel(plan, b0_in, diag_in, codes, weights, b0, diag, pairing, inside, tables, *vecs):
    del b0_in, diag_in
    ix, iy = lax.axis_index("gx"), lax.axis_index("gy")
    rows, layers, buf = plan.rows, plan.layers, plan.buf
    row = lax.broadcasted_iota(jnp.int32, (buf, LANES), 0) + ix * rows - PAD
    lane = lane_iota(buf)
    in_rows = jnp.logical_and(row >= 0, row < plan.nx * rows)
    right = jnp.logical_and(lane < STRIP, iy < plan.ny - 1)
    left = jnp.logical_and(lane >= LANES - STRIP, iy > 0)
    inside[0] = jnp.where(in_rows, 1.0, 0.0)
    inside[1] = jnp.where(jnp.logical_and(in_rows, jnp.logical_or(right, left)), 1.0, 0.0)
    zero = jnp.zeros((PAD, LANES), F32)
    for t in (0, 1):
        for span in (pl.ds(0, PAD), pl.ds(buf - PAD, PAD)):
            for layer in range(layers):
                b0[t, layer + 1, span, :] = zero
                diag[t, layer, span, :] = zero
            for k in range(plan.pairs):
                for i in (0, 1):
                    pairing[i, k, t, span, :] = zero
        for edge in (0, layers + 1):
            b0[t, edge] = jnp.zeros((buf, LANES), F32)
        for offset in range(SPAN * SPAN):
            tables[offset, t, pl.ds(PAD - 16, 8), :] = jnp.zeros((8, LANES), F32)
            tables[offset, t, pl.ds(PAD + rows + 8, 8), :] = jnp.zeros((8, LANES), F32)
    for vec in vecs:
        clear_frame(plan, vec)
    for layer in range(layers):
        diag[0, layer, plan.own, :] = diag[0, layer, plan.own, :] + (6.0 - CENTRE)
    for k in range(plan.pairs):
        pairing[0, k, 0, plan.own, :] = codes[k].astype(F32)
        pairing[1, k, 0, plan.own, :] = weights[k]
    for first, size in chunks(PAD, rows, 32):
        table_rows(plan, pairing, tables, 0, first, size)


def operate(src, at, diag, layer, inside, first, size, tiles=(0, 1), masked=True):
    lane = lane_iota(size)
    start, end = lane == 0, lane == LANES - 1
    rows = pl.ds(first, size)
    middle = [src[t, at, rows, :] for t in (0, 1)]
    before = [pltpu.roll(m, 1, 1) for m in middle]
    after = [pltpu.roll(m, LANES - 1, 1) for m in middle]
    done = []
    for t in tiles:
        total = jnp.where(start, before[1 - t], before[t]) + jnp.where(end, after[1 - t], after[t])
        total = total + src[t, at, pl.ds(first - 1, size), :]
        total = total + src[t, at, pl.ds(first + 1, size), :]
        total = total + (src[t, at - 1, rows, :] + src[t, at + 1, rows, :])
        if masked or t == 1:
            total = total * inside[t, rows, :]
        done.append(diag[t, layer, rows, :] * middle[t] - total)
    return done


def apply_rows(src, dst, at, diag, layer, inside, parts):
    values = [operate(src, at, diag, layer, inside, first, size, masked=masked) for first, size, masked in parts]
    for (first, size, _), pair in zip(parts, values):
        for t in (0, 1):
            dst[t, at, pl.ds(first, size), :] = pair[t]
    return [pair[0] for pair in values]


def apply_joined(src, dst, at, diag, layer, inside, parts):
    spans = [pl.ds(first, size) for first, size, _ in parts]
    size = sum(p[1] for p in parts)
    lane = lane_iota(size)
    start, end = lane == 0, lane == LANES - 1
    join = lambda values: values[0] if len(values) == 1 else jnp.concatenate(values, axis=0)
    middle = [join([src[t, at, span, :] for span in spans]) for t in (0, 1)]
    before = [pltpu.roll(m, 1, 1) for m in middle]
    after = [pltpu.roll(m, LANES - 1, 1) for m in middle]
    done = []
    for t in (0, 1):
        sides = jnp.where(start, before[1 - t], before[t]) + jnp.where(end, after[1 - t], after[t])
        values, low = [], 0
        for (first, rows, masked), span in zip(parts, spans):
            total = sides[low : low + rows]
            total = total + src[t, at, pl.ds(first - 1, rows), :]
            total = total + src[t, at, pl.ds(first + 1, rows), :]
            total = total + (src[t, at - 1, span, :] + src[t, at + 1, span, :])
            if masked or t == 1:
                total = total * inside[t, span, :]
            values.append(diag[t, layer, span, :] * middle[t][low : low + rows] - total)
            low += rows
        done.append(values)
    for i, span in enumerate(spans):
        for t in (0, 1):
            dst[t, at, span, :] = done[t][i]
    return done[0]


def near_rows(plan):
    outer = [(PAD - 8, 8, True), (PAD + plan.rows, 8, True)]
    return outer + [(first, size, False) for first, size in chunks(PAD, plan.rows, 32)]


def inner_rows(plan, step):
    return [(first, size, False) for first, size in chunks(PAD + 8 * step, plan.rows - 16 * step, 32)]


def outer_rows(plan, step):
    wide = 8 * step
    outer = [(PAD - 8, 8, True), (PAD + plan.rows, 8, True)]
    return outer + [(PAD, wide, False), (PAD + plan.rows - wide, wide, False)]


def apply_all(plan, src, dst, diag, inside, parts, apply=apply_rows):
    def one(layer, carry):
        apply(src, dst, layer + 1, diag, layer, inside, parts)
        return carry

    lax.fori_loop(0, plan.layers, one, 0, unroll=UNROLL)


def apply_own(plan, src, at, diag, layer, inside):
    parts = [
        operate(src, at, diag, layer, inside, first, size, (0,), False)[0] for first, size in chunks(PAD, plan.rows, 32)
    ]
    return jnp.concatenate(parts, axis=0)


def six_sums(parts):
    lane = lax.broadcasted_iota(jnp.int32, (1, LANES), 1)
    row = jnp.zeros((1, LANES), F32)
    for k, part in enumerate(parts):
        row = jnp.where(lane == k, jnp.sum(part), row)
    return row


def fold(value):
    return jnp.sum(value.reshape(-1, 8, LANES), axis=0)


def add_products(sums, v):
    pairs = ((v[0], v[0]), (v[0], v[1]), (v[1], v[1]), (v[1], v[2]), (v[2], v[2]), (v[2], v[3]))
    return tuple(s + fold(a * b) for s, (a, b) in zip(sums, pairs))


def put_moments(moments, sums):
    moments[...] = jnp.broadcast_to(six_sums(sums).reshape(1, 1, LANES), moments.shape)


def no_sums():
    return (jnp.zeros((8, LANES), F32),) * 6


def put_cells(arrays, which, k, t, where, value):
    b0, diag, pairing = arrays
    if which == 0:
        b0[t, k + 1, where, :] = value
    elif which == 1:
        diag[t, k, where, :] = value + (6.0 - CENTRE)
    else:
        pairing[which - 2, k, t, where, :] = value


def unpack(plan, msgs, tile, size):
    iy = lax.axis_index("gy")
    sides = []
    for right in (True, False):
        total = jnp.zeros((size, LANES), F32)
        for kind, msg in zip(plan.sy, msgs):
            use = jnp.logical_and(swap_up(kind, iy) == right, swap_valid(kind, iy, plan.ny))
            total = jnp.where(use, msg[tile], total)
        sides.append(total)
    even = lax.rem(lane_iota(size) // STRIP, 2) == 0
    return jnp.where(even, sides[1], sides[0]), jnp.where(even, sides[0], sides[1])


def piece(both, slot):
    turn = STRIP * (SLOTS - 1 - slot)
    return pltpu.roll(both[slot % 2], turn, 1) if turn else both[slot % 2]


def inner_kernel(plan, *refs):
    args = Args(refs)
    msgs = args.take(len(plan.sy))
    inside, _, _, _, _, _, _ = args.take(7)
    b0, diag, pairing, b1, b2, tables, b3 = args.take(7)
    for tile in range(plan.strip_tiles):
        both = unpack(plan, msgs, tile, plan.rows)
        for slot, (which, k) in enumerate(plan.strips[tile * SLOTS : (tile + 1) * SLOTS]):
            put_cells((b0, diag, pairing), which, k, 1, plan.own, piece(both, slot))
    for step, (src, dst) in enumerate(((b0, b1), (b1, b2), (b2, b3))):
        apply_all(plan, src, dst, diag, inside, inner_rows(plan, step + 1))
    for first, size in chunks(PAD, plan.rows, 32):
        table_rows(plan, pairing, tables, 1, first, size)


def krylov_kernel(plan, *refs):
    args = Args(refs)
    row_msgs = args.take(len(plan.sx))
    corner_msgs = args.take(len(plan.sx) * len(plan.sy))
    inside = args.one()
    args.take(7)
    moments, = args.take(1)
    faces = args.take(len(plan.sb))
    b0, diag, pairing, b1, b2, tables, b3 = args.take(7)
    ix = lax.axis_index("gx")
    rows, layers = plan.rows, plan.layers
    arrays = (b0, diag, pairing)

    def spots(kind):
        up = swap_up(kind, ix)
        near = aligned(jnp.where(up, PAD + rows, PAD - 8))
        far = aligned(jnp.where(up, PAD + rows + 8, PAD - 16))
        return near, far, swap_valid(kind, ix, plan.nx)

    for kind, msg in zip(plan.sx, row_msgs):
        near, far, ok = spots(kind)
        for u, (which, k, is_far) in enumerate(plan.units):
            put_cells(arrays, which, k, 0, pl.ds(far if is_far else near, 8), jnp.where(ok, msg[u], 0.0))
    for i, row_kind in enumerate(plan.sx):
        near, far, ok = spots(row_kind)
        for tile in range(plan.unit_tiles):
            both = unpack(plan, corner_msgs[i * len(plan.sy) : (i + 1) * len(plan.sy)], tile, 8)
            both = [jnp.where(ok, b, 0.0) for b in both]
            for slot, (which, k, is_far) in enumerate(plan.units[tile * SLOTS : (tile + 1) * SLOTS]):
                put_cells(arrays, which, k, 1, pl.ds(far if is_far else near, 8), piece(both, slot))

    for step, (src, dst, wide) in enumerate(((b0, b1, (0, layers - 2, layers - 1)), (b1, b2, (layers - 1,)))):
        apply_all(plan, src, dst, diag, inside, outer_rows(plan, step + 1), apply_joined)
        for layer in wide:
            for first in (PAD - 16, PAD + rows + 8):
                for t, value in enumerate(operate(src, layer + 1, diag, layer, inside, first, 8)):
                    dst[t, layer + 1, pl.ds(first, 8), :] = value

    middle = pl.ds(PAD + 8 * ORDER, rows - 16 * ORDER)

    def one(layer, sums):
        ends = apply_joined(b2, b3, layer + 1, diag, layer, inside, outer_rows(plan, ORDER))[2:]
        last = jnp.concatenate([ends[0], b3[0, layer + 1, middle, :], ends[1]], axis=0)
        return add_products(sums, [v[0, layer + 1, plan.own, :] for v in (b0, b1, b2)] + [last])

    put_moments(moments, lax.fori_loop(0, layers, one, no_sums(), unroll=UNROLL))

    for t in (0, 1):
        for first in (PAD - 8, PAD + rows):
            table_rows(plan, pairing, tables, t, first, 8)
    vecs = (b0, b1, b2)
    put_faces(plan, lambda k, t: vecs[k][t, layers, plan.near, :], lambda k, t: vecs[k][t, 1, plan.near, :], faces)


def lane_shift(first, second, by, lane):
    if by == 0:
        return first, second
    a, b = pltpu.roll(first, (-by) % LANES, 1), pltpu.roll(second, (-by) % LANES, 1)
    keep = lane < LANES - by if by > 0 else lane >= -by
    return jnp.where(keep, a, b), jnp.where(keep, b, a)


def put_shifted(shifted, n, first, size, planes):
    lane = lane_iota(size)
    for i in range(SPAN):
        for t, value in enumerate(lane_shift(planes[0], planes[1], i - REACH, lane)):
            shifted[n, i, t, pl.ds(first, size), :] = value


def pull(tables, shifted, count, t, first, size):
    total = [jnp.zeros((size, LANES), F32)] * count
    for offset in range(SPAN * SPAN):
        table = tables[offset, t, pl.ds(first, size), :]
        window = pl.ds(first + offset // SPAN - REACH, size)
        for n in range(count):
            total[n] = total[n] + table * shifted[n, offset % SPAN, t, window, :]
    return total


def push(tables, face, first, size, tiles=(0, 1)):
    lane = lane_iota(size)
    total = [jnp.zeros((size, LANES), F32)] * 2
    for i in range(SPAN):
        column = [jnp.zeros((size, LANES), F32)] * 2
        for j in range(SPAN):
            window = pl.ds(first - (j - REACH), size)
            for t in (0, 1):
                column[t] = column[t] + tables[j * SPAN + i, t, window, :] * face[t, window, :]
        moved = lane_shift(column[0], column[1], REACH - i, lane)
        total = [total[t] + moved[t] for t in (0, 1)]
    return [total[t] for t in tiles]


def put_faces(plan, tops, bottoms, outs):
    ib = lax.axis_index("body")
    lane = lane_iota(plan.face)
    for kind, out in zip(plan.sb, outs):
        up = swap_up(kind, ib)
        packed = jnp.zeros((plan.face, LANES), F32)
        for k in range(ORDER):
            out[k] = jnp.where(up, tops(k, 0), bottoms(k, 0))
            strips = pltpu.roll(jnp.where(up, tops(k, 1), bottoms(k, 1)), STRIP + 2 * STRIP * k, 1)
            packed = jnp.where(lane // (2 * STRIP) == k, strips, packed)
        out[ORDER] = packed


def get_face(plan, msgs, coef, up, tiles=(0, 1)):
    ib = lax.axis_index("body")
    total = [jnp.zeros((plan.face, LANES), F32)] * 2
    for kind, msg in zip(plan.sb, msgs):
        use = jnp.logical_and(swap_up(kind, ib) == up, swap_valid(kind, ib, plan.nb))
        for t in tiles:
            if t == 0:
                value = sum(coef[k] * msg[k] for k in range(ORDER))
            else:
                value = sum(
                    coef[k] * pltpu.roll(msg[ORDER], (LANES - STRIP - 2 * STRIP * k) % LANES, 1) for k in range(ORDER)
                )
            total[t] = jnp.where(use, value, total[t])
    return [total[t] for t in tiles]


def solve(plan, moments):
    per = plan.nx * plan.ny
    body = lax.broadcasted_iota(jnp.int32, (plan.nb, LANES), 0)
    table = jnp.zeros((plan.nb, LANES), F32)
    for b in range(plan.nb):
        row = [moments[b * per + i] for i in range(per)]
        while len(row) > 1:
            row = [x + y for x, y in zip(row[::2], row[1::2])] + row[len(row) // 2 * 2 :]
        table = jnp.where(body == b, row[0], table)
    lane = lax.broadcasted_iota(jnp.int32, (plan.nb, LANES), 1)
    m = [
        jnp.broadcast_to(jnp.sum(jnp.where(lane == k, table, 0.0), axis=1, keepdims=True), table.shape)
        for k in range(6)
    ]
    h = [m[n + 1] + CENTRE * m[n] for n in range(5)]
    f1, f2 = h[1] / h[0], h[2] / h[0]
    d1 = h[2] - f1 * h[1]
    e = h[3] - f1 * h[2]
    f3 = e / d1
    d2 = h[4] - f2 * h[2] - f3 * e
    g1 = m[1] - f1 * m[0]
    g2 = m[2] - f2 * m[0] - f3 * g1
    c2 = g2 / d2
    c1 = (g1 - e * c2) / d1
    c0 = (m[0] - h[1] * c1 - h[2] * c2) / h[0]

    steady = jnp.minimum(d1 / h[2], d2 / h[4])

    def pick(index):
        return [jnp.sum(jnp.where(body == index, c, 0.0), axis=0, keepdims=True) for c in (c0, c1, c2)]

    ib = lax.axis_index("body")
    return pick(ib), pick(ib + 1), pick(ib - 1), jnp.where(steady > STEADY, 0.0, 1.0)


def residual_coefs(c):
    return 1.0 - CENTRE * c[0], -(c[0] + CENTRE * c[1]), -(c[1] + CENTRE * c[2]), -c[2]


def middle_kernel(plan, moments_in, *refs):
    args = Args(refs)
    msgs = args.take(len(plan.sb))
    basis = args.take(4)
    diag, inside, tables = args.take(3)
    moments, = args.take(1)
    faces = args.take(len(plan.sb))
    vecs = args.take(3)
    base, above_lambda, below_lambda, doubt, shifted = args.take(5)
    ib = lax.axis_index("body")
    rows, layers = plan.rows, plan.layers
    has_above, has_below = ib < plan.nb - 1, ib > 0
    c, above_c, below_c, doubt[...] = solve(plan, moments_in)
    d = residual_coefs(c)
    near, own = plan.near, plan.own
    for vec in vecs:
        clear_frame(plan, vec)

    def combine(layer, carry):
        for first, size in chunks(PAD - 8, plan.face, 40):
            for t in (0, 1):
                span = pl.ds(first, size)
                vecs[0][t, layer + 1, span, :] = sum(x * v[t, layer + 1, span, :] for x, v in zip(d, basis))
        base[layer] = sum(x * v[0, layer + 1, own, :] for x, v in zip(c, basis))
        return carry

    lax.fori_loop(0, layers, combine, 0)

    zero = jnp.zeros((8, LANES), F32)
    slave = get_face(plan, msgs, above_c, True)
    wide = pl.ds(PAD - 16, plan.face + 16)
    top = [sum(x * v[t, layers, wide, :] for x, v in zip(c, basis)) for t in (0, 1)]
    put_shifted(shifted, 0, PAD - 16, plan.face + 16, top)
    for t in (0, 1):
        for i in range(SPAN):
            shifted[1, i, t, pl.ds(PAD - 16, 8), :] = zero
            shifted[1, i, t, pl.ds(PAD + rows + 8, 8), :] = zero
    put_shifted(shifted, 1, PAD - 8, plan.face, get_face(plan, msgs, below_c, False))
    for t in (0, 1):
        above_lambda[t, pl.ds(PAD - 16, 8), :] = zero
        above_lambda[t, pl.ds(PAD + rows + 8, 8), :] = zero
        for first, size in chunks(PAD - 8, plan.face, 40):
            span = pl.ds(first, size)
            low = first - PAD + 8
            pulled, master = pull(tables, shifted, 2, t, first, size)
            above_lambda[t, span, :] = jnp.where(has_above, RATE * (slave[t][low : low + size] - pulled), 0.0)
            gap = sum(x * basis[k][t, 1, span, :] for k, x in enumerate(c)) - master
            gap = jnp.where(has_below, RATE * gap, 0.0)
            if t == 0:
                below_lambda[span, :] = gap
            vecs[0][t, 1, span, :] = vecs[0][t, 1, span, :] - gap
    for first, size in chunks(PAD - 8, plan.face, 40):
        span = pl.ds(first, size)
        for t, value in enumerate(push(tables, above_lambda, first, size)):
            vecs[0][t, layers, span, :] = vecs[0][t, layers, span, :] + value * inside[t, span, :]

    for step in range(2):
        apply_all(plan, vecs[step], vecs[step + 1], diag, inside, near_rows(plan))

    def one(layer, sums):
        last = apply_own(plan, vecs[2], layer + 1, diag, layer, inside)
        return add_products(sums, [v[0, layer + 1, own, :] for v in vecs] + [last])

    put_moments(moments, lax.fori_loop(0, layers, one, no_sums(), unroll=UNROLL))

    put_faces(plan, lambda k, t: vecs[k][t, layers, near, :], lambda k, t: vecs[k][t, 1, near, :], faces)


def final_kernel(plan, moments_in, *refs):
    args = Args(refs)
    msgs = args.take(len(plan.sb))
    vecs = args.take(3)
    base, above_lambda, below_lambda, doubt, tables = args.take(5)
    solution_out, interface_out, again, solution, interface, lifted, shifted, sems = args.take(8)
    ib = lax.axis_index("body")
    rows, layers = plan.rows, plan.layers
    has_above, has_below = ib < plan.nb - 1, ib > 0
    inner = pl.ds(1, layers - 2)
    copies = [pltpu.make_async_copy(interface.at[inner], interface_out.at[inner], sems.at[0])]
    for layer in range(1, layers - 1):
        interface[layer] = jnp.zeros((rows, LANES), F32)
    copies[0].start()
    c, above_c, below_c, doubt_now = solve(plan, moments_in)
    again[0, 0] = jnp.where(jnp.max(jnp.maximum(doubt[...], doubt_now)) > 0.5, 1, 0)
    near, own = plan.near, plan.own
    half = layers // 2
    for i, (low, high) in enumerate(((0, half), (half, layers))):

        def combine(layer, carry):
            solution[layer] = base[layer] + sum(x * v[0, layer + 1, own, :] for x, v in zip(c, vecs))
            return carry

        lax.fori_loop(low, high, combine, 0, unroll=UNROLL)
        part = pl.ds(low, high - low)
        copies.append(pltpu.make_async_copy(solution.at[part], solution_out.at[part], sems.at[1 + i]))
        copies[-1].start()

    zero = jnp.zeros((8, LANES), F32)
    for n in (0, 1):
        for t in (0, 1):
            for i in range(SPAN):
                shifted[n, i, t, pl.ds(PAD - 16, 8), :] = zero
                shifted[n, i, t, pl.ds(PAD + rows + 8, 8), :] = zero
    put_shifted(shifted, 0, PAD - 8, plan.face, get_face(plan, msgs, below_c, False))
    top = [sum(x * v[t, layers, near, :] for x, v in zip(c, vecs)) for t in (0, 1)]
    put_shifted(shifted, 1, PAD - 8, plan.face, top)
    master = pull(tables, shifted, 1, 0, PAD, rows)[0]
    gap = sum(x * v[0, 1, own, :] for x, v in zip(c, vecs)) - master
    interface[0] = -(2.0 * below_lambda[own, :] + jnp.where(has_below, RATE * gap, 0.0))
    copies.append(pltpu.make_async_copy(interface.at[0], interface_out.at[0], sems.at[3]))
    copies[-1].start()
    slave = get_face(plan, msgs, above_c, True)
    for t in (0, 1):
        lifted[t, pl.ds(PAD - 16, 8), :] = zero
        lifted[t, pl.ds(PAD + rows + 8, 8), :] = zero
        for first, size in chunks(PAD - 8, plan.face, 40):
            span = pl.ds(first, size)
            gap = slave[t][first - PAD + 8 : first - PAD + 8 + size] - pull(tables, shifted.at[pl.ds(1, 1)], 1, t, first, size)[0]
            lifted[t, span, :] = 2.0 * above_lambda[t, span, :] + jnp.where(has_above, RATE * gap, 0.0)
    interface[layers - 1] = push(tables, lifted, PAD, rows, (0,))[0]
    copies.append(pltpu.make_async_copy(interface.at[layers - 1], interface_out.at[layers - 1], sems.at[4]))
    copies[-1].start()
    for copy in copies:
        copy.wait()


def with_halo(cells, sides, width):
    for axis, dim in sides:
        count = lax.axis_size(axis)
        head = lax.slice_in_dim(cells, 0, width, axis=dim)
        tail = lax.slice_in_dim(cells, cells.shape[dim] - width, cells.shape[dim], axis=dim)
        left = lax.ppermute(tail, axis, [(i, i + 1) for i in range(count - 1)])
        right = lax.ppermute(head, axis, [(i + 1, i) for i in range(count - 1)])
        cells = jnp.concatenate([left, cells, right], axis=dim)
    return cells


def passed_along(array, axis, by):
    count = lax.axis_size(axis)
    return lax.ppermute(array, axis, [(i, i + by) for i in range(count) if 0 <= i + by < count])


def copy_refs(flag, *refs):
    del flag
    half = len(refs) // 2
    for src, dst in zip(refs[:half], refs[half:]):
        dst[...] = src[...]


def step_by_step(load, stiffness, pair_code, pair_weight):
    layers, rows, cols = load.shape
    position = lax.axis_index("body")
    has_above = position < lax.axis_size("body") - 1
    layer_index = lax.broadcasted_iota(jnp.int32, load.shape, 0)
    lateral = (("gx", 0), ("gy", 1))

    def apply_a(vector):
        padded = with_halo(vector, (("gx", 1), ("gy", 2)), 1)
        stacked = jnp.pad(vector, ((1, 1), (0, 0), (0, 0)))
        beside_it = stacked[2:] + stacked[:-2] + padded[:, 2:, 1:-1] + padded[:, :-2, 1:-1]
        beside_it = beside_it + padded[:, 1:-1, 2:] + padded[:, 1:-1, :-2]
        return (6.0 + stiffness) * vector - beside_it

    def body_sum(first, second):
        return lax.psum(jnp.sum(first * second), G)

    offsets = jnp.arange(SPAN * SPAN, dtype=jnp.int32)[:, None, None, None]
    tables = jnp.sum(jnp.where(pair_code[None] == offsets, pair_weight[None], 0.0), axis=1)
    tables_grown = with_halo(tables, (("gx", 1), ("gy", 2)), REACH)

    def update(_, state):
        solution, multiplier, interface_load = state
        residual = load + interface_load - apply_a(solution)

        def inner(_, state):
            solution, residual, direction, norm = state
            image = apply_a(direction)
            alpha = norm / body_sum(direction, image)
            solution = solution + alpha * direction
            residual = residual - alpha * image
            new = body_sum(residual, residual)
            return solution, residual, residual + (new / norm) * direction, new

        start = (solution, residual, residual, body_sum(residual, residual))
        solution = lax.fori_loop(0, ORDER, inner, start)[0]
        master = with_halo(solution[layers - 1], lateral, REACH)
        slave = passed_along(solution[0], "body", -1)

        def pull_one(offset, total):
            window = lax.dynamic_slice(master, (offset // SPAN, offset % SPAN), (rows, cols))
            return total + tables[offset] * window

        pulled = lax.fori_loop(0, SPAN * SPAN, pull_one, jnp.zeros((rows, cols), F32))
        multiplier = jnp.where(has_above, multiplier + RATE * (slave - pulled), 0.0)
        grown = with_halo(multiplier, lateral, REACH)

        def push_one(offset, total):
            at = (2 * REACH - offset // SPAN, 2 * REACH - offset % SPAN)
            return total + lax.dynamic_slice(tables_grown[offset] * grown, at, (rows, cols))

        force = lax.fori_loop(0, SPAN * SPAN, push_one, jnp.zeros((rows, cols), F32))
        lifted = passed_along(multiplier, "body", 1)
        interface_load = jnp.where(layer_index == layers - 1, force[None], 0.0)
        interface_load = interface_load + jnp.where(layer_index == 0, -lifted[None], 0.0)
        return solution, multiplier, interface_load

    state = (jnp.zeros_like(load), jnp.zeros((rows, cols), F32), jnp.zeros_like(load))
    solution, _, interface_load = lax.fori_loop(0, UPDATES, update, state)
    return solution, interface_load


def shaped(*shape):
    return jax.ShapeDtypeStruct(shape, F32)


def held(*shape, dtype=F32):
    return pltpu.VMEM(shape, dtype)


def kept(*shape):
    return pltpu.HBM(shape, F32)


def call(kernel, args, outs, name, scratch=(), aliases=None, hbm_args=()):
    vmem = pl.BlockSpec(memory_space=pltpu.VMEM)
    hbm = pl.BlockSpec(memory_space=pltpu.HBM)
    smem = pl.BlockSpec(memory_space=pltpu.SMEM)
    in_hbm = lambda out: getattr(out, "memory_space", None) == pltpu.HBM
    return pl.pallas_call(
        kernel,
        out_shape=tuple(outs),
        in_specs=[vmem] * len(args) + [hbm] * len(hbm_args),
        out_specs=tuple(hbm if in_hbm(out) else (smem if out.dtype == jnp.int32 and out.shape == (1, 1) else vmem) for out in outs),
        scratch_shapes=list(scratch),
        input_output_aliases=aliases or {},
        compiler_params=pltpu.CompilerParams(vmem_limit_bytes=8 * 1024 * 1024),
        name=name,
    )(*args, *[pltpu.with_memory_space_constraint(x, pltpu.HBM) for x in hbm_args])


def per_device(mesh, load, stiffness, pair_code, pair_weight):
    layers, rows, lanes = load.shape
    pairs = pair_code.shape[0]
    assert lanes == LANES and rows % 8 == 0 and rows >= 16 * ORDER + 8 and layers % 4 == 0
    plan = Plan(mesh, layers, rows, pairs)
    nb, nx, ny = plan.nb, plan.nx, plan.ny
    count = nb * nx * ny
    nf = len(plan.sb)
    buf = plan.buf
    bind = lambda kernel: functools.partial(kernel, plan)
    sems = lambda n: pltpu.SemaphoreType.DMA((n,))

    def lateral(row_kind, lane_kind, array):
        a, b = swap_perm(row_kind, nx), swap_perm(lane_kind, ny)
        aside = nb > 1 and nb % 2 == 0
        pairs = []
        for body in range(nb):
            for i, j in itertools.product(range(nx), range(ny)):
                wraps = abs(a[i][1] - i) > 1 or abs(b[j][1] - j) > 1
                here, there = (body, i, j), (body, a[i][1], b[j][1])
                if wraps and aside:
                    there = (body ^ 1, i, j)
                pairs.append(tuple((p * nx + q) * ny + r for p, q, r in (here, there)))
        return lax.ppermute(array, ALL, pairs)

    def across(kind, array):
        side = nx * ny
        pairs = []
        for b, to in swap_perm(kind, nb):
            for i in range(side):
                pairs.append((b * side + i, to * side + i) if abs(to - b) == 1 else (b * side + i, b * side + (i ^ 1)))
        return lax.ppermute(array, ALL, pairs)

    def spread(moments, faces):
        return lax.all_to_all(moments, ALL, 0, 0, tiled=True), [across(k, f) for k, f in zip(plan.sb, faces)]

    kinds = [(k, "") for k in plan.sx] + [("", k) for k in plan.sy] + [(a, b) for a in plan.sx for b in plan.sy]
    vec, stack = held(*plan.vec), held(2, layers, buf, LANES)
    face = shaped(ORDER + 1, plan.face, LANES)
    message = shaped(count, 1, LANES)
    mask = held(2, buf, LANES)
    pairing, tables = held(2, pairs, 2, buf, LANES), held(SPAN * SPAN, 2, buf, LANES)
    cells = (layers, rows, LANES)
    shifted = pltpu.VMEM((2, SPAN, 2, buf, LANES), F32)

    shapes = [shaped(len(plan.units), 8, LANES) for _ in plan.sx]
    shapes += [shaped(plan.strip_tiles, rows, LANES) for _ in plan.sy]
    shapes += [shaped(plan.unit_tiles, 8, LANES) for _ in plan.sx for _ in plan.sy]
    b0, diag, codes, weights, *packed = call(
        bind(pack_kernel),
        (),
        [vec, stack, held(pairs, rows, LANES, dtype=jnp.int32), held(pairs, rows, LANES)] + shapes,
        "pack",
        [sems(4)],
        hbm_args=(load, stiffness, pair_code, pair_weight),
    )
    halos = [lateral(a, b, m) for (a, b), m in zip(kinds, packed)]
    b0, diag, pair, inside, table, b1, b2 = call(
        bind(prepare_kernel),
        (b0, diag, codes, weights),
        [vec, stack, pairing, mask, tables, vec, vec],
        "prepare",
        aliases={0: 0, 1: 1},
    )
    nx_msgs, ny_msgs = len(plan.sx), len(plan.sy)
    row_halos, lane_halos, corner_halos = halos[:nx_msgs], halos[nx_msgs : nx_msgs + ny_msgs], halos[nx_msgs + ny_msgs :]
    b0, diag, pair, b1, b2, table, b3 = call(
        bind(inner_kernel),
        (*lane_halos, inside, b0, diag, pair, b1, b2, table),
        [vec, stack, pairing, vec, vec, tables, vec],
        "inner",
        aliases={ny_msgs + 1 + i: i for i in range(6)},
    )
    at = len(row_halos) + len(corner_halos) + 1
    moments, *rest = call(
        bind(krylov_kernel),
        (*row_halos, *corner_halos, inside, b0, diag, pair, b1, b2, table, b3),
        [message] + [face] * nf + [vec, stack, pairing, vec, vec, tables, vec],
        "krylov",
        aliases={at + i: 1 + nf + i for i in range(7)},
    )
    faces, (b0, diag, _, b1, b2, table, b3) = rest[:nf], rest[nf:]
    moments, faces = spread(moments, faces)
    moments, *rest = call(
        bind(middle_kernel),
        (moments, *faces, b0, b1, b2, b3, diag, inside, table),
        [message] + [face] * nf + [vec] * 3 + [held(*cells), mask, held(buf, LANES), held(nb, LANES)],
        "middle",
        [shifted],
    )
    faces, kept_arrays = rest[:nf], rest[nf:]
    moments, faces = spread(moments, faces)
    found, lifted, again = call(
        bind(final_kernel),
        (moments, *faces, *kept_arrays, table),
        [kept(*cells)] * 2 + [jax.ShapeDtypeStruct((1, 1), jnp.int32)],
        "final",
        [pltpu.VMEM(cells, F32), pltpu.VMEM(cells, F32), pltpu.VMEM((2, buf, LANES), F32), shifted, sems(5)],
    )

    def same(arrays, flag):
        vmem = pl.BlockSpec(memory_space=pltpu.VMEM)
        return pl.pallas_call(
copy_refs,
            out_shape=[jax.ShapeDtypeStruct(a.shape, a.dtype) for a in arrays],
            in_specs=[pl.BlockSpec(memory_space=pltpu.SMEM)] + [vmem] * len(arrays),
            out_specs=[vmem] * len(arrays),
            name="same",
        )(flag, *arrays)

    def redo(state):
        inputs = same((load, stiffness, pair_code, pair_weight), state[2])
        return (*same(step_by_step(*inputs), state[2]), jnp.zeros_like(state[2]))

    found, lifted, _ = lax.while_loop(lambda state: state[2][0, 0] > 0, redo, (found, lifted, again))
    return found, lifted


def solution(mesh):
    return jax.shard_map(
        functools.partial(per_device, mesh),
        mesh=mesh,
        in_specs=(P("body", "gx", "gy"), P("body", "gx", "gy"), P(None, "gx", "gy"), P(None, "gx", "gy")),
        out_specs=(P("body", "gx", "gy"), P("body", "gx", "gy")),
        check_vma=False,
    )
```

```python
import functools
import itertools

import jax
import jax.numpy as jnp
from jax import lax
from jax.experimental import pallas as pl
from jax.experimental.pallas import tpu as pltpu
from jax.sharding import PartitionSpec as P


REACH = 2
SPAN = 2 * REACH + 1
RATE = 2.0
CENTRE = 7.5
LANES = 128
STRIP = 16
SLOTS = LANES // STRIP
PAD = 24
ORDER = 3
UNROLL = 4
UPDATES = 2
STEADY = 0.05
F32 = jnp.float32
G = ("gx", "gy")
ALL = ("body", "gx", "gy")


def swaps_of(count):
    return () if count < 2 else (("A",) if count == 2 else ("A", "B"))


def swap_perm(kind, count):
    if kind == "":
        return [(i, i) for i in range(count)]
    step = 1 if kind == "A" else -1
    return [(i, (i + (step if i % 2 == 0 else -step)) % count) for i in range(count)]


def swap_up(kind, index):
    even = lax.rem(index, 2) == 0
    return even if kind == "A" else jnp.logical_not(even)


def swap_valid(kind, index, count):
    if kind == "A":
        return index >= 0
    return jnp.where(swap_up(kind, index), index < count - 1, index > 0)


def row_units(layers, pairs):
    wide_load = (0, 1, layers - 3, layers - 2, layers - 1)
    wide_stiff = (0, layers - 3, layers - 2, layers - 1)
    units = []
    for which, wide in ((0, wide_load), (1, wide_stiff)):
        for layer in range(layers):
            units.append((which, layer, False))
            if layer in wide:
                units.append((which, layer, True))
    for which in (2, 3):
        units += [(which, k, False) for k in range(pairs)]
    return units


def row_pieces(layers, pairs):
    top = layers - 1
    load = {top: 12, top - 1: 11, top - 2: 10, 0: 10, 1: 9, 2: 8}
    stiff = {top: 11, top - 1: 10, top - 2: 6, 0: 9, 1: 8}
    pieces = [(0, k, load.get(k, 6)) for k in range(layers)] + [(1, k, stiff.get(k, 5)) for k in range(layers)]
    pieces += [(which, k, 8) for which in (2, 3) for k in range(pairs)]
    placed, at = [], 0
    for which, k, size in pieces:
        placed.append((which, k, size, at))
        at += size
    return placed


def strip_list(layers, pairs):
    return [(w, k) for w in (0, 1) for k in range(layers)] + [(w, k) for w in (2, 3) for k in range(pairs)]


def lane_iota(rows):
    return lax.broadcasted_iota(jnp.int32, (rows, LANES), 1)


def aligned(start):
    return pl.multiple_of(start, 8)


def chunks(first, size, step):
    return [(at, min(step, first + size - at)) for at in range(first, first + size, step)]


class Plan:
    def __init__(self, mesh, layers, rows, pairs):
        self.nb, self.nx, self.ny = (mesh.shape[a] for a in ALL)
        self.layers, self.rows, self.pairs = layers, rows, pairs
        self.buf = rows + 2 * PAD
        self.units = row_units(layers, pairs)
        self.strips = strip_list(layers, pairs)
        self.pieces = row_pieces(layers, pairs)
        self.piece_rows = -(-(self.pieces[-1][2] + self.pieces[-1][3]) // 8) * 8
        self.sx, self.sy, self.sb = swaps_of(self.nx), swaps_of(self.ny), swaps_of(self.nb)
        self.face = rows + 16
        self.vec = (2, layers + 2, self.buf, LANES)
        self.own = pl.ds(PAD, rows)
        self.near = pl.ds(PAD - 8, self.face)
        self.unit_tiles = -(-len(self.units) // SLOTS)
        self.strip_tiles = -(-len(self.strips) // SLOTS)


class Args:
    def __init__(self, refs):
        self.refs = list(refs)

    def take(self, count):
        got, self.refs = self.refs[:count], self.refs[count:]
        return got

    def one(self):
        return self.refs.pop(0)


def pack_kernel(plan, load, stiff, code, weight, *refs):
    args = Args(refs)
    b0, diag, codes, weights = args.take(4)
    row_out, lane_out = args.take(len(plan.sx)), args.take(len(plan.sy))
    corner_out = args.take(len(plan.sx) * len(plan.sy))
    sems = args.one()
    ix, iy = lax.axis_index("gx"), lax.axis_index("gy")
    rows, layers = plan.rows, plan.layers
    places = (b0.at[0, pl.ds(1, layers), plan.own, :], diag.at[0, :, plan.own, :], codes, weights)
    copies = [
        pltpu.make_async_copy(src, dst, sems.at[i]) for i, (src, dst) in enumerate(zip((load, stiff, code, weight), places))
    ]
    for copy in copies:
        copy.start()
    arrived = set()

    def take(which, k, start, size):
        if which not in arrived:
            copies[which].wait()
            arrived.add(which)
        if which == 0:
            return b0[0, k + 1, pl.ds(PAD + start, size), :]
        if which == 1:
            return diag[0, k, pl.ds(PAD + start, size), :]
        return (codes, weights)[which - 2][k, pl.ds(start, size), :].astype(F32)

    def starts(kind):
        up = swap_up(kind, ix)
        return aligned(jnp.where(up, rows - 8, 0)), aligned(jnp.where(up, rows - 16, 8))

    def gather(pieces, size, tile, outs):
        slot_of = lane_iota(size) // STRIP
        last, first = jnp.zeros((size, LANES), F32), jnp.zeros((size, LANES), F32)
        for slot, value in enumerate(pieces):
            moved = pltpu.roll(value, STRIP * (slot + 1) % LANES, 1) if slot + 1 < SLOTS else value
            last = jnp.where(slot_of == slot, moved, last)
            first = jnp.where(slot_of == (slot + 1) % SLOTS, moved, first)
        for kind, out in zip(plan.sy, outs):
            out[tile] = jnp.where(swap_up(kind, iy), last, first)

    for kind, out in zip(plan.sx, row_out):
        up = swap_up(kind, ix)
        for which, k, size, at in plan.pieces:
            out[pl.ds(at, size), :] = jnp.where(up, take(which, k, rows - size, size), take(which, k, 0, size))
        used = plan.pieces[-1][2] + plan.pieces[-1][3]
        if used < plan.piece_rows:
            out[pl.ds(used, plan.piece_rows - used), :] = jnp.zeros((plan.piece_rows - used, LANES), F32)
    for tile in range(plan.strip_tiles):
        members = plan.strips[tile * SLOTS : (tile + 1) * SLOTS]
        gather([take(which, k, 0, rows) for which, k in members], rows, tile, lane_out)
    for i, row_kind in enumerate(plan.sx):
        near, far = starts(row_kind)
        outs = corner_out[i * len(plan.sy) : (i + 1) * len(plan.sy)]
        for tile in range(plan.unit_tiles):
            members = plan.units[tile * SLOTS : (tile + 1) * SLOTS]
            gather([take(which, k, far if is_far else near, 8) for which, k, is_far in members], 8, tile, outs)


def clear_frame(plan, vec):
    zero = jnp.zeros((16, LANES), F32)
    for t in (0, 1):
        for edge in (0, plan.layers + 1):
            vec[t, edge] = jnp.zeros((plan.buf, LANES), F32)
        for layer in range(1, plan.layers + 1):
            vec[t, layer, pl.ds(0, 16), :] = zero
            vec[t, layer, pl.ds(plan.buf - 16, 16), :] = zero


def table_rows(plan, pairing, tables, t, first, size):
    span = pl.ds(first, size)
    codes = [pairing[0, k, t, span, :] for k in range(plan.pairs)]
    weights = [pairing[1, k, t, span, :] for k in range(plan.pairs)]
    for offset in range(SPAN * SPAN):
        total = jnp.where(codes[0] == offset, weights[0], 0.0)
        for k in range(1, plan.pairs):
            total = total + jnp.where(codes[k] == offset, weights[k], 0.0)
        tables[offset, t, span, :] = total


def prepare_kernel(plan, b0_in, diag_in, codes, weights, b0, diag, pairing, inside, tables, *vecs):
    del b0_in, diag_in
    ix, iy = lax.axis_index("gx"), lax.axis_index("gy")
    rows, layers, buf = plan.rows, plan.layers, plan.buf
    row = lax.broadcasted_iota(jnp.int32, (buf, LANES), 0) + ix * rows - PAD
    lane = lane_iota(buf)
    in_rows = jnp.logical_and(row >= 0, row < plan.nx * rows)
    right = jnp.logical_and(lane < STRIP, iy < plan.ny - 1)
    left = jnp.logical_and(lane >= LANES - STRIP, iy > 0)
    inside[0] = jnp.where(in_rows, 1.0, 0.0)
    inside[1] = jnp.where(jnp.logical_and(in_rows, jnp.logical_or(right, left)), 1.0, 0.0)
    zero = jnp.zeros((PAD, LANES), F32)
    for t in (0, 1):
        for span in (pl.ds(0, PAD), pl.ds(buf - PAD, PAD)):
            for layer in range(layers):
                b0[t, layer + 1, span, :] = zero
                diag[t, layer, span, :] = zero
            for k in range(plan.pairs):
                for i in (0, 1):
                    pairing[i, k, t, span, :] = zero
        for edge in (0, layers + 1):
            b0[t, edge] = jnp.zeros((buf, LANES), F32)
        for offset in range(SPAN * SPAN):
            tables[offset, t, pl.ds(PAD - 16, 8), :] = jnp.zeros((8, LANES), F32)
            tables[offset, t, pl.ds(PAD + rows + 8, 8), :] = jnp.zeros((8, LANES), F32)
    for vec in vecs:
        clear_frame(plan, vec)
    for layer in range(layers):
        diag[0, layer, plan.own, :] = diag[0, layer, plan.own, :] + (6.0 - CENTRE)
    for k in range(plan.pairs):
        pairing[0, k, 0, plan.own, :] = codes[k].astype(F32)
        pairing[1, k, 0, plan.own, :] = weights[k]
    for first, size in chunks(PAD, rows, 32):
        table_rows(plan, pairing, tables, 0, first, size)


def operate(src, at, diag, layer, inside, first, size, tiles=(0, 1), masked=True):
    lane = lane_iota(size)
    start, end = lane == 0, lane == LANES - 1
    rows = pl.ds(first, size)
    middle = [src[t, at, rows, :] for t in (0, 1)]
    before = [pltpu.roll(m, 1, 1) for m in middle]
    after = [pltpu.roll(m, LANES - 1, 1) for m in middle]
    done = []
    for t in tiles:
        total = jnp.where(start, before[1 - t], before[t]) + jnp.where(end, after[1 - t], after[t])
        total = total + src[t, at, pl.ds(first - 1, size), :]
        total = total + src[t, at, pl.ds(first + 1, size), :]
        total = total + (src[t, at - 1, rows, :] + src[t, at + 1, rows, :])
        if masked or t == 1:
            total = total * inside[t, rows, :]
        done.append(diag[t, layer, rows, :] * middle[t] - total)
    return done


def apply_rows(src, dst, at, diag, layer, inside, parts):
    values = [operate(src, at, diag, layer, inside, first, size, masked=masked) for first, size, masked in parts]
    for (first, size, _), pair in zip(parts, values):
        for t in (0, 1):
            dst[t, at, pl.ds(first, size), :] = pair[t]
    return [pair[0] for pair in values]


def apply_joined(src, dst, at, diag, layer, inside, parts):
    spans = [pl.ds(first, size) for first, size, _ in parts]
    size = sum(p[1] for p in parts)
    lane = lane_iota(size)
    start, end = lane == 0, lane == LANES - 1
    join = lambda values: values[0] if len(values) == 1 else jnp.concatenate(values, axis=0)
    middle = [join([src[t, at, span, :] for span in spans]) for t in (0, 1)]
    before = [pltpu.roll(m, 1, 1) for m in middle]
    after = [pltpu.roll(m, LANES - 1, 1) for m in middle]
    done = []
    for t in (0, 1):
        sides = jnp.where(start, before[1 - t], before[t]) + jnp.where(end, after[1 - t], after[t])
        values, low = [], 0
        for (first, rows, masked), span in zip(parts, spans):
            total = sides[low : low + rows]
            total = total + src[t, at, pl.ds(first - 1, rows), :]
            total = total + src[t, at, pl.ds(first + 1, rows), :]
            total = total + (src[t, at - 1, span, :] + src[t, at + 1, span, :])
            if masked or t == 1:
                total = total * inside[t, span, :]
            values.append(diag[t, layer, span, :] * middle[t][low : low + rows] - total)
            low += rows
        done.append(values)
    for i, span in enumerate(spans):
        for t in (0, 1):
            dst[t, at, span, :] = done[t][i]
    return done[0]


def near_rows(plan):
    outer = [(PAD - 8, 8, True), (PAD + plan.rows, 8, True)]
    return outer + [(first, size, False) for first, size in chunks(PAD, plan.rows, 32)]


def inner_rows(plan, step):
    return [(first, size, False) for first, size in chunks(PAD + 8 * step, plan.rows - 16 * step, 32)]


def outer_rows(plan, step):
    wide = 8 * step
    outer = [(PAD - 8, 8, True), (PAD + plan.rows, 8, True)]
    return outer + [(PAD, wide, False), (PAD + plan.rows - wide, wide, False)]


def apply_all(plan, src, dst, diag, inside, parts, apply=apply_rows):
    def one(layer, carry):
        apply(src, dst, layer + 1, diag, layer, inside, parts)
        return carry

    lax.fori_loop(0, plan.layers, one, 0, unroll=UNROLL)


def apply_own(plan, src, at, diag, layer, inside):
    parts = [
        operate(src, at, diag, layer, inside, first, size, (0,), False)[0] for first, size in chunks(PAD, plan.rows, 32)
    ]
    return jnp.concatenate(parts, axis=0)


def six_sums(parts):
    lane = lax.broadcasted_iota(jnp.int32, (1, LANES), 1)
    row = jnp.zeros((1, LANES), F32)
    for k, part in enumerate(parts):
        row = jnp.where(lane == k, jnp.sum(part), row)
    return row


def fold(value):
    return jnp.sum(value.reshape(-1, 8, LANES), axis=0)


def add_products(sums, v):
    pairs = ((v[0], v[0]), (v[0], v[1]), (v[1], v[1]), (v[1], v[2]), (v[2], v[2]), (v[2], v[3]))
    return tuple(s + fold(a * b) for s, (a, b) in zip(sums, pairs))


def put_moments(moments, sums):
    moments[...] = jnp.broadcast_to(six_sums(sums).reshape(1, 1, LANES), moments.shape)


def no_sums():
    return (jnp.zeros((8, LANES), F32),) * 6


def put_cells(arrays, which, k, t, where, value):
    b0, diag, pairing = arrays
    if which == 0:
        b0[t, k + 1, where, :] = value
    elif which == 1:
        diag[t, k, where, :] = value + (6.0 - CENTRE)
    else:
        pairing[which - 2, k, t, where, :] = value


def unpack(plan, msgs, tile, size):
    iy = lax.axis_index("gy")
    sides = []
    for right in (True, False):
        total = jnp.zeros((size, LANES), F32)
        for kind, msg in zip(plan.sy, msgs):
            use = jnp.logical_and(swap_up(kind, iy) == right, swap_valid(kind, iy, plan.ny))
            total = jnp.where(use, msg[tile], total)
        sides.append(total)
    even = lax.rem(lane_iota(size) // STRIP, 2) == 0
    return jnp.where(even, sides[1], sides[0]), jnp.where(even, sides[0], sides[1])


def piece(both, slot):
    turn = STRIP * (SLOTS - 1 - slot)
    return pltpu.roll(both[slot % 2], turn, 1) if turn else both[slot % 2]


def inner_kernel(plan, *refs):
    args = Args(refs)
    msgs = args.take(len(plan.sy))
    inside, _, _, _, _, _, _ = args.take(7)
    b0, diag, pairing, b1, b2, tables, b3 = args.take(7)
    for tile in range(plan.strip_tiles):
        both = unpack(plan, msgs, tile, plan.rows)
        for slot, (which, k) in enumerate(plan.strips[tile * SLOTS : (tile + 1) * SLOTS]):
            put_cells((b0, diag, pairing), which, k, 1, plan.own, piece(both, slot))
    for step, (src, dst) in enumerate(((b0, b1), (b1, b2), (b2, b3))):
        apply_all(plan, src, dst, diag, inside, inner_rows(plan, step + 1))
    for first, size in chunks(PAD, plan.rows, 32):
        table_rows(plan, pairing, tables, 1, first, size)


def krylov_kernel(plan, *refs):
    args = Args(refs)
    row_msgs = args.take(len(plan.sx))
    corner_msgs = args.take(len(plan.sx) * len(plan.sy))
    inside = args.one()
    args.take(7)
    moments, = args.take(1)
    faces = args.take(len(plan.sb))
    b0, diag, pairing, b1, b2, tables, b3 = args.take(7)
    ix = lax.axis_index("gx")
    rows, layers = plan.rows, plan.layers
    arrays = (b0, diag, pairing)

    def spots(kind):
        up = swap_up(kind, ix)
        near = aligned(jnp.where(up, PAD + rows, PAD - 8))
        far = aligned(jnp.where(up, PAD + rows + 8, PAD - 16))
        return near, far, swap_valid(kind, ix, plan.nx)

    for kind, msg in zip(plan.sx, row_msgs):
        up, ok = swap_up(kind, ix), swap_valid(kind, ix, plan.nx)

        @pl.when(jnp.logical_and(up, ok))
        def _():
            for which, k, size, at in plan.pieces:
                put_cells(arrays, which, k, 0, pl.ds(PAD + rows, size), msg[pl.ds(at, size), :])

        @pl.when(jnp.logical_and(jnp.logical_not(up), ok))
        def _():
            for which, k, size, at in plan.pieces:
                put_cells(arrays, which, k, 0, pl.ds(PAD - size, size), msg[pl.ds(at, size), :])

    for i, row_kind in enumerate(plan.sx):
        near, far, ok = spots(row_kind)
        for tile in range(plan.unit_tiles):
            both = unpack(plan, corner_msgs[i * len(plan.sy) : (i + 1) * len(plan.sy)], tile, 8)
            both = [jnp.where(ok, b, 0.0) for b in both]
            for slot, (which, k, is_far) in enumerate(plan.units[tile * SLOTS : (tile + 1) * SLOTS]):
                put_cells(arrays, which, k, 1, pl.ds(far if is_far else near, 8), piece(both, slot))

    for step, (src, dst, wide) in enumerate(((b0, b1, (0, layers - 2, layers - 1)), (b1, b2, (layers - 1,)))):
        apply_all(plan, src, dst, diag, inside, outer_rows(plan, step + 1), apply_joined)
        for layer in wide:
            for first in (PAD - 16, PAD + rows + 8):
                for t, value in enumerate(operate(src, layer + 1, diag, layer, inside, first, 8)):
                    dst[t, layer + 1, pl.ds(first, 8), :] = value

    middle = pl.ds(PAD + 8 * ORDER, rows - 16 * ORDER)

    def one(layer, sums):
        ends = apply_joined(b2, b3, layer + 1, diag, layer, inside, outer_rows(plan, ORDER))[2:]
        last = jnp.concatenate([ends[0], b3[0, layer + 1, middle, :], ends[1]], axis=0)
        return add_products(sums, [v[0, layer + 1, plan.own, :] for v in (b0, b1, b2)] + [last])

    put_moments(moments, lax.fori_loop(0, layers, one, no_sums(), unroll=UNROLL))

    for t in (0, 1):
        for first in (PAD - 8, PAD + rows):
            table_rows(plan, pairing, tables, t, first, 8)
    vecs = (b0, b1, b2)
    put_faces(plan, lambda k, t: vecs[k][t, layers, plan.near, :], lambda k, t: vecs[k][t, 1, plan.near, :], faces)


def lane_shift(first, second, by, lane):
    if by == 0:
        return first, second
    a, b = pltpu.roll(first, (-by) % LANES, 1), pltpu.roll(second, (-by) % LANES, 1)
    keep = lane < LANES - by if by > 0 else lane >= -by
    return jnp.where(keep, a, b), jnp.where(keep, b, a)


def put_shifted(shifted, n, first, size, planes):
    lane = lane_iota(size)
    for i in range(SPAN):
        for t, value in enumerate(lane_shift(planes[0], planes[1], i - REACH, lane)):
            shifted[n, i, t, pl.ds(first, size), :] = value


def pull(tables, shifted, count, t, first, size):
    total = [jnp.zeros((size, LANES), F32)] * count
    for offset in range(SPAN * SPAN):
        table = tables[offset, t, pl.ds(first, size), :]
        window = pl.ds(first + offset // SPAN - REACH, size)
        for n in range(count):
            total[n] = total[n] + table * shifted[n, offset % SPAN, t, window, :]
    return total


def push(tables, face, first, size, tiles=(0, 1)):
    lane = lane_iota(size)
    total = [jnp.zeros((size, LANES), F32)] * 2
    for i in range(SPAN):
        column = [jnp.zeros((size, LANES), F32)] * 2
        for j in range(SPAN):
            window = pl.ds(first - (j - REACH), size)
            for t in (0, 1):
                column[t] = column[t] + tables[j * SPAN + i, t, window, :] * face[t, window, :]
        moved = lane_shift(column[0], column[1], REACH - i, lane)
        total = [total[t] + moved[t] for t in (0, 1)]
    return [total[t] for t in tiles]


def put_faces(plan, tops, bottoms, outs):
    ib = lax.axis_index("body")
    lane = lane_iota(plan.face)
    for kind, out in zip(plan.sb, outs):
        up = swap_up(kind, ib)
        packed = jnp.zeros((plan.face, LANES), F32)
        for k in range(ORDER):
            out[k] = jnp.where(up, tops(k, 0), bottoms(k, 0))
            strips = pltpu.roll(jnp.where(up, tops(k, 1), bottoms(k, 1)), STRIP + 2 * STRIP * k, 1)
            packed = jnp.where(lane // (2 * STRIP) == k, strips, packed)
        out[ORDER] = packed


def get_face(plan, msgs, coef, up, tiles=(0, 1)):
    ib = lax.axis_index("body")
    total = [jnp.zeros((plan.face, LANES), F32)] * 2
    for kind, msg in zip(plan.sb, msgs):
        use = jnp.logical_and(swap_up(kind, ib) == up, swap_valid(kind, ib, plan.nb))
        for t in tiles:
            if t == 0:
                value = sum(coef[k] * msg[k] for k in range(ORDER))
            else:
                value = sum(
                    coef[k] * pltpu.roll(msg[ORDER], (LANES - STRIP - 2 * STRIP * k) % LANES, 1) for k in range(ORDER)
                )
            total[t] = jnp.where(use, value, total[t])
    return [total[t] for t in tiles]


def solve(plan, moments):
    per = plan.nx * plan.ny
    body = lax.broadcasted_iota(jnp.int32, (plan.nb, LANES), 0)
    table = jnp.zeros((plan.nb, LANES), F32)
    for b in range(plan.nb):
        row = [moments[b * per + i] for i in range(per)]
        while len(row) > 1:
            row = [x + y for x, y in zip(row[::2], row[1::2])] + row[len(row) // 2 * 2 :]
        table = jnp.where(body == b, row[0], table)
    lane = lax.broadcasted_iota(jnp.int32, (plan.nb, LANES), 1)
    m = [
        jnp.broadcast_to(jnp.sum(jnp.where(lane == k, table, 0.0), axis=1, keepdims=True), table.shape)
        for k in range(6)
    ]
    h = [m[n + 1] + CENTRE * m[n] for n in range(5)]
    f1, f2 = h[1] / h[0], h[2] / h[0]
    d1 = h[2] - f1 * h[1]
    e = h[3] - f1 * h[2]
    f3 = e / d1
    d2 = h[4] - f2 * h[2] - f3 * e
    g1 = m[1] - f1 * m[0]
    g2 = m[2] - f2 * m[0] - f3 * g1
    c2 = g2 / d2
    c1 = (g1 - e * c2) / d1
    c0 = (m[0] - h[1] * c1 - h[2] * c2) / h[0]

    steady = jnp.minimum(d1 / h[2], d2 / h[4])

    def pick(index):
        return [jnp.sum(jnp.where(body == index, c, 0.0), axis=0, keepdims=True) for c in (c0, c1, c2)]

    ib = lax.axis_index("body")
    return pick(ib), pick(ib + 1), pick(ib - 1), jnp.where(steady > STEADY, 0.0, 1.0)


def residual_coefs(c):
    return 1.0 - CENTRE * c[0], -(c[0] + CENTRE * c[1]), -(c[1] + CENTRE * c[2]), -c[2]


def middle_kernel(plan, moments_in, *refs):
    args = Args(refs)
    msgs = args.take(len(plan.sb))
    basis = args.take(4)
    diag, inside, tables = args.take(3)
    moments, = args.take(1)
    faces = args.take(len(plan.sb))
    vecs = args.take(3)
    base, above_lambda, below_lambda, doubt, shifted = args.take(5)
    ib = lax.axis_index("body")
    rows, layers = plan.rows, plan.layers
    has_above, has_below = ib < plan.nb - 1, ib > 0
    c, above_c, below_c, doubt[...] = solve(plan, moments_in)
    d = residual_coefs(c)
    near, own = plan.near, plan.own
    for vec in vecs:
        clear_frame(plan, vec)

    def combine(layer, carry):
        for first, size in chunks(PAD - 8, plan.face, 40):
            for t in (0, 1):
                span = pl.ds(first, size)
                vecs[0][t, layer + 1, span, :] = sum(x * v[t, layer + 1, span, :] for x, v in zip(d, basis))
        base[layer] = sum(x * v[0, layer + 1, own, :] for x, v in zip(c, basis))
        return carry

    lax.fori_loop(0, layers, combine, 0)

    zero = jnp.zeros((8, LANES), F32)
    slave = get_face(plan, msgs, above_c, True)
    wide = pl.ds(PAD - 16, plan.face + 16)
    top = [sum(x * v[t, layers, wide, :] for x, v in zip(c, basis)) for t in (0, 1)]
    put_shifted(shifted, 0, PAD - 16, plan.face + 16, top)
    for t in (0, 1):
        for i in range(SPAN):
            shifted[1, i, t, pl.ds(PAD - 16, 8), :] = zero
            shifted[1, i, t, pl.ds(PAD + rows + 8, 8), :] = zero
    put_shifted(shifted, 1, PAD - 8, plan.face, get_face(plan, msgs, below_c, False))
    for t in (0, 1):
        above_lambda[t, pl.ds(PAD - 16, 8), :] = zero
        above_lambda[t, pl.ds(PAD + rows + 8, 8), :] = zero
        for first, size in chunks(PAD - 8, plan.face, 40):
            span = pl.ds(first, size)
            low = first - PAD + 8
            pulled, master = pull(tables, shifted, 2, t, first, size)
            above_lambda[t, span, :] = jnp.where(has_above, RATE * (slave[t][low : low + size] - pulled), 0.0)
            gap = sum(x * basis[k][t, 1, span, :] for k, x in enumerate(c)) - master
            gap = jnp.where(has_below, RATE * gap, 0.0)
            if t == 0:
                below_lambda[span, :] = gap
            vecs[0][t, 1, span, :] = vecs[0][t, 1, span, :] - gap
    for first, size in chunks(PAD - 8, plan.face, 40):
        span = pl.ds(first, size)
        for t, value in enumerate(push(tables, above_lambda, first, size)):
            vecs[0][t, layers, span, :] = vecs[0][t, layers, span, :] + value * inside[t, span, :]

    for step in range(2):
        apply_all(plan, vecs[step], vecs[step + 1], diag, inside, near_rows(plan))

    def one(layer, sums):
        last = apply_own(plan, vecs[2], layer + 1, diag, layer, inside)
        return add_products(sums, [v[0, layer + 1, own, :] for v in vecs] + [last])

    put_moments(moments, lax.fori_loop(0, layers, one, no_sums(), unroll=UNROLL))

    put_faces(plan, lambda k, t: vecs[k][t, layers, near, :], lambda k, t: vecs[k][t, 1, near, :], faces)


def final_kernel(plan, moments_in, *refs):
    args = Args(refs)
    msgs = args.take(len(plan.sb))
    vecs = args.take(3)
    base, above_lambda, below_lambda, doubt, tables = args.take(5)
    solution_out, interface_out, again, solution, interface, lifted, shifted, sems = args.take(8)
    ib = lax.axis_index("body")
    rows, layers = plan.rows, plan.layers
    has_above, has_below = ib < plan.nb - 1, ib > 0
    inner = pl.ds(1, layers - 2)
    copies = [pltpu.make_async_copy(interface.at[inner], interface_out.at[inner], sems.at[0])]
    for layer in range(1, layers - 1):
        interface[layer] = jnp.zeros((rows, LANES), F32)
    copies[0].start()
    c, above_c, below_c, doubt_now = solve(plan, moments_in)
    again[0, 0] = jnp.where(jnp.max(jnp.maximum(doubt[...], doubt_now)) > 0.5, 1, 0)
    near, own = plan.near, plan.own
    half = layers // 2
    for i, (low, high) in enumerate(((0, half), (half, layers))):

        def combine(layer, carry):
            solution[layer] = base[layer] + sum(x * v[0, layer + 1, own, :] for x, v in zip(c, vecs))
            return carry

        lax.fori_loop(low, high, combine, 0, unroll=UNROLL)
        part = pl.ds(low, high - low)
        copies.append(pltpu.make_async_copy(solution.at[part], solution_out.at[part], sems.at[1 + i]))
        copies[-1].start()

    zero = jnp.zeros((8, LANES), F32)
    for n in (0, 1):
        for t in (0, 1):
            for i in range(SPAN):
                shifted[n, i, t, pl.ds(PAD - 16, 8), :] = zero
                shifted[n, i, t, pl.ds(PAD + rows + 8, 8), :] = zero
    put_shifted(shifted, 0, PAD - 8, plan.face, get_face(plan, msgs, below_c, False))
    top = [sum(x * v[t, layers, near, :] for x, v in zip(c, vecs)) for t in (0, 1)]
    put_shifted(shifted, 1, PAD - 8, plan.face, top)
    master = pull(tables, shifted, 1, 0, PAD, rows)[0]
    gap = sum(x * v[0, 1, own, :] for x, v in zip(c, vecs)) - master
    interface[0] = -(2.0 * below_lambda[own, :] + jnp.where(has_below, RATE * gap, 0.0))
    copies.append(pltpu.make_async_copy(interface.at[0], interface_out.at[0], sems.at[3]))
    copies[-1].start()
    slave = get_face(plan, msgs, above_c, True)
    for t in (0, 1):
        lifted[t, pl.ds(PAD - 16, 8), :] = zero
        lifted[t, pl.ds(PAD + rows + 8, 8), :] = zero
        for first, size in chunks(PAD - 8, plan.face, 40):
            span = pl.ds(first, size)
            gap = slave[t][first - PAD + 8 : first - PAD + 8 + size] - pull(tables, shifted.at[pl.ds(1, 1)], 1, t, first, size)[0]
            lifted[t, span, :] = 2.0 * above_lambda[t, span, :] + jnp.where(has_above, RATE * gap, 0.0)
    interface[layers - 1] = push(tables, lifted, PAD, rows, (0,))[0]
    copies.append(pltpu.make_async_copy(interface.at[layers - 1], interface_out.at[layers - 1], sems.at[4]))
    copies[-1].start()
    for copy in copies:
        copy.wait()


def with_halo(cells, sides, width):
    for axis, dim in sides:
        count = lax.axis_size(axis)
        head = lax.slice_in_dim(cells, 0, width, axis=dim)
        tail = lax.slice_in_dim(cells, cells.shape[dim] - width, cells.shape[dim], axis=dim)
        left = lax.ppermute(tail, axis, [(i, i + 1) for i in range(count - 1)])
        right = lax.ppermute(head, axis, [(i + 1, i) for i in range(count - 1)])
        cells = jnp.concatenate([left, cells, right], axis=dim)
    return cells


def passed_along(array, axis, by):
    count = lax.axis_size(axis)
    return lax.ppermute(array, axis, [(i, i + by) for i in range(count) if 0 <= i + by < count])


def copy_refs(flag, *refs):
    del flag
    half = len(refs) // 2
    for src, dst in zip(refs[:half], refs[half:]):
        dst[...] = src[...]


def step_by_step(load, stiffness, pair_code, pair_weight):
    layers, rows, cols = load.shape
    position = lax.axis_index("body")
    has_above = position < lax.axis_size("body") - 1
    layer_index = lax.broadcasted_iota(jnp.int32, load.shape, 0)
    lateral = (("gx", 0), ("gy", 1))

    def apply_a(vector):
        padded = with_halo(vector, (("gx", 1), ("gy", 2)), 1)
        stacked = jnp.pad(vector, ((1, 1), (0, 0), (0, 0)))
        beside_it = stacked[2:] + stacked[:-2] + padded[:, 2:, 1:-1] + padded[:, :-2, 1:-1]
        beside_it = beside_it + padded[:, 1:-1, 2:] + padded[:, 1:-1, :-2]
        return (6.0 + stiffness) * vector - beside_it

    def body_sum(first, second):
        return lax.psum(jnp.sum(first * second), G)

    offsets = jnp.arange(SPAN * SPAN, dtype=jnp.int32)[:, None, None, None]
    tables = jnp.sum(jnp.where(pair_code[None] == offsets, pair_weight[None], 0.0), axis=1)
    tables_grown = with_halo(tables, (("gx", 1), ("gy", 2)), REACH)

    def update(_, state):
        solution, multiplier, interface_load = state
        residual = load + interface_load - apply_a(solution)

        def inner(_, state):
            solution, residual, direction, norm = state
            image = apply_a(direction)
            alpha = norm / body_sum(direction, image)
            solution = solution + alpha * direction
            residual = residual - alpha * image
            new = body_sum(residual, residual)
            return solution, residual, residual + (new / norm) * direction, new

        start = (solution, residual, residual, body_sum(residual, residual))
        solution = lax.fori_loop(0, ORDER, inner, start)[0]
        master = with_halo(solution[layers - 1], lateral, REACH)
        slave = passed_along(solution[0], "body", -1)

        def pull_one(offset, total):
            window = lax.dynamic_slice(master, (offset // SPAN, offset % SPAN), (rows, cols))
            return total + tables[offset] * window

        pulled = lax.fori_loop(0, SPAN * SPAN, pull_one, jnp.zeros((rows, cols), F32))
        multiplier = jnp.where(has_above, multiplier + RATE * (slave - pulled), 0.0)
        grown = with_halo(multiplier, lateral, REACH)

        def push_one(offset, total):
            at = (2 * REACH - offset // SPAN, 2 * REACH - offset % SPAN)
            return total + lax.dynamic_slice(tables_grown[offset] * grown, at, (rows, cols))

        force = lax.fori_loop(0, SPAN * SPAN, push_one, jnp.zeros((rows, cols), F32))
        lifted = passed_along(multiplier, "body", 1)
        interface_load = jnp.where(layer_index == layers - 1, force[None], 0.0)
        interface_load = interface_load + jnp.where(layer_index == 0, -lifted[None], 0.0)
        return solution, multiplier, interface_load

    state = (jnp.zeros_like(load), jnp.zeros((rows, cols), F32), jnp.zeros_like(load))
    solution, _, interface_load = lax.fori_loop(0, UPDATES, update, state)
    return solution, interface_load


def shaped(*shape):
    return jax.ShapeDtypeStruct(shape, F32)


def held(*shape, dtype=F32):
    return pltpu.VMEM(shape, dtype)


def kept(*shape):
    return pltpu.HBM(shape, F32)


def call(kernel, args, outs, scratch=(), aliases=None, hbm_args=()):
    vmem = pl.BlockSpec(memory_space=pltpu.VMEM)
    hbm = pl.BlockSpec(memory_space=pltpu.HBM)
    smem = pl.BlockSpec(memory_space=pltpu.SMEM)
    in_hbm = lambda out: getattr(out, "memory_space", None) == pltpu.HBM
    return pl.pallas_call(
        kernel,
        out_shape=tuple(outs),
        in_specs=[vmem] * len(args) + [hbm] * len(hbm_args),
        out_specs=tuple(hbm if in_hbm(out) else (smem if out.dtype == jnp.int32 and out.shape == (1, 1) else vmem) for out in outs),
        scratch_shapes=list(scratch),
        input_output_aliases=aliases or {},
        compiler_params=pltpu.CompilerParams(vmem_limit_bytes=8 * 1024 * 1024),
    )(*args, *[pltpu.with_memory_space_constraint(x, pltpu.HBM) for x in hbm_args])


def per_device(mesh, load, stiffness, pair_code, pair_weight):
    layers, rows, lanes = load.shape
    pairs = pair_code.shape[0]
    assert lanes == LANES and rows % 8 == 0 and rows >= 16 * ORDER + 8 and layers % 4 == 0
    plan = Plan(mesh, layers, rows, pairs)
    nb, nx, ny = plan.nb, plan.nx, plan.ny
    count = nb * nx * ny
    nf = len(plan.sb)
    buf = plan.buf
    bind = lambda kernel: functools.partial(kernel, plan)
    sems = lambda n: pltpu.SemaphoreType.DMA((n,))

    def lateral(row_kind, lane_kind, array):
        a, b = swap_perm(row_kind, nx), swap_perm(lane_kind, ny)
        aside = nb > 1 and nb % 2 == 0
        pairs = []
        for body in range(nb):
            for i, j in itertools.product(range(nx), range(ny)):
                wraps = abs(a[i][1] - i) > 1 or abs(b[j][1] - j) > 1
                here, there = (body, i, j), (body, a[i][1], b[j][1])
                if wraps and aside:
                    there = (body ^ 1, i, j)
                pairs.append(tuple((p * nx + q) * ny + r for p, q, r in (here, there)))
        return lax.ppermute(array, ALL, pairs)

    def across(kind, array):
        side = nx * ny
        pairs = []
        for b, to in swap_perm(kind, nb):
            for i in range(side):
                pairs.append((b * side + i, to * side + i) if abs(to - b) == 1 else (b * side + i, b * side + (i ^ 1)))
        return lax.ppermute(array, ALL, pairs)

    def spread(moments, faces):
        return lax.all_to_all(moments, ALL, 0, 0, tiled=True), [across(k, f) for k, f in zip(plan.sb, faces)]

    kinds = [(k, "") for k in plan.sx] + [("", k) for k in plan.sy] + [(a, b) for a in plan.sx for b in plan.sy]
    vec, stack = held(*plan.vec), held(2, layers, buf, LANES)
    face = shaped(ORDER + 1, plan.face, LANES)
    message = shaped(count, 1, LANES)
    mask = held(2, buf, LANES)
    pairing, tables = held(2, pairs, 2, buf, LANES), held(SPAN * SPAN, 2, buf, LANES)
    cells = (layers, rows, LANES)
    shifted = pltpu.VMEM((2, SPAN, 2, buf, LANES), F32)

    shapes = [shaped(plan.piece_rows, LANES) for _ in plan.sx]
    shapes += [shaped(plan.strip_tiles, rows, LANES) for _ in plan.sy]
    shapes += [shaped(plan.unit_tiles, 8, LANES) for _ in plan.sx for _ in plan.sy]
    b0, diag, codes, weights, *packed = call(
        bind(pack_kernel),
        (),
        [vec, stack, held(pairs, rows, LANES, dtype=jnp.int32), held(pairs, rows, LANES)] + shapes,
        [sems(4)],
        hbm_args=(load, stiffness, pair_code, pair_weight),
    )
    halos = []
    for (a, b), m in zip(kinds, packed):
        halos.append(lateral(a, b, m))
    b0, diag, pair, inside, table, b1, b2 = call(
        bind(prepare_kernel),
        (b0, diag, codes, weights),
        [vec, stack, pairing, mask, tables, vec, vec],
        aliases={0: 0, 1: 1},
    )
    nx_msgs, ny_msgs = len(plan.sx), len(plan.sy)
    row_halos, lane_halos, corner_halos = halos[:nx_msgs], halos[nx_msgs : nx_msgs + ny_msgs], halos[nx_msgs + ny_msgs :]
    b0, diag, pair, b1, b2, table, b3 = call(
        bind(inner_kernel),
        (*lane_halos, inside, b0, diag, pair, b1, b2, table),
        [vec, stack, pairing, vec, vec, tables, vec],
        aliases={ny_msgs + 1 + i: i for i in range(6)},
    )
    at = len(row_halos) + len(corner_halos) + 1
    moments, *rest = call(
        bind(krylov_kernel),
        (*row_halos, *corner_halos, inside, b0, diag, pair, b1, b2, table, b3),
        [message] + [face] * nf + [vec, stack, pairing, vec, vec, tables, vec],
        aliases={at + i: 1 + nf + i for i in range(7)},
    )
    faces, (b0, diag, _, b1, b2, table, b3) = rest[:nf], rest[nf:]
    moments, faces = spread(moments, faces)
    moments, *rest = call(
        bind(middle_kernel),
        (moments, *faces, b0, b1, b2, b3, diag, inside, table),
        [message] + [face] * nf + [vec] * 3 + [held(*cells), mask, held(buf, LANES), held(nb, LANES)],
        [shifted],
    )
    faces, kept_arrays = rest[:nf], rest[nf:]
    moments, faces = spread(moments, faces)
    found, lifted, again = call(
        bind(final_kernel),
        (moments, *faces, *kept_arrays, table),
        [kept(*cells)] * 2 + [jax.ShapeDtypeStruct((1, 1), jnp.int32)],
        [pltpu.VMEM(cells, F32), pltpu.VMEM(cells, F32), pltpu.VMEM((2, buf, LANES), F32), shifted, sems(5)],
    )

    def same(arrays, flag):
        vmem = pl.BlockSpec(memory_space=pltpu.VMEM)
        return pl.pallas_call(
copy_refs,
            out_shape=[jax.ShapeDtypeStruct(a.shape, a.dtype) for a in arrays],
            in_specs=[pl.BlockSpec(memory_space=pltpu.SMEM)] + [vmem] * len(arrays),
            out_specs=[vmem] * len(arrays),
            name="same",
        )(flag, *arrays)

    def redo(state):
        inputs = same((load, stiffness, pair_code, pair_weight), state[2])
        return (*same(step_by_step(*inputs), state[2]), jnp.zeros_like(state[2]))

    found, lifted, _ = lax.while_loop(lambda state: state[2][0, 0] > 0, redo, (found, lifted, again))
    return found, lifted


def solution(mesh):
    def whole(*args):
        return per_device(mesh, *args)

    step = jax.shard_map(
        whole,
        mesh=mesh,
        in_specs=(P("body", "gx", "gy"), P("body", "gx", "gy"), P(None, "gx", "gy"), P(None, "gx", "gy")),
        out_specs=(P("body", "gx", "gy"), P("body", "gx", "gy")),
        check_vma=False,
    )
    if "B" not in swaps_of(mesh.shape["gy"]) or not swaps_of(mesh.shape["gx"]):
        return step
    return step
```

```python
import functools
import itertools

import jax
import jax.numpy as jnp
from jax import lax
from jax.experimental import pallas as pl
from jax.experimental.pallas import tpu as pltpu
from jax.sharding import PartitionSpec as P


REACH = 2
SPAN = 2 * REACH + 1
RATE = 2.0
CENTRE = 7.5
LANES = 128
STRIP = 16
SLOTS = LANES // STRIP
PAD = 24
ORDER = 3
UNROLL = 8
CHUNK = 40
UPDATES = 2
STEADY = 0.05
F32 = jnp.float32
G = ("gx", "gy")
ALL = ("body", "gx", "gy")


def swaps_of(count):
    return () if count < 2 else (("A",) if count == 2 else ("A", "B"))


def swap_perm(kind, count):
    if kind == "":
        return [(i, i) for i in range(count)]
    step = 1 if kind == "A" else -1
    return [(i, (i + (step if i % 2 == 0 else -step)) % count) for i in range(count)]


def swap_up(kind, index):
    even = lax.rem(index, 2) == 0
    return even if kind == "A" else jnp.logical_not(even)


def swap_valid(kind, index, count):
    if kind == "A":
        return index >= 0
    return jnp.where(swap_up(kind, index), index < count - 1, index > 0)


def row_units(layers, pairs):
    wide_load = (0, 1, layers - 3, layers - 2, layers - 1)
    wide_stiff = (0, layers - 3, layers - 2, layers - 1)
    units = []
    for which, wide in ((0, wide_load), (1, wide_stiff)):
        for layer in range(layers):
            units.append((which, layer, False))
            if layer in wide:
                units.append((which, layer, True))
    for which in (2, 3):
        units += [(which, k, False) for k in range(pairs)]
    return units


def row_pieces(layers, pairs):
    top = layers - 1
    load = {top: 12, top - 1: 11, top - 2: 10, 0: 10, 1: 9, 2: 8}
    stiff = {top: 11, top - 1: 10, top - 2: 6, 0: 9, 1: 8}
    pieces = [(0, k, load.get(k, 6)) for k in range(layers)] + [(1, k, stiff.get(k, 5)) for k in range(layers)]
    pieces += [(which, k, 8) for which in (2, 3) for k in range(pairs)]
    placed, at = [], 0
    for which, k, size in pieces:
        placed.append((which, k, size, at))
        at += size
    return placed


def strip_list(layers, pairs):
    return [(w, k) for w in (0, 1) for k in range(layers)] + [(w, k) for w in (2, 3) for k in range(pairs)]


def lane_iota(rows):
    return lax.broadcasted_iota(jnp.int32, (rows, LANES), 1)


def aligned(start):
    return pl.multiple_of(start, 8)


def chunks(first, size, step):
    return [(at, min(step, first + size - at)) for at in range(first, first + size, step)]


class Plan:
    def __init__(self, mesh, layers, rows, pairs):
        self.nb, self.nx, self.ny = (mesh.shape[a] for a in ALL)
        self.layers, self.rows, self.pairs = layers, rows, pairs
        self.buf = rows + 2 * PAD
        self.units = row_units(layers, pairs)
        self.strips = strip_list(layers, pairs)
        self.pieces = row_pieces(layers, pairs)
        self.piece_rows = -(-(self.pieces[-1][2] + self.pieces[-1][3]) // 8) * 8
        self.sx, self.sy, self.sb = swaps_of(self.nx), swaps_of(self.ny), swaps_of(self.nb)
        self.face = rows + 16
        self.vec = (2, layers + 2, self.buf, LANES)
        self.own = pl.ds(PAD, rows)
        self.near = pl.ds(PAD - 8, self.face)
        self.unit_tiles = -(-len(self.units) // SLOTS)
        self.strip_tiles = -(-len(self.strips) // SLOTS)


class Args:
    def __init__(self, refs):
        self.refs = list(refs)

    def take(self, count):
        got, self.refs = self.refs[:count], self.refs[count:]
        return got

    def one(self):
        return self.refs.pop(0)


def pack_kernel(plan, load, stiff, code, weight, *refs):
    args = Args(refs)
    b0, diag, codes, weights = args.take(4)
    row_out, lane_out = args.take(len(plan.sx)), args.take(len(plan.sy))
    corner_out = args.take(len(plan.sx) * len(plan.sy))
    sems = args.one()
    ix, iy = lax.axis_index("gx"), lax.axis_index("gy")
    rows, layers = plan.rows, plan.layers
    places = (b0.at[0, pl.ds(1, layers), plan.own, :], diag.at[0, :, plan.own, :], codes, weights)
    copies = [
        pltpu.make_async_copy(src, dst, sems.at[i]) for i, (src, dst) in enumerate(zip((load, stiff, code, weight), places))
    ]
    for copy in copies:
        copy.start()
    arrived = set()

    def take(which, k, start, size):
        if which not in arrived:
            copies[which].wait()
            arrived.add(which)
        if which == 0:
            return b0[0, k + 1, pl.ds(PAD + start, size), :]
        if which == 1:
            return diag[0, k, pl.ds(PAD + start, size), :]
        return (codes, weights)[which - 2][k, pl.ds(start, size), :].astype(F32)

    def starts(kind):
        up = swap_up(kind, ix)
        return aligned(jnp.where(up, rows - 8, 0)), aligned(jnp.where(up, rows - 16, 8))

    def gather(pieces, size, tile, outs):
        slot_of = lane_iota(size) // STRIP
        last, first = jnp.zeros((size, LANES), F32), jnp.zeros((size, LANES), F32)
        for slot, value in enumerate(pieces):
            moved = pltpu.roll(value, STRIP * (slot + 1) % LANES, 1) if slot + 1 < SLOTS else value
            last = jnp.where(slot_of == slot, moved, last)
            first = jnp.where(slot_of == (slot + 1) % SLOTS, moved, first)
        for kind, out in zip(plan.sy, outs):
            out[tile] = jnp.where(swap_up(kind, iy), last, first)

    for kind, out in zip(plan.sx, row_out):
        up = swap_up(kind, ix)
        for which, k, size, at in plan.pieces:
            out[pl.ds(at, size), :] = jnp.where(up, take(which, k, rows - size, size), take(which, k, 0, size))
        used = plan.pieces[-1][2] + plan.pieces[-1][3]
        if used < plan.piece_rows:
            out[pl.ds(used, plan.piece_rows - used), :] = jnp.zeros((plan.piece_rows - used, LANES), F32)
    for tile in range(plan.strip_tiles):
        members = plan.strips[tile * SLOTS : (tile + 1) * SLOTS]
        gather([take(which, k, 0, rows) for which, k in members], rows, tile, lane_out)
    for i, row_kind in enumerate(plan.sx):
        near, far = starts(row_kind)
        outs = corner_out[i * len(plan.sy) : (i + 1) * len(plan.sy)]
        for tile in range(plan.unit_tiles):
            members = plan.units[tile * SLOTS : (tile + 1) * SLOTS]
            gather([take(which, k, far if is_far else near, 8) for which, k, is_far in members], 8, tile, outs)


def clear_frame(plan, vec):
    zero = jnp.zeros((16, LANES), F32)
    for t in (0, 1):
        for edge in (0, plan.layers + 1):
            vec[t, edge] = jnp.zeros((plan.buf, LANES), F32)
        for layer in range(1, plan.layers + 1):
            vec[t, layer, pl.ds(0, 16), :] = zero
            vec[t, layer, pl.ds(plan.buf - 16, 16), :] = zero


def table_rows(plan, pairing, tables, t, first, size):
    span = pl.ds(first, size)
    codes = [pairing[0, k, t, span, :] for k in range(plan.pairs)]
    weights = [pairing[1, k, t, span, :] for k in range(plan.pairs)]
    for offset in range(SPAN * SPAN):
        total = jnp.where(codes[0] == offset, weights[0], 0.0)
        for k in range(1, plan.pairs):
            total = total + jnp.where(codes[k] == offset, weights[k], 0.0)
        tables[offset, t, span, :] = total


def prepare_kernel(plan, b0_in, diag_in, codes, weights, b0, diag, pairing, inside, tables, *vecs):
    del b0_in, diag_in
    ix, iy = lax.axis_index("gx"), lax.axis_index("gy")
    rows, layers, buf = plan.rows, plan.layers, plan.buf
    row = lax.broadcasted_iota(jnp.int32, (buf, LANES), 0) + ix * rows - PAD
    lane = lane_iota(buf)
    in_rows = jnp.logical_and(row >= 0, row < plan.nx * rows)
    right = jnp.logical_and(lane < STRIP, iy < plan.ny - 1)
    left = jnp.logical_and(lane >= LANES - STRIP, iy > 0)
    inside[0] = jnp.where(in_rows, 1.0, 0.0)
    inside[1] = jnp.where(jnp.logical_and(in_rows, jnp.logical_or(right, left)), 1.0, 0.0)
    zero = jnp.zeros((PAD, LANES), F32)
    for t in (0, 1):
        for span in (pl.ds(0, PAD), pl.ds(buf - PAD, PAD)):
            for layer in range(layers):
                b0[t, layer + 1, span, :] = zero
                diag[t, layer, span, :] = zero
            for k in range(plan.pairs):
                for i in (0, 1):
                    pairing[i, k, t, span, :] = zero
        for edge in (0, layers + 1):
            b0[t, edge] = jnp.zeros((buf, LANES), F32)
        for offset in range(SPAN * SPAN):
            tables[offset, t, pl.ds(PAD - 16, 8), :] = jnp.zeros((8, LANES), F32)
            tables[offset, t, pl.ds(PAD + rows + 8, 8), :] = jnp.zeros((8, LANES), F32)
    for vec in vecs:
        clear_frame(plan, vec)
    for layer in range(layers):
        diag[0, layer, plan.own, :] = diag[0, layer, plan.own, :] + (6.0 - CENTRE)
    for k in range(plan.pairs):
        pairing[0, k, 0, plan.own, :] = codes[k].astype(F32)
        pairing[1, k, 0, plan.own, :] = weights[k]
    for first, size in chunks(PAD, rows, 32):
        table_rows(plan, pairing, tables, 0, first, size)


def operate(src, at, diag, layer, inside, first, size, tiles=(0, 1), masked=True):
    lane = lane_iota(size)
    start, end = lane == 0, lane == LANES - 1
    rows = pl.ds(first, size)
    middle = [src[t, at, rows, :] for t in (0, 1)]
    before = [pltpu.roll(m, 1, 1) for m in middle]
    after = [pltpu.roll(m, LANES - 1, 1) for m in middle]
    done = []
    for t in tiles:
        total = jnp.where(start, before[1 - t], before[t]) + jnp.where(end, after[1 - t], after[t])
        total = total + src[t, at, pl.ds(first - 1, size), :]
        total = total + src[t, at, pl.ds(first + 1, size), :]
        total = total + (src[t, at - 1, rows, :] + src[t, at + 1, rows, :])
        if masked or t == 1:
            total = total * inside[t, rows, :]
        done.append(diag[t, layer, rows, :] * middle[t] - total)
    return done


def apply_rows(src, dst, at, diag, layer, inside, parts):
    values = [operate(src, at, diag, layer, inside, first, size, masked=masked) for first, size, masked in parts]
    for (first, size, _), pair in zip(parts, values):
        for t in (0, 1):
            dst[t, at, pl.ds(first, size), :] = pair[t]
    return [pair[0] for pair in values]


def apply_joined(src, dst, at, diag, layer, inside, parts):
    spans = [pl.ds(first, size) for first, size, _ in parts]
    size = sum(p[1] for p in parts)
    lane = lane_iota(size)
    start, end = lane == 0, lane == LANES - 1
    join = lambda values: values[0] if len(values) == 1 else jnp.concatenate(values, axis=0)
    middle = [join([src[t, at, span, :] for span in spans]) for t in (0, 1)]
    before = [pltpu.roll(m, 1, 1) for m in middle]
    after = [pltpu.roll(m, LANES - 1, 1) for m in middle]
    done = []
    for t in (0, 1):
        sides = jnp.where(start, before[1 - t], before[t]) + jnp.where(end, after[1 - t], after[t])
        values, low = [], 0
        for (first, rows, masked), span in zip(parts, spans):
            total = sides[low : low + rows]
            total = total + src[t, at, pl.ds(first - 1, rows), :]
            total = total + src[t, at, pl.ds(first + 1, rows), :]
            total = total + (src[t, at - 1, span, :] + src[t, at + 1, span, :])
            if masked or t == 1:
                total = total * inside[t, span, :]
            values.append(diag[t, layer, span, :] * middle[t][low : low + rows] - total)
            low += rows
        done.append(values)
    for i, span in enumerate(spans):
        for t in (0, 1):
            dst[t, at, span, :] = done[t][i]
    return done[0]


def near_rows(plan):
    outer = [(PAD - 8, 8, True), (PAD + plan.rows, 8, True)]
    return outer + [(first, size, False) for first, size in chunks(PAD, plan.rows, 32)]


def inner_rows(plan, step):
    return [(first, size, False) for first, size in chunks(PAD + 8 * step, plan.rows - 16 * step, 32)]


def outer_rows(plan, step):
    wide = 8 * step
    outer = [(PAD - 8, 8, True), (PAD + plan.rows, 8, True)]
    return outer + [(PAD, wide, False), (PAD + plan.rows - wide, wide, False)]


def apply_all(plan, src, dst, diag, inside, parts, apply=apply_rows):
    def one(layer, carry):
        apply(src, dst, layer + 1, diag, layer, inside, parts)
        return carry

    lax.fori_loop(0, plan.layers, one, 0, unroll=UNROLL)


def apply_own(plan, src, at, diag, layer, inside):
    parts = [
        operate(src, at, diag, layer, inside, first, size, (0,), False)[0] for first, size in chunks(PAD, plan.rows, 32)
    ]
    return jnp.concatenate(parts, axis=0)


def six_sums(parts):
    lane = lax.broadcasted_iota(jnp.int32, (1, LANES), 1)
    row = jnp.zeros((1, LANES), F32)
    for k, part in enumerate(parts):
        row = jnp.where(lane == k, jnp.sum(part), row)
    return row


def fold(value):
    return jnp.sum(value.reshape(-1, 8, LANES), axis=0)


def add_products(sums, v):
    pairs = ((v[0], v[0]), (v[0], v[1]), (v[1], v[1]), (v[1], v[2]), (v[2], v[2]), (v[2], v[3]))
    return tuple(s + fold(a * b) for s, (a, b) in zip(sums, pairs))


def put_moments(moments, sums):
    moments[...] = jnp.broadcast_to(six_sums(sums).reshape(1, 1, LANES), moments.shape)


def no_sums():
    return (jnp.zeros((8, LANES), F32),) * 6


def put_cells(arrays, which, k, t, where, value):
    b0, diag, pairing = arrays
    if which == 0:
        b0[t, k + 1, where, :] = value
    elif which == 1:
        diag[t, k, where, :] = value + (6.0 - CENTRE)
    else:
        pairing[which - 2, k, t, where, :] = value


def unpack(plan, msgs, tile, size):
    iy = lax.axis_index("gy")
    sides = []
    for right in (True, False):
        total = jnp.zeros((size, LANES), F32)
        for kind, msg in zip(plan.sy, msgs):
            use = jnp.logical_and(swap_up(kind, iy) == right, swap_valid(kind, iy, plan.ny))
            total = jnp.where(use, msg[tile], total)
        sides.append(total)
    even = lax.rem(lane_iota(size) // STRIP, 2) == 0
    return jnp.where(even, sides[1], sides[0]), jnp.where(even, sides[0], sides[1])


def piece(both, slot):
    turn = STRIP * (SLOTS - 1 - slot)
    return pltpu.roll(both[slot % 2], turn, 1) if turn else both[slot % 2]


def inner_kernel(plan, *refs):
    args = Args(refs)
    msgs = args.take(len(plan.sy))
    inside, _, _, _, _, _, _ = args.take(7)
    b0, diag, pairing, b1, b2, tables, b3 = args.take(7)
    for tile in range(plan.strip_tiles):
        both = unpack(plan, msgs, tile, plan.rows)
        for slot, (which, k) in enumerate(plan.strips[tile * SLOTS : (tile + 1) * SLOTS]):
            put_cells((b0, diag, pairing), which, k, 1, plan.own, piece(both, slot))
    for step, (src, dst) in enumerate(((b0, b1), (b1, b2), (b2, b3))):
        apply_all(plan, src, dst, diag, inside, inner_rows(plan, step + 1))
    for first, size in chunks(PAD, plan.rows, 32):
        table_rows(plan, pairing, tables, 1, first, size)


def krylov_kernel(plan, *refs):
    args = Args(refs)
    row_msgs = args.take(len(plan.sx))
    corner_msgs = args.take(len(plan.sx) * len(plan.sy))
    inside = args.one()
    args.take(7)
    moments, = args.take(1)
    faces = args.take(len(plan.sb))
    b0, diag, pairing, b1, b2, tables, b3 = args.take(7)
    ix = lax.axis_index("gx")
    rows, layers = plan.rows, plan.layers
    arrays = (b0, diag, pairing)

    def spots(kind):
        up = swap_up(kind, ix)
        near = aligned(jnp.where(up, PAD + rows, PAD - 8))
        far = aligned(jnp.where(up, PAD + rows + 8, PAD - 16))
        return near, far, swap_valid(kind, ix, plan.nx)

    for kind, msg in zip(plan.sx, row_msgs):
        up, ok = swap_up(kind, ix), swap_valid(kind, ix, plan.nx)

        @pl.when(jnp.logical_and(up, ok))
        def _():
            for which, k, size, at in plan.pieces:
                put_cells(arrays, which, k, 0, pl.ds(PAD + rows, size), msg[pl.ds(at, size), :])

        @pl.when(jnp.logical_and(jnp.logical_not(up), ok))
        def _():
            for which, k, size, at in plan.pieces:
                put_cells(arrays, which, k, 0, pl.ds(PAD - size, size), msg[pl.ds(at, size), :])

    for i, row_kind in enumerate(plan.sx):
        near, far, ok = spots(row_kind)
        for tile in range(plan.unit_tiles):
            both = unpack(plan, corner_msgs[i * len(plan.sy) : (i + 1) * len(plan.sy)], tile, 8)
            both = [jnp.where(ok, b, 0.0) for b in both]
            for slot, (which, k, is_far) in enumerate(plan.units[tile * SLOTS : (tile + 1) * SLOTS]):
                put_cells(arrays, which, k, 1, pl.ds(far if is_far else near, 8), piece(both, slot))

    for step, (src, dst, wide) in enumerate(((b0, b1, (0, layers - 2, layers - 1)), (b1, b2, (layers - 1,)))):
        apply_all(plan, src, dst, diag, inside, outer_rows(plan, step + 1), apply_joined)
        for layer in wide:
            for first in (PAD - 16, PAD + rows + 8):
                for t, value in enumerate(operate(src, layer + 1, diag, layer, inside, first, 8)):
                    dst[t, layer + 1, pl.ds(first, 8), :] = value

    middle = pl.ds(PAD + 8 * ORDER, rows - 16 * ORDER)

    def one(layer, sums):
        ends = apply_joined(b2, b3, layer + 1, diag, layer, inside, outer_rows(plan, ORDER))[2:]
        last = jnp.concatenate([ends[0], b3[0, layer + 1, middle, :], ends[1]], axis=0)
        return add_products(sums, [v[0, layer + 1, plan.own, :] for v in (b0, b1, b2)] + [last])

    put_moments(moments, lax.fori_loop(0, layers, one, no_sums(), unroll=UNROLL))

    for t in (0, 1):
        for first in (PAD - 8, PAD + rows):
            table_rows(plan, pairing, tables, t, first, 8)
    vecs = (b0, b1, b2)
    put_faces(plan, lambda k, t: vecs[k][t, layers, plan.near, :], lambda k, t: vecs[k][t, 1, plan.near, :], faces)


def lane_shift(first, second, by, lane):
    if by == 0:
        return first, second
    a, b = pltpu.roll(first, (-by) % LANES, 1), pltpu.roll(second, (-by) % LANES, 1)
    keep = lane < LANES - by if by > 0 else lane >= -by
    return jnp.where(keep, a, b), jnp.where(keep, b, a)


def put_shifted(shifted, n, first, size, planes):
    lane = lane_iota(size)
    for i in range(SPAN):
        for t, value in enumerate(lane_shift(planes[0], planes[1], i - REACH, lane)):
            shifted[n, i, t, pl.ds(first, size), :] = value


def pull(tables, shifted, count, t, first, size):
    total = [jnp.zeros((size, LANES), F32)] * count
    for offset in range(SPAN * SPAN):
        table = tables[offset, t, pl.ds(first, size), :]
        window = pl.ds(first + offset // SPAN - REACH, size)
        for n in range(count):
            total[n] = total[n] + table * shifted[n, offset % SPAN, t, window, :]
    return total


def push(tables, face, first, size, tiles=(0, 1)):
    lane = lane_iota(size)
    total = [jnp.zeros((size, LANES), F32)] * 2
    for i in range(SPAN):
        column = [jnp.zeros((size, LANES), F32)] * 2
        for j in range(SPAN):
            window = pl.ds(first - (j - REACH), size)
            for t in (0, 1):
                column[t] = column[t] + tables[j * SPAN + i, t, window, :] * face[t, window, :]
        moved = lane_shift(column[0], column[1], REACH - i, lane)
        total = [total[t] + moved[t] for t in (0, 1)]
    return [total[t] for t in tiles]


def put_faces(plan, tops, bottoms, outs):
    ib = lax.axis_index("body")
    lane = lane_iota(plan.face)
    for kind, out in zip(plan.sb, outs):
        up = swap_up(kind, ib)
        packed = jnp.zeros((plan.face, LANES), F32)
        for k in range(ORDER):
            out[k] = jnp.where(up, tops(k, 0), bottoms(k, 0))
            strips = pltpu.roll(jnp.where(up, tops(k, 1), bottoms(k, 1)), STRIP + 2 * STRIP * k, 1)
            packed = jnp.where(lane // (2 * STRIP) == k, strips, packed)
        out[ORDER] = packed


def get_face(plan, msgs, coef, up, low, size, tiles=(0, 1)):
    ib = lax.axis_index("body")
    total = [jnp.zeros((size, LANES), F32)] * 2
    for kind, msg in zip(plan.sb, msgs):
        use = jnp.logical_and(swap_up(kind, ib) == up, swap_valid(kind, ib, plan.nb))
        rows = pl.ds(low, size)
        for t in tiles:
            if t == 0:
                value = sum(coef[k] * msg[k, rows, :] for k in range(ORDER))
            else:
                strips = msg[ORDER, rows, :]
                value = sum(
                    coef[k] * pltpu.roll(strips, (LANES - STRIP - 2 * STRIP * k) % LANES, 1) for k in range(ORDER)
                )
            total[t] = jnp.where(use, value, total[t])
    return [total[t] for t in tiles]


def solve(plan, moments):
    per = plan.nx * plan.ny
    body = lax.broadcasted_iota(jnp.int32, (plan.nb, LANES), 0)
    table = jnp.zeros((plan.nb, LANES), F32)
    for b in range(plan.nb):
        row = [moments[b * per + i] for i in range(per)]
        while len(row) > 1:
            row = [x + y for x, y in zip(row[::2], row[1::2])] + row[len(row) // 2 * 2 :]
        table = jnp.where(body == b, row[0], table)
    lane = lax.broadcasted_iota(jnp.int32, (plan.nb, LANES), 1)
    m = [
        jnp.broadcast_to(jnp.sum(jnp.where(lane == k, table, 0.0), axis=1, keepdims=True), table.shape)
        for k in range(6)
    ]
    h = [m[n + 1] + CENTRE * m[n] for n in range(5)]
    f1, f2 = h[1] / h[0], h[2] / h[0]
    d1 = h[2] - f1 * h[1]
    e = h[3] - f1 * h[2]
    f3 = e / d1
    d2 = h[4] - f2 * h[2] - f3 * e
    g1 = m[1] - f1 * m[0]
    g2 = m[2] - f2 * m[0] - f3 * g1
    c2 = g2 / d2
    c1 = (g1 - e * c2) / d1
    c0 = (m[0] - h[1] * c1 - h[2] * c2) / h[0]

    steady = jnp.minimum(d1 / h[2], d2 / h[4])

    def pick(index):
        return [jnp.sum(jnp.where(body == index, c, 0.0), axis=0, keepdims=True) for c in (c0, c1, c2)]

    ib = lax.axis_index("body")
    return pick(ib), pick(ib + 1), pick(ib - 1), jnp.where(steady > STEADY, 0.0, 1.0)


def residual_coefs(c):
    return 1.0 - CENTRE * c[0], -(c[0] + CENTRE * c[1]), -(c[1] + CENTRE * c[2]), -c[2]


def middle_kernel(plan, moments_in, *refs):
    args = Args(refs)
    msgs = args.take(len(plan.sb))
    basis = args.take(4)
    diag, inside, tables = args.take(3)
    args.take(ORDER)
    moments, = args.take(1)
    faces = args.take(len(plan.sb))
    vecs = args.take(3)
    base, above_lambda, below_lambda, doubt, shifted = args.take(5)
    ib = lax.axis_index("body")
    rows, layers = plan.rows, plan.layers
    has_above, has_below = ib < plan.nb - 1, ib > 0
    c, above_c, below_c, doubt[...] = solve(plan, moments_in)
    d = residual_coefs(c)
    near, own = plan.near, plan.own

    def combine(layer, carry):
        for first, size in chunks(PAD - 8, plan.face, 40):
            for t in (0, 1):
                span = pl.ds(first, size)
                vecs[0][t, layer + 1, span, :] = sum(x * v[t, layer + 1, span, :] for x, v in zip(d, basis))
        base[layer] = sum(x * v[0, layer + 1, own, :] for x, v in zip(c, basis))
        return carry

    lax.fori_loop(0, layers, combine, 0)

    zero = jnp.zeros((8, LANES), F32)
    for first, size in chunks(PAD - 16, plan.face + 16, 32):
        span = pl.ds(first, size)
        top = [sum(x * v[t, layers, span, :] for x, v in zip(c, basis)) for t in (0, 1)]
        put_shifted(shifted, 0, first, size, top)
    for t in (0, 1):
        for i in range(SPAN):
            shifted[1, i, t, pl.ds(PAD - 16, 8), :] = zero
            shifted[1, i, t, pl.ds(PAD + rows + 8, 8), :] = zero
    for first, size in chunks(PAD - 8, plan.face, CHUNK):
        low = first - PAD + 8
        put_shifted(shifted, 1, first, size, get_face(plan, msgs, below_c, False, low, size))
        for t, value in enumerate(get_face(plan, msgs, above_c, True, low, size)):
            above_lambda[t, pl.ds(first, size), :] = value
    for t in (0, 1):
        above_lambda[t, pl.ds(PAD - 16, 8), :] = zero
        above_lambda[t, pl.ds(PAD + rows + 8, 8), :] = zero
        for first, size in chunks(PAD - 8, plan.face, CHUNK):
            span = pl.ds(first, size)
            pulled, master = pull(tables, shifted, 2, t, first, size)
            above_lambda[t, span, :] = jnp.where(has_above, RATE * (above_lambda[t, span, :] - pulled), 0.0)
            gap = sum(x * basis[k][t, 1, span, :] for k, x in enumerate(c)) - master
            gap = jnp.where(has_below, RATE * gap, 0.0)
            if t == 0:
                below_lambda[span, :] = gap
            vecs[0][t, 1, span, :] = vecs[0][t, 1, span, :] - gap
    for first, size in chunks(PAD - 8, plan.face, CHUNK):
        span = pl.ds(first, size)
        for t, value in enumerate(push(tables, above_lambda, first, size)):
            vecs[0][t, layers, span, :] = vecs[0][t, layers, span, :] + value * inside[t, span, :]

    for step in range(2):
        apply_all(plan, vecs[step], vecs[step + 1], diag, inside, near_rows(plan))

    def one(layer, sums):
        last = apply_own(plan, vecs[2], layer + 1, diag, layer, inside)
        return add_products(sums, [v[0, layer + 1, own, :] for v in vecs] + [last])

    put_moments(moments, lax.fori_loop(0, layers, one, no_sums(), unroll=UNROLL))

    put_faces(plan, lambda k, t: vecs[k][t, layers, near, :], lambda k, t: vecs[k][t, 1, near, :], faces)


def final_kernel(plan, moments_in, *refs):
    args = Args(refs)
    msgs = args.take(len(plan.sb))
    vecs = args.take(3)
    base, above_lambda, below_lambda, doubt, tables = args.take(5)
    solution_out, interface_out, again, solution, interface, lifted, shifted, sems = args.take(8)
    ib = lax.axis_index("body")
    rows, layers = plan.rows, plan.layers
    has_above, has_below = ib < plan.nb - 1, ib > 0
    inner = pl.ds(1, layers - 2)
    copies = [pltpu.make_async_copy(interface.at[inner], interface_out.at[inner], sems.at[0])]
    for layer in range(1, layers - 1):
        interface[layer] = jnp.zeros((rows, LANES), F32)
    copies[0].start()
    c, above_c, below_c, doubt_now = solve(plan, moments_in)
    again[0, 0] = jnp.where(jnp.max(jnp.maximum(doubt[...], doubt_now)) > 0.5, 1, 0)
    own = plan.own
    half = layers // 2
    for i, (low, high) in enumerate(((0, half), (half, layers))):

        def combine(layer, carry):
            solution[layer] = base[layer] + sum(x * v[0, layer + 1, own, :] for x, v in zip(c, vecs))
            return carry

        lax.fori_loop(low, high, combine, 0, unroll=UNROLL)
        part = pl.ds(low, high - low)
        copies.append(pltpu.make_async_copy(solution.at[part], solution_out.at[part], sems.at[1 + i]))
        copies[-1].start()

    zero = jnp.zeros((8, LANES), F32)
    for n in (0, 1):
        for t in (0, 1):
            for i in range(SPAN):
                shifted[n, i, t, pl.ds(PAD - 16, 8), :] = zero
                shifted[n, i, t, pl.ds(PAD + rows + 8, 8), :] = zero
    for first, size in chunks(PAD - 8, plan.face, CHUNK):
        span = pl.ds(first, size)
        low = first - PAD + 8
        put_shifted(shifted, 0, first, size, get_face(plan, msgs, below_c, False, low, size))
        put_shifted(shifted, 1, first, size, [sum(x * v[t, layers, span, :] for x, v in zip(c, vecs)) for t in (0, 1)])
        for t, value in enumerate(get_face(plan, msgs, above_c, True, low, size)):
            lifted[t, span, :] = value
    master = pull(tables, shifted, 1, 0, PAD, rows)[0]
    gap = sum(x * v[0, 1, own, :] for x, v in zip(c, vecs)) - master
    interface[0] = -(2.0 * below_lambda[own, :] + jnp.where(has_below, RATE * gap, 0.0))
    copies.append(pltpu.make_async_copy(interface.at[0], interface_out.at[0], sems.at[3]))
    copies[-1].start()
    for t in (0, 1):
        lifted[t, pl.ds(PAD - 16, 8), :] = zero
        lifted[t, pl.ds(PAD + rows + 8, 8), :] = zero
        for first, size in chunks(PAD - 8, plan.face, CHUNK):
            span = pl.ds(first, size)
            gap = lifted[t, span, :] - pull(tables, shifted.at[pl.ds(1, 1)], 1, t, first, size)[0]
            lifted[t, span, :] = 2.0 * above_lambda[t, span, :] + jnp.where(has_above, RATE * gap, 0.0)
    for first, size in chunks(PAD, rows, CHUNK):
        interface[layers - 1, pl.ds(first - PAD, size), :] = push(tables, lifted, first, size, (0,))[0]
    copies.append(pltpu.make_async_copy(interface.at[layers - 1], interface_out.at[layers - 1], sems.at[4]))
    copies[-1].start()
    for copy in copies:
        copy.wait()


def with_halo(cells, sides, width):
    for axis, dim in sides:
        count = lax.axis_size(axis)
        head = lax.slice_in_dim(cells, 0, width, axis=dim)
        tail = lax.slice_in_dim(cells, cells.shape[dim] - width, cells.shape[dim], axis=dim)
        left = lax.ppermute(tail, axis, [(i, i + 1) for i in range(count - 1)])
        right = lax.ppermute(head, axis, [(i + 1, i) for i in range(count - 1)])
        cells = jnp.concatenate([left, cells, right], axis=dim)
    return cells


def passed_along(array, axis, by):
    count = lax.axis_size(axis)
    return lax.ppermute(array, axis, [(i, i + by) for i in range(count) if 0 <= i + by < count])


def copy_refs(flag, *refs):
    del flag
    half = len(refs) // 2
    for src, dst in zip(refs[:half], refs[half:]):
        dst[...] = src[...]


def step_by_step(load, stiffness, pair_code, pair_weight):
    layers, rows, cols = load.shape
    position = lax.axis_index("body")
    has_above = position < lax.axis_size("body") - 1
    layer_index = lax.broadcasted_iota(jnp.int32, load.shape, 0)
    lateral = (("gx", 0), ("gy", 1))

    def apply_a(vector):
        padded = with_halo(vector, (("gx", 1), ("gy", 2)), 1)
        stacked = jnp.pad(vector, ((1, 1), (0, 0), (0, 0)))
        beside_it = stacked[2:] + stacked[:-2] + padded[:, 2:, 1:-1] + padded[:, :-2, 1:-1]
        beside_it = beside_it + padded[:, 1:-1, 2:] + padded[:, 1:-1, :-2]
        return (6.0 + stiffness) * vector - beside_it

    def body_sum(first, second):
        return lax.psum(jnp.sum(first * second), G)

    offsets = jnp.arange(SPAN * SPAN, dtype=jnp.int32)[:, None, None, None]
    tables = jnp.sum(jnp.where(pair_code[None] == offsets, pair_weight[None], 0.0), axis=1)
    tables_grown = with_halo(tables, (("gx", 1), ("gy", 2)), REACH)

    def update(_, state):
        solution, multiplier, interface_load = state
        residual = load + interface_load - apply_a(solution)

        def inner(_, state):
            solution, residual, direction, norm = state
            image = apply_a(direction)
            alpha = norm / body_sum(direction, image)
            solution = solution + alpha * direction
            residual = residual - alpha * image
            new = body_sum(residual, residual)
            return solution, residual, residual + (new / norm) * direction, new

        start = (solution, residual, residual, body_sum(residual, residual))
        solution = lax.fori_loop(0, ORDER, inner, start)[0]
        master = with_halo(solution[layers - 1], lateral, REACH)
        slave = passed_along(solution[0], "body", -1)

        def pull_one(offset, total):
            window = lax.dynamic_slice(master, (offset // SPAN, offset % SPAN), (rows, cols))
            return total + tables[offset] * window

        pulled = lax.fori_loop(0, SPAN * SPAN, pull_one, jnp.zeros((rows, cols), F32))
        multiplier = jnp.where(has_above, multiplier + RATE * (slave - pulled), 0.0)
        grown = with_halo(multiplier, lateral, REACH)

        def push_one(offset, total):
            at = (2 * REACH - offset // SPAN, 2 * REACH - offset % SPAN)
            return total + lax.dynamic_slice(tables_grown[offset] * grown, at, (rows, cols))

        force = lax.fori_loop(0, SPAN * SPAN, push_one, jnp.zeros((rows, cols), F32))
        lifted = passed_along(multiplier, "body", 1)
        interface_load = jnp.where(layer_index == layers - 1, force[None], 0.0)
        interface_load = interface_load + jnp.where(layer_index == 0, -lifted[None], 0.0)
        return solution, multiplier, interface_load

    state = (jnp.zeros_like(load), jnp.zeros((rows, cols), F32), jnp.zeros_like(load))
    solution, _, interface_load = lax.fori_loop(0, UPDATES, update, state)
    return solution, interface_load


def shaped(*shape):
    return jax.ShapeDtypeStruct(shape, F32)


def held(*shape, dtype=F32):
    return pltpu.VMEM(shape, dtype)


def kept(*shape):
    return pltpu.HBM(shape, F32)


def call(kernel, args, outs, scratch=(), aliases=None, hbm_args=()):
    vmem = pl.BlockSpec(memory_space=pltpu.VMEM)
    hbm = pl.BlockSpec(memory_space=pltpu.HBM)
    smem = pl.BlockSpec(memory_space=pltpu.SMEM)
    in_hbm = lambda out: getattr(out, "memory_space", None) == pltpu.HBM
    return pl.pallas_call(
        kernel,
        out_shape=tuple(outs),
        in_specs=[vmem] * len(args) + [hbm] * len(hbm_args),
        out_specs=tuple(hbm if in_hbm(out) else (smem if out.dtype == jnp.int32 and out.shape == (1, 1) else vmem) for out in outs),
        scratch_shapes=list(scratch),
        input_output_aliases=aliases or {},
        compiler_params=pltpu.CompilerParams(vmem_limit_bytes=8 * 1024 * 1024),
    )(*args, *[pltpu.with_memory_space_constraint(x, pltpu.HBM) for x in hbm_args])


def per_device(mesh, load, stiffness, pair_code, pair_weight):
    layers, rows, lanes = load.shape
    pairs = pair_code.shape[0]
    assert lanes == LANES and rows % 8 == 0 and rows >= 16 * ORDER + 8 and layers % 4 == 0
    plan = Plan(mesh, layers, rows, pairs)
    nb, nx, ny = plan.nb, plan.nx, plan.ny
    count = nb * nx * ny
    nf = len(plan.sb)
    buf = plan.buf
    bind = lambda kernel: functools.partial(kernel, plan)
    sems = lambda n: pltpu.SemaphoreType.DMA((n,))

    def lateral(row_kind, lane_kind, array):
        a, b = swap_perm(row_kind, nx), swap_perm(lane_kind, ny)
        aside = nb > 1 and nb % 2 == 0
        pairs = []
        for body in range(nb):
            for i, j in itertools.product(range(nx), range(ny)):
                wraps = abs(a[i][1] - i) > 1 or abs(b[j][1] - j) > 1
                here, there = (body, i, j), (body, a[i][1], b[j][1])
                if wraps and aside:
                    there = (body ^ 1, i, j)
                pairs.append(tuple((p * nx + q) * ny + r for p, q, r in (here, there)))
        return lax.ppermute(array, ALL, pairs)

    def across(kind, array):
        side = nx * ny
        pairs = []
        for b, to in swap_perm(kind, nb):
            for i in range(side):
                pairs.append((b * side + i, to * side + i) if abs(to - b) == 1 else (b * side + i, b * side + (i ^ 1)))
        return lax.ppermute(array, ALL, pairs)

    def spread(moments, faces):
        return lax.all_to_all(moments, ALL, 0, 0, tiled=True), [across(k, f) for k, f in zip(plan.sb, faces)]

    kinds = [(k, "") for k in plan.sx] + [("", k) for k in plan.sy] + [(a, b) for a in plan.sx for b in plan.sy]
    vec, stack = held(*plan.vec), held(2, layers, buf, LANES)
    face = shaped(ORDER + 1, plan.face, LANES)
    message = shaped(count, 1, LANES)
    mask = held(2, buf, LANES)
    pairing, tables = held(2, pairs, 2, buf, LANES), held(SPAN * SPAN, 2, buf, LANES)
    cells = (layers, rows, LANES)
    shifted = pltpu.VMEM((2, SPAN, 2, buf, LANES), F32)

    shapes = [shaped(plan.piece_rows, LANES) for _ in plan.sx]
    shapes += [shaped(plan.strip_tiles, rows, LANES) for _ in plan.sy]
    shapes += [shaped(plan.unit_tiles, 8, LANES) for _ in plan.sx for _ in plan.sy]
    b0, diag, codes, weights, *packed = call(
        bind(pack_kernel),
        (),
        [vec, stack, held(pairs, rows, LANES, dtype=jnp.int32), held(pairs, rows, LANES)] + shapes,
        [sems(4)],
        hbm_args=(load, stiffness, pair_code, pair_weight),
    )
    halos = []
    for (a, b), m in zip(kinds, packed):
        halos.append(lateral(a, b, m))
    b0, diag, pair, inside, table, b1, b2, *blank = call(
        bind(prepare_kernel),
        (b0, diag, codes, weights),
        [vec, stack, pairing, mask, tables] + [vec] * (2 + ORDER),
        aliases={0: 0, 1: 1},
    )
    nx_msgs, ny_msgs = len(plan.sx), len(plan.sy)
    row_halos, lane_halos, corner_halos = halos[:nx_msgs], halos[nx_msgs : nx_msgs + ny_msgs], halos[nx_msgs + ny_msgs :]
    b0, diag, pair, b1, b2, table, b3 = call(
        bind(inner_kernel),
        (*lane_halos, inside, b0, diag, pair, b1, b2, table),
        [vec, stack, pairing, vec, vec, tables, vec],
        aliases={ny_msgs + 1 + i: i for i in range(6)},
    )
    at = len(row_halos) + len(corner_halos) + 1
    moments, *rest = call(
        bind(krylov_kernel),
        (*row_halos, *corner_halos, inside, b0, diag, pair, b1, b2, table, b3),
        [message] + [face] * nf + [vec, stack, pairing, vec, vec, tables, vec],
        aliases={at + i: 1 + nf + i for i in range(7)},
    )
    faces, (b0, diag, _, b1, b2, table, b3) = rest[:nf], rest[nf:]
    moments, faces = spread(moments, faces)
    moments, *rest = call(
        bind(middle_kernel),
        (moments, *faces, b0, b1, b2, b3, diag, inside, table, *blank),
        [message] + [face] * nf + [vec] * 3 + [held(*cells), mask, held(buf, LANES), held(nb, LANES)],
        [shifted],
        {1 + nf + 7 + i: 1 + nf + i for i in range(ORDER)},
    )
    faces, kept_arrays = rest[:nf], rest[nf:]
    moments, faces = spread(moments, faces)
    found, lifted, again = call(
        bind(final_kernel),
        (moments, *faces, *kept_arrays, table),
        [kept(*cells)] * 2 + [jax.ShapeDtypeStruct((1, 1), jnp.int32)],
        [pltpu.VMEM(cells, F32), pltpu.VMEM(cells, F32), pltpu.VMEM((2, buf, LANES), F32), shifted, sems(5)],
    )

    def same(arrays, flag):
        vmem = pl.BlockSpec(memory_space=pltpu.VMEM)
        return pl.pallas_call(
copy_refs,
            out_shape=[jax.ShapeDtypeStruct(a.shape, a.dtype) for a in arrays],
            in_specs=[pl.BlockSpec(memory_space=pltpu.SMEM)] + [vmem] * len(arrays),
            out_specs=[vmem] * len(arrays),
            name="same",
        )(flag, *arrays)

    def redo(state):
        inputs = same((load, stiffness, pair_code, pair_weight), state[2])
        return (*same(step_by_step(*inputs), state[2]), jnp.zeros_like(state[2]))

    found, lifted, _ = lax.while_loop(lambda state: state[2][0, 0] > 0, redo, (found, lifted, again))
    return found, lifted


def solution(mesh):
    def whole(*args):
        return per_device(mesh, *args)

    step = jax.shard_map(
        whole,
        mesh=mesh,
        in_specs=(P("body", "gx", "gy"), P("body", "gx", "gy"), P(None, "gx", "gy"), P(None, "gx", "gy")),
        out_specs=(P("body", "gx", "gy"), P("body", "gx", "gy")),
        check_vma=False,
    )
    if "B" not in swaps_of(mesh.shape["gy"]) or not swaps_of(mesh.shape["gx"]):
        return step
    return step
```

```python
import functools
import itertools

import jax
import jax.numpy as jnp
from jax import lax
from jax.experimental import pallas as pl
from jax.experimental.pallas import tpu as pltpu
from jax.sharding import PartitionSpec as P


REACH = 2
SPAN = 2 * REACH + 1
RATE = 2.0
CENTRE = 7.5
LANES = 128
STRIP = 16
SLOTS = LANES // STRIP
PAD = 24
ORDER = 3
UNROLL = 16
CHUNK = 40
UPDATES = 2
STEADY = 0.05
F32 = jnp.float32
G = ("gx", "gy")
ALL = ("body", "gx", "gy")


def swaps_of(count):
    return () if count < 2 else (("A",) if count == 2 else ("A", "B"))


def swap_perm(kind, count):
    if kind == "":
        return [(i, i) for i in range(count)]
    step = 1 if kind == "A" else -1
    return [(i, (i + (step if i % 2 == 0 else -step)) % count) for i in range(count)]


def swap_up(kind, index):
    even = lax.rem(index, 2) == 0
    return even if kind == "A" else jnp.logical_not(even)


def swap_valid(kind, index, count):
    if kind == "A":
        return index >= 0
    return jnp.where(swap_up(kind, index), index < count - 1, index > 0)


def row_units(layers, pairs):
    wide_load = (0, 1, layers - 3, layers - 2, layers - 1)
    wide_stiff = (0, layers - 3, layers - 2, layers - 1)
    units = []
    for which, wide in ((0, wide_load), (1, wide_stiff)):
        for layer in range(layers):
            units.append((which, layer, False))
            if layer in wide:
                units.append((which, layer, True))
    for which in (2, 3):
        units += [(which, k, False) for k in range(pairs)]
    return units


def row_pieces(layers, pairs):
    top = layers - 1
    load = {top: 12, top - 1: 11, top - 2: 10, 0: 10, 1: 9, 2: 8}
    stiff = {top: 11, top - 1: 10, top - 2: 6, 0: 9, 1: 8}
    pieces = [(0, k, load.get(k, 6)) for k in range(layers)] + [(1, k, stiff.get(k, 5)) for k in range(layers)]
    pieces += [(which, k, 8) for which in (2, 3) for k in range(pairs)]
    placed, at = [], 0
    for which, k, size in pieces:
        placed.append((which, k, size, at))
        at += size
    return placed


def strip_list(layers, pairs):
    return [(w, k) for w in (0, 1) for k in range(layers)] + [(w, k) for w in (2, 3) for k in range(pairs)]


def lane_iota(rows):
    return lax.broadcasted_iota(jnp.int32, (rows, LANES), 1)


def aligned(start):
    return pl.multiple_of(start, 8)


def chunks(first, size, step):
    return [(at, min(step, first + size - at)) for at in range(first, first + size, step)]


class Plan:
    def __init__(self, mesh, layers, rows, pairs):
        self.nb, self.nx, self.ny = (mesh.shape[a] for a in ALL)
        self.layers, self.rows, self.pairs = layers, rows, pairs
        self.buf = rows + 2 * PAD
        self.units = row_units(layers, pairs)
        self.strips = strip_list(layers, pairs)
        self.pieces = row_pieces(layers, pairs)
        self.piece_rows = -(-(self.pieces[-1][2] + self.pieces[-1][3]) // 8) * 8
        self.sx, self.sy, self.sb = swaps_of(self.nx), swaps_of(self.ny), swaps_of(self.nb)
        self.face = rows + 16
        self.vec = (2, layers + 2, self.buf, LANES)
        self.own = pl.ds(PAD, rows)
        self.near = pl.ds(PAD - 8, self.face)
        self.unit_tiles = -(-len(self.units) // SLOTS)
        self.strip_tiles = -(-len(self.strips) // SLOTS)


class Args:
    def __init__(self, refs):
        self.refs = list(refs)

    def take(self, count):
        got, self.refs = self.refs[:count], self.refs[count:]
        return got

    def one(self):
        return self.refs.pop(0)


def pack_kernel(plan, load, stiff, code, weight, *refs):
    args = Args(refs)
    b0, diag, codes, weights = args.take(4)
    row_out, lane_out = args.take(len(plan.sx)), args.take(len(plan.sy))
    corner_out = args.take(len(plan.sx) * len(plan.sy))
    sems = args.one()
    ix, iy = lax.axis_index("gx"), lax.axis_index("gy")
    rows, layers = plan.rows, plan.layers
    places = (b0.at[0, pl.ds(1, layers), plan.own, :], diag.at[0, :, plan.own, :], codes, weights)
    copies = [
        pltpu.make_async_copy(src, dst, sems.at[i]) for i, (src, dst) in enumerate(zip((load, stiff, code, weight), places))
    ]
    for copy in copies:
        copy.start()
    arrived = set()

    def take(which, k, start, size):
        if which not in arrived:
            copies[which].wait()
            arrived.add(which)
        if which == 0:
            return b0[0, k + 1, pl.ds(PAD + start, size), :]
        if which == 1:
            return diag[0, k, pl.ds(PAD + start, size), :]
        return (codes, weights)[which - 2][k, pl.ds(start, size), :].astype(F32)

    def starts(kind):
        up = swap_up(kind, ix)
        return aligned(jnp.where(up, rows - 8, 0)), aligned(jnp.where(up, rows - 16, 8))

    def gather(pieces, size, tile, outs):
        slot_of = lane_iota(size) // STRIP
        last, first = jnp.zeros((size, LANES), F32), jnp.zeros((size, LANES), F32)
        for slot, value in enumerate(pieces):
            moved = pltpu.roll(value, STRIP * (slot + 1) % LANES, 1) if slot + 1 < SLOTS else value
            last = jnp.where(slot_of == slot, moved, last)
            first = jnp.where(slot_of == (slot + 1) % SLOTS, moved, first)
        for kind, out in zip(plan.sy, outs):
            out[tile] = jnp.where(swap_up(kind, iy), last, first)

    for kind, out in zip(plan.sx, row_out):
        up = swap_up(kind, ix)
        for which, k, size, at in plan.pieces:
            out[pl.ds(at, size), :] = jnp.where(up, take(which, k, rows - size, size), take(which, k, 0, size))
        used = plan.pieces[-1][2] + plan.pieces[-1][3]
        if used < plan.piece_rows:
            out[pl.ds(used, plan.piece_rows - used), :] = jnp.zeros((plan.piece_rows - used, LANES), F32)
    for tile in range(plan.strip_tiles):
        members = plan.strips[tile * SLOTS : (tile + 1) * SLOTS]
        gather([take(which, k, 0, rows) for which, k in members], rows, tile, lane_out)
    for i, row_kind in enumerate(plan.sx):
        near, far = starts(row_kind)
        outs = corner_out[i * len(plan.sy) : (i + 1) * len(plan.sy)]
        for tile in range(plan.unit_tiles):
            members = plan.units[tile * SLOTS : (tile + 1) * SLOTS]
            gather([take(which, k, far if is_far else near, 8) for which, k, is_far in members], 8, tile, outs)


def clear_frame(plan, vec):
    zero = jnp.zeros((16, LANES), F32)
    for t in (0, 1):
        for edge in (0, plan.layers + 1):
            vec[t, edge] = jnp.zeros((plan.buf, LANES), F32)
        for layer in range(1, plan.layers + 1):
            vec[t, layer, pl.ds(0, 16), :] = zero
            vec[t, layer, pl.ds(plan.buf - 16, 16), :] = zero


def table_rows(plan, pairing, tables, t, first, size):
    span = pl.ds(first, size)
    codes = [pairing[0, k, t, span, :] for k in range(plan.pairs)]
    weights = [pairing[1, k, t, span, :] for k in range(plan.pairs)]
    for offset in range(SPAN * SPAN):
        total = jnp.where(codes[0] == offset, weights[0], 0.0)
        for k in range(1, plan.pairs):
            total = total + jnp.where(codes[k] == offset, weights[k], 0.0)
        tables[offset, t, span, :] = total


def prepare_kernel(plan, b0_in, diag_in, codes, weights, b0, diag, pairing, inside, tables, *vecs):
    del b0_in, diag_in
    ix, iy = lax.axis_index("gx"), lax.axis_index("gy")
    rows, layers, buf = plan.rows, plan.layers, plan.buf
    row = lax.broadcasted_iota(jnp.int32, (buf, LANES), 0) + ix * rows - PAD
    lane = lane_iota(buf)
    in_rows = jnp.logical_and(row >= 0, row < plan.nx * rows)
    right = jnp.logical_and(lane < STRIP, iy < plan.ny - 1)
    left = jnp.logical_and(lane >= LANES - STRIP, iy > 0)
    inside[0] = jnp.where(in_rows, 1.0, 0.0)
    inside[1] = jnp.where(jnp.logical_and(in_rows, jnp.logical_or(right, left)), 1.0, 0.0)
    zero = jnp.zeros((PAD, LANES), F32)
    for t in (0, 1):
        for span in (pl.ds(0, PAD), pl.ds(buf - PAD, PAD)):
            for layer in range(layers):
                b0[t, layer + 1, span, :] = zero
                diag[t, layer, span, :] = zero
            for k in range(plan.pairs):
                for i in (0, 1):
                    pairing[i, k, t, span, :] = zero
        for edge in (0, layers + 1):
            b0[t, edge] = jnp.zeros((buf, LANES), F32)
        for offset in range(SPAN * SPAN):
            tables[offset, t, pl.ds(PAD - 16, 8), :] = jnp.zeros((8, LANES), F32)
            tables[offset, t, pl.ds(PAD + rows + 8, 8), :] = jnp.zeros((8, LANES), F32)
    for vec in vecs:
        clear_frame(plan, vec)
    for layer in range(layers):
        diag[0, layer, plan.own, :] = diag[0, layer, plan.own, :] + (6.0 - CENTRE)
    for k in range(plan.pairs):
        pairing[0, k, 0, plan.own, :] = codes[k].astype(F32)
        pairing[1, k, 0, plan.own, :] = weights[k]
    for first, size in chunks(PAD, rows, 32):
        table_rows(plan, pairing, tables, 0, first, size)


def operate(src, at, diag, layer, inside, first, size, tiles=(0, 1), masked=True):
    lane = lane_iota(size)
    start, end = lane == 0, lane == LANES - 1
    rows = pl.ds(first, size)
    middle = [src[t, at, rows, :] for t in (0, 1)]
    before = [pltpu.roll(m, 1, 1) for m in middle]
    after = [pltpu.roll(m, LANES - 1, 1) for m in middle]
    done = []
    for t in tiles:
        total = jnp.where(start, before[1 - t], before[t]) + jnp.where(end, after[1 - t], after[t])
        total = total + src[t, at, pl.ds(first - 1, size), :]
        total = total + src[t, at, pl.ds(first + 1, size), :]
        total = total + (src[t, at - 1, rows, :] + src[t, at + 1, rows, :])
        if masked or t == 1:
            total = total * inside[t, rows, :]
        done.append(diag[t, layer, rows, :] * middle[t] - total)
    return done


def apply_rows(src, dst, at, diag, layer, inside, parts):
    values = [operate(src, at, diag, layer, inside, first, size, masked=masked) for first, size, masked in parts]
    for (first, size, _), pair in zip(parts, values):
        for t in (0, 1):
            dst[t, at, pl.ds(first, size), :] = pair[t]
    return [pair[0] for pair in values]


def apply_joined(src, dst, at, diag, layer, inside, parts):
    spans = [pl.ds(first, size) for first, size, _ in parts]
    size = sum(p[1] for p in parts)
    lane = lane_iota(size)
    start, end = lane == 0, lane == LANES - 1
    join = lambda values: values[0] if len(values) == 1 else jnp.concatenate(values, axis=0)
    middle = [join([src[t, at, span, :] for span in spans]) for t in (0, 1)]
    before = [pltpu.roll(m, 1, 1) for m in middle]
    after = [pltpu.roll(m, LANES - 1, 1) for m in middle]
    done = []
    for t in (0, 1):
        sides = jnp.where(start, before[1 - t], before[t]) + jnp.where(end, after[1 - t], after[t])
        values, low = [], 0
        for (first, rows, masked), span in zip(parts, spans):
            total = sides[low : low + rows]
            total = total + src[t, at, pl.ds(first - 1, rows), :]
            total = total + src[t, at, pl.ds(first + 1, rows), :]
            total = total + (src[t, at - 1, span, :] + src[t, at + 1, span, :])
            if masked or t == 1:
                total = total * inside[t, span, :]
            values.append(diag[t, layer, span, :] * middle[t][low : low + rows] - total)
            low += rows
        done.append(values)
    for i, span in enumerate(spans):
        for t in (0, 1):
            dst[t, at, span, :] = done[t][i]
    return done[0]


def near_rows(plan):
    outer = [(PAD - 8, 8, True), (PAD + plan.rows, 8, True)]
    return outer + [(first, size, False) for first, size in chunks(PAD, plan.rows, 32)]


def inner_rows(plan, step):
    return [(first, size, False) for first, size in chunks(PAD + 8 * step, plan.rows - 16 * step, 32)]


def outer_rows(plan, step):
    wide = 8 * step
    outer = [(PAD - 8, 8, True), (PAD + plan.rows, 8, True)]
    return outer + [(PAD, wide, False), (PAD + plan.rows - wide, wide, False)]


def apply_all(plan, src, dst, diag, inside, parts, apply=apply_rows):
    def one(layer, carry):
        apply(src, dst, layer + 1, diag, layer, inside, parts)
        return carry

    lax.fori_loop(0, plan.layers, one, 0, unroll=min(UNROLL, plan.layers))


def apply_own(plan, src, at, diag, layer, inside):
    parts = [
        operate(src, at, diag, layer, inside, first, size, (0,), False)[0] for first, size in chunks(PAD, plan.rows, 32)
    ]
    return jnp.concatenate(parts, axis=0)


def six_sums(parts):
    lane = lax.broadcasted_iota(jnp.int32, (1, LANES), 1)
    row = jnp.zeros((1, LANES), F32)
    for k, part in enumerate(parts):
        row = jnp.where(lane == k, jnp.sum(part), row)
    return row


def fold(value):
    return jnp.sum(value.reshape(-1, 8, LANES), axis=0)


def add_products(sums, v):
    pairs = ((v[0], v[0]), (v[0], v[1]), (v[1], v[1]), (v[1], v[2]), (v[2], v[2]), (v[2], v[3]))
    return tuple(s + fold(a * b) for s, (a, b) in zip(sums, pairs))


def put_moments(moments, sums):
    moments[...] = jnp.broadcast_to(six_sums(sums).reshape(1, 1, LANES), moments.shape)


def no_sums():
    return (jnp.zeros((8, LANES), F32),) * 6


def put_cells(arrays, which, k, t, where, value):
    b0, diag, pairing = arrays
    if which == 0:
        b0[t, k + 1, where, :] = value
    elif which == 1:
        diag[t, k, where, :] = value + (6.0 - CENTRE)
    else:
        pairing[which - 2, k, t, where, :] = value


def unpack(plan, msgs, tile, size):
    iy = lax.axis_index("gy")
    sides = []
    for right in (True, False):
        total = jnp.zeros((size, LANES), F32)
        for kind, msg in zip(plan.sy, msgs):
            use = jnp.logical_and(swap_up(kind, iy) == right, swap_valid(kind, iy, plan.ny))
            total = jnp.where(use, msg[tile], total)
        sides.append(total)
    even = lax.rem(lane_iota(size) // STRIP, 2) == 0
    return jnp.where(even, sides[1], sides[0]), jnp.where(even, sides[0], sides[1])


def piece(both, slot):
    turn = STRIP * (SLOTS - 1 - slot)
    return pltpu.roll(both[slot % 2], turn, 1) if turn else both[slot % 2]


def inner_kernel(plan, *refs):
    args = Args(refs)
    msgs = args.take(len(plan.sy))
    inside, _, _, _, _, _, _ = args.take(7)
    b0, diag, pairing, b1, b2, tables, b3 = args.take(7)
    for tile in range(plan.strip_tiles):
        both = unpack(plan, msgs, tile, plan.rows)
        for slot, (which, k) in enumerate(plan.strips[tile * SLOTS : (tile + 1) * SLOTS]):
            put_cells((b0, diag, pairing), which, k, 1, plan.own, piece(both, slot))
    for step, (src, dst) in enumerate(((b0, b1), (b1, b2), (b2, b3))):
        apply_all(plan, src, dst, diag, inside, inner_rows(plan, step + 1))
    for first, size in chunks(PAD, plan.rows, 32):
        table_rows(plan, pairing, tables, 1, first, size)


def krylov_kernel(plan, *refs):
    args = Args(refs)
    row_msgs = args.take(len(plan.sx))
    corner_msgs = args.take(len(plan.sx) * len(plan.sy))
    inside = args.one()
    args.take(7)
    moments, = args.take(1)
    faces = args.take(len(plan.sb))
    b0, diag, pairing, b1, b2, tables, b3 = args.take(7)
    ix = lax.axis_index("gx")
    rows, layers = plan.rows, plan.layers
    arrays = (b0, diag, pairing)

    def spots(kind):
        up = swap_up(kind, ix)
        near = aligned(jnp.where(up, PAD + rows, PAD - 8))
        far = aligned(jnp.where(up, PAD + rows + 8, PAD - 16))
        return near, far, swap_valid(kind, ix, plan.nx)

    for kind, msg in zip(plan.sx, row_msgs):
        up, ok = swap_up(kind, ix), swap_valid(kind, ix, plan.nx)

        @pl.when(jnp.logical_and(up, ok))
        def _():
            for which, k, size, at in plan.pieces:
                put_cells(arrays, which, k, 0, pl.ds(PAD + rows, size), msg[pl.ds(at, size), :])

        @pl.when(jnp.logical_and(jnp.logical_not(up), ok))
        def _():
            for which, k, size, at in plan.pieces:
                put_cells(arrays, which, k, 0, pl.ds(PAD - size, size), msg[pl.ds(at, size), :])

    for i, row_kind in enumerate(plan.sx):
        near, far, ok = spots(row_kind)
        for tile in range(plan.unit_tiles):
            both = unpack(plan, corner_msgs[i * len(plan.sy) : (i + 1) * len(plan.sy)], tile, 8)
            both = [jnp.where(ok, b, 0.0) for b in both]
            for slot, (which, k, is_far) in enumerate(plan.units[tile * SLOTS : (tile + 1) * SLOTS]):
                put_cells(arrays, which, k, 1, pl.ds(far if is_far else near, 8), piece(both, slot))

    for step, (src, dst, wide) in enumerate(((b0, b1, (0, layers - 2, layers - 1)), (b1, b2, (layers - 1,)))):
        apply_all(plan, src, dst, diag, inside, outer_rows(plan, step + 1), apply_joined)
        for layer in wide:
            for first in (PAD - 16, PAD + rows + 8):
                for t, value in enumerate(operate(src, layer + 1, diag, layer, inside, first, 8)):
                    dst[t, layer + 1, pl.ds(first, 8), :] = value

    middle = pl.ds(PAD + 8 * ORDER, rows - 16 * ORDER)

    def one(layer, sums):
        ends = apply_joined(b2, b3, layer + 1, diag, layer, inside, outer_rows(plan, ORDER))[2:]
        last = jnp.concatenate([ends[0], b3[0, layer + 1, middle, :], ends[1]], axis=0)
        return add_products(sums, [v[0, layer + 1, plan.own, :] for v in (b0, b1, b2)] + [last])

    put_moments(moments, lax.fori_loop(0, layers, one, no_sums(), unroll=min(UNROLL, plan.layers)))

    for t in (0, 1):
        for first in (PAD - 8, PAD + rows):
            table_rows(plan, pairing, tables, t, first, 8)
    vecs = (b0, b1, b2)
    put_faces(plan, lambda k, t: vecs[k][t, layers, plan.near, :], lambda k, t: vecs[k][t, 1, plan.near, :], faces)


def lane_shift(first, second, by, lane):
    if by == 0:
        return first, second
    a, b = pltpu.roll(first, (-by) % LANES, 1), pltpu.roll(second, (-by) % LANES, 1)
    keep = lane < LANES - by if by > 0 else lane >= -by
    return jnp.where(keep, a, b), jnp.where(keep, b, a)


def put_shifted(shifted, n, first, size, planes):
    lane = lane_iota(size)
    for i in range(SPAN):
        for t, value in enumerate(lane_shift(planes[0], planes[1], i - REACH, lane)):
            shifted[n, i, t, pl.ds(first, size), :] = value


def pull(tables, shifted, count, t, first, size):
    total = [jnp.zeros((size, LANES), F32)] * count
    for offset in range(SPAN * SPAN):
        table = tables[offset, t, pl.ds(first, size), :]
        window = pl.ds(first + offset // SPAN - REACH, size)
        for n in range(count):
            total[n] = total[n] + table * shifted[n, offset % SPAN, t, window, :]
    return total


def push(tables, face, first, size, tiles=(0, 1)):
    lane = lane_iota(size)
    total = [jnp.zeros((size, LANES), F32)] * 2
    for i in range(SPAN):
        column = [jnp.zeros((size, LANES), F32)] * 2
        for j in range(SPAN):
            window = pl.ds(first - (j - REACH), size)
            for t in (0, 1):
                column[t] = column[t] + tables[j * SPAN + i, t, window, :] * face[t, window, :]
        moved = lane_shift(column[0], column[1], REACH - i, lane)
        total = [total[t] + moved[t] for t in (0, 1)]
    return [total[t] for t in tiles]


def put_faces(plan, tops, bottoms, outs):
    ib = lax.axis_index("body")
    lane = lane_iota(plan.face)
    for kind, out in zip(plan.sb, outs):
        up = swap_up(kind, ib)
        packed = jnp.zeros((plan.face, LANES), F32)
        for k in range(ORDER):
            out[k] = jnp.where(up, tops(k, 0), bottoms(k, 0))
            strips = pltpu.roll(jnp.where(up, tops(k, 1), bottoms(k, 1)), STRIP + 2 * STRIP * k, 1)
            packed = jnp.where(lane // (2 * STRIP) == k, strips, packed)
        out[ORDER] = packed


def get_face(plan, msgs, coef, up, low, size, tiles=(0, 1)):
    ib = lax.axis_index("body")
    total = [jnp.zeros((size, LANES), F32)] * 2
    for kind, msg in zip(plan.sb, msgs):
        use = jnp.logical_and(swap_up(kind, ib) == up, swap_valid(kind, ib, plan.nb))
        rows = pl.ds(low, size)
        for t in tiles:
            if t == 0:
                value = sum(coef[k] * msg[k, rows, :] for k in range(ORDER))
            else:
                strips = msg[ORDER, rows, :]
                value = sum(
                    coef[k] * pltpu.roll(strips, (LANES - STRIP - 2 * STRIP * k) % LANES, 1) for k in range(ORDER)
                )
            total[t] = jnp.where(use, value, total[t])
    return [total[t] for t in tiles]


def solve(plan, moments):
    per = plan.nx * plan.ny
    body = lax.broadcasted_iota(jnp.int32, (plan.nb, LANES), 0)
    table = jnp.zeros((plan.nb, LANES), F32)
    for b in range(plan.nb):
        row = [moments[b * per + i] for i in range(per)]
        while len(row) > 1:
            row = [x + y for x, y in zip(row[::2], row[1::2])] + row[len(row) // 2 * 2 :]
        table = jnp.where(body == b, row[0], table)
    lane = lax.broadcasted_iota(jnp.int32, (plan.nb, LANES), 1)
    m = [
        jnp.broadcast_to(jnp.sum(jnp.where(lane == k, table, 0.0), axis=1, keepdims=True), table.shape)
        for k in range(6)
    ]
    h = [m[n + 1] + CENTRE * m[n] for n in range(5)]
    f1, f2 = h[1] / h[0], h[2] / h[0]
    d1 = h[2] - f1 * h[1]
    e = h[3] - f1 * h[2]
    f3 = e / d1
    d2 = h[4] - f2 * h[2] - f3 * e
    g1 = m[1] - f1 * m[0]
    g2 = m[2] - f2 * m[0] - f3 * g1
    c2 = g2 / d2
    c1 = (g1 - e * c2) / d1
    c0 = (m[0] - h[1] * c1 - h[2] * c2) / h[0]

    steady = jnp.minimum(d1 / h[2], d2 / h[4])

    def pick(index):
        return [jnp.sum(jnp.where(body == index, c, 0.0), axis=0, keepdims=True) for c in (c0, c1, c2)]

    ib = lax.axis_index("body")
    return pick(ib), pick(ib + 1), pick(ib - 1), jnp.where(steady > STEADY, 0.0, 1.0)


def residual_coefs(c):
    return 1.0 - CENTRE * c[0], -(c[0] + CENTRE * c[1]), -(c[1] + CENTRE * c[2]), -c[2]


def middle_kernel(plan, moments_in, *refs):
    args = Args(refs)
    msgs = args.take(len(plan.sb))
    basis = args.take(4)
    diag, inside, tables = args.take(3)
    args.take(ORDER)
    moments, = args.take(1)
    faces = args.take(len(plan.sb))
    vecs = args.take(3)
    base, above_lambda, below_lambda, doubt, shifted = args.take(5)
    ib = lax.axis_index("body")
    rows, layers = plan.rows, plan.layers
    has_above, has_below = ib < plan.nb - 1, ib > 0
    c, above_c, below_c, doubt[...] = solve(plan, moments_in)
    d = residual_coefs(c)
    near, own = plan.near, plan.own

    def combine(layer, carry):
        for first, size in chunks(PAD - 8, plan.face, 40):
            for t in (0, 1):
                span = pl.ds(first, size)
                vecs[0][t, layer + 1, span, :] = sum(x * v[t, layer + 1, span, :] for x, v in zip(d, basis))
        base[layer] = sum(x * v[0, layer + 1, own, :] for x, v in zip(c, basis))
        return carry

    lax.fori_loop(0, layers, combine, 0, unroll=min(UNROLL, layers))

    zero = jnp.zeros((8, LANES), F32)
    for first, size in chunks(PAD - 16, plan.face + 16, 32):
        span = pl.ds(first, size)
        top = [sum(x * v[t, layers, span, :] for x, v in zip(c, basis)) for t in (0, 1)]
        put_shifted(shifted, 0, first, size, top)
    for t in (0, 1):
        for i in range(SPAN):
            shifted[1, i, t, pl.ds(PAD - 16, 8), :] = zero
            shifted[1, i, t, pl.ds(PAD + rows + 8, 8), :] = zero
    for first, size in chunks(PAD - 8, plan.face, CHUNK):
        low = first - PAD + 8
        put_shifted(shifted, 1, first, size, get_face(plan, msgs, below_c, False, low, size))
        for t, value in enumerate(get_face(plan, msgs, above_c, True, low, size)):
            above_lambda[t, pl.ds(first, size), :] = value
    for t in (0, 1):
        above_lambda[t, pl.ds(PAD - 16, 8), :] = zero
        above_lambda[t, pl.ds(PAD + rows + 8, 8), :] = zero
        for first, size in chunks(PAD - 8, plan.face, CHUNK):
            span = pl.ds(first, size)
            pulled, master = pull(tables, shifted, 2, t, first, size)
            above_lambda[t, span, :] = jnp.where(has_above, RATE * (above_lambda[t, span, :] - pulled), 0.0)
            gap = sum(x * basis[k][t, 1, span, :] for k, x in enumerate(c)) - master
            gap = jnp.where(has_below, RATE * gap, 0.0)
            if t == 0:
                below_lambda[span, :] = gap
            vecs[0][t, 1, span, :] = vecs[0][t, 1, span, :] - gap
    for first, size in chunks(PAD - 8, plan.face, CHUNK):
        span = pl.ds(first, size)
        for t, value in enumerate(push(tables, above_lambda, first, size)):
            vecs[0][t, layers, span, :] = vecs[0][t, layers, span, :] + value * inside[t, span, :]

    for step in range(2):
        apply_all(plan, vecs[step], vecs[step + 1], diag, inside, near_rows(plan))

    def one(layer, sums):
        last = apply_own(plan, vecs[2], layer + 1, diag, layer, inside)
        return add_products(sums, [v[0, layer + 1, own, :] for v in vecs] + [last])

    put_moments(moments, lax.fori_loop(0, layers, one, no_sums(), unroll=min(UNROLL, plan.layers)))

    put_faces(plan, lambda k, t: vecs[k][t, layers, near, :], lambda k, t: vecs[k][t, 1, near, :], faces)


def final_kernel(plan, moments_in, *refs):
    args = Args(refs)
    msgs = args.take(len(plan.sb))
    vecs = args.take(3)
    base, above_lambda, below_lambda, doubt, tables = args.take(5)
    solution_out, interface_out, again, solution, interface, lifted, shifted, sems = args.take(8)
    ib = lax.axis_index("body")
    rows, layers = plan.rows, plan.layers
    has_above, has_below = ib < plan.nb - 1, ib > 0
    inner = pl.ds(1, layers - 2)
    copies = [pltpu.make_async_copy(interface.at[inner], interface_out.at[inner], sems.at[0])]
    for layer in range(1, layers - 1):
        interface[layer] = jnp.zeros((rows, LANES), F32)
    copies[0].start()
    c, above_c, below_c, doubt_now = solve(plan, moments_in)
    again[0, 0] = jnp.where(jnp.max(jnp.maximum(doubt[...], doubt_now)) > 0.5, 1, 0)
    own = plan.own
    half = layers // 2
    for i, (low, high) in enumerate(((0, half), (half, layers))):

        def combine(layer, carry):
            solution[layer] = base[layer] + sum(x * v[0, layer + 1, own, :] for x, v in zip(c, vecs))
            return carry

        lax.fori_loop(low, high, combine, 0, unroll=min(UNROLL, half))
        part = pl.ds(low, high - low)
        copies.append(pltpu.make_async_copy(solution.at[part], solution_out.at[part], sems.at[1 + i]))
        copies[-1].start()

    zero = jnp.zeros((8, LANES), F32)
    for n in (0, 1):
        for t in (0, 1):
            for i in range(SPAN):
                shifted[n, i, t, pl.ds(PAD - 16, 8), :] = zero
                shifted[n, i, t, pl.ds(PAD + rows + 8, 8), :] = zero
    for first, size in chunks(PAD - 8, plan.face, CHUNK):
        span = pl.ds(first, size)
        low = first - PAD + 8
        put_shifted(shifted, 0, first, size, get_face(plan, msgs, below_c, False, low, size))
        put_shifted(shifted, 1, first, size, [sum(x * v[t, layers, span, :] for x, v in zip(c, vecs)) for t in (0, 1)])
        for t, value in enumerate(get_face(plan, msgs, above_c, True, low, size)):
            lifted[t, span, :] = value
    master = pull(tables, shifted, 1, 0, PAD, rows)[0]
    gap = sum(x * v[0, 1, own, :] for x, v in zip(c, vecs)) - master
    interface[0] = -(2.0 * below_lambda[own, :] + jnp.where(has_below, RATE * gap, 0.0))
    copies.append(pltpu.make_async_copy(interface.at[0], interface_out.at[0], sems.at[3]))
    copies[-1].start()
    for t in (0, 1):
        lifted[t, pl.ds(PAD - 16, 8), :] = zero
        lifted[t, pl.ds(PAD + rows + 8, 8), :] = zero
        for first, size in chunks(PAD - 8, plan.face, CHUNK):
            span = pl.ds(first, size)
            gap = lifted[t, span, :] - pull(tables, shifted.at[pl.ds(1, 1)], 1, t, first, size)[0]
            lifted[t, span, :] = 2.0 * above_lambda[t, span, :] + jnp.where(has_above, RATE * gap, 0.0)
    for first, size in chunks(PAD, rows, CHUNK):
        interface[layers - 1, pl.ds(first - PAD, size), :] = push(tables, lifted, first, size, (0,))[0]
    copies.append(pltpu.make_async_copy(interface.at[layers - 1], interface_out.at[layers - 1], sems.at[4]))
    copies[-1].start()
    for copy in copies:
        copy.wait()


def with_halo(cells, sides, width):
    for axis, dim in sides:
        count = lax.axis_size(axis)
        head = lax.slice_in_dim(cells, 0, width, axis=dim)
        tail = lax.slice_in_dim(cells, cells.shape[dim] - width, cells.shape[dim], axis=dim)
        left = lax.ppermute(tail, axis, [(i, i + 1) for i in range(count - 1)])
        right = lax.ppermute(head, axis, [(i + 1, i) for i in range(count - 1)])
        cells = jnp.concatenate([left, cells, right], axis=dim)
    return cells


def passed_along(array, axis, by):
    count = lax.axis_size(axis)
    return lax.ppermute(array, axis, [(i, i + by) for i in range(count) if 0 <= i + by < count])


def copy_refs(flag, *refs):
    del flag
    half = len(refs) // 2
    for src, dst in zip(refs[:half], refs[half:]):
        dst[...] = src[...]


def step_by_step(load, stiffness, pair_code, pair_weight):
    layers, rows, cols = load.shape
    position = lax.axis_index("body")
    has_above = position < lax.axis_size("body") - 1
    layer_index = lax.broadcasted_iota(jnp.int32, load.shape, 0)
    lateral = (("gx", 0), ("gy", 1))

    def apply_a(vector):
        padded = with_halo(vector, (("gx", 1), ("gy", 2)), 1)
        stacked = jnp.pad(vector, ((1, 1), (0, 0), (0, 0)))
        beside_it = stacked[2:] + stacked[:-2] + padded[:, 2:, 1:-1] + padded[:, :-2, 1:-1]
        beside_it = beside_it + padded[:, 1:-1, 2:] + padded[:, 1:-1, :-2]
        return (6.0 + stiffness) * vector - beside_it

    def body_sum(first, second):
        return lax.psum(jnp.sum(first * second), G)

    offsets = jnp.arange(SPAN * SPAN, dtype=jnp.int32)[:, None, None, None]
    tables = jnp.sum(jnp.where(pair_code[None] == offsets, pair_weight[None], 0.0), axis=1)
    tables_grown = with_halo(tables, (("gx", 1), ("gy", 2)), REACH)

    def update(_, state):
        solution, multiplier, interface_load = state
        residual = load + interface_load - apply_a(solution)

        def inner(_, state):
            solution, residual, direction, norm = state
            image = apply_a(direction)
            alpha = norm / body_sum(direction, image)
            solution = solution + alpha * direction
            residual = residual - alpha * image
            new = body_sum(residual, residual)
            return solution, residual, residual + (new / norm) * direction, new

        start = (solution, residual, residual, body_sum(residual, residual))
        solution = lax.fori_loop(0, ORDER, inner, start)[0]
        master = with_halo(solution[layers - 1], lateral, REACH)
        slave = passed_along(solution[0], "body", -1)

        def pull_one(offset, total):
            window = lax.dynamic_slice(master, (offset // SPAN, offset % SPAN), (rows, cols))
            return total + tables[offset] * window

        pulled = lax.fori_loop(0, SPAN * SPAN, pull_one, jnp.zeros((rows, cols), F32))
        multiplier = jnp.where(has_above, multiplier + RATE * (slave - pulled), 0.0)
        grown = with_halo(multiplier, lateral, REACH)

        def push_one(offset, total):
            at = (2 * REACH - offset // SPAN, 2 * REACH - offset % SPAN)
            return total + lax.dynamic_slice(tables_grown[offset] * grown, at, (rows, cols))

        force = lax.fori_loop(0, SPAN * SPAN, push_one, jnp.zeros((rows, cols), F32))
        lifted = passed_along(multiplier, "body", 1)
        interface_load = jnp.where(layer_index == layers - 1, force[None], 0.0)
        interface_load = interface_load + jnp.where(layer_index == 0, -lifted[None], 0.0)
        return solution, multiplier, interface_load

    state = (jnp.zeros_like(load), jnp.zeros((rows, cols), F32), jnp.zeros_like(load))
    solution, _, interface_load = lax.fori_loop(0, UPDATES, update, state)
    return solution, interface_load


def shaped(*shape):
    return jax.ShapeDtypeStruct(shape, F32)


def held(*shape, dtype=F32):
    return pltpu.VMEM(shape, dtype)


def kept(*shape):
    return pltpu.HBM(shape, F32)


def call(kernel, args, outs, scratch=(), aliases=None, hbm_args=()):
    vmem = pl.BlockSpec(memory_space=pltpu.VMEM)
    hbm = pl.BlockSpec(memory_space=pltpu.HBM)
    smem = pl.BlockSpec(memory_space=pltpu.SMEM)
    in_hbm = lambda out: getattr(out, "memory_space", None) == pltpu.HBM
    return pl.pallas_call(
        kernel,
        out_shape=tuple(outs),
        in_specs=[vmem] * len(args) + [hbm] * len(hbm_args),
        out_specs=tuple(hbm if in_hbm(out) else (smem if out.dtype == jnp.int32 and out.shape == (1, 1) else vmem) for out in outs),
        scratch_shapes=list(scratch),
        input_output_aliases=aliases or {},
        compiler_params=pltpu.CompilerParams(vmem_limit_bytes=8 * 1024 * 1024),
    )(*args, *[pltpu.with_memory_space_constraint(x, pltpu.HBM) for x in hbm_args])


def per_device(mesh, load, stiffness, pair_code, pair_weight):
    layers, rows, lanes = load.shape
    pairs = pair_code.shape[0]
    assert lanes == LANES and rows % 8 == 0 and rows >= 16 * ORDER + 8 and layers % 4 == 0
    plan = Plan(mesh, layers, rows, pairs)
    nb, nx, ny = plan.nb, plan.nx, plan.ny
    count = nb * nx * ny
    nf = len(plan.sb)
    buf = plan.buf
    bind = lambda kernel: functools.partial(kernel, plan)
    sems = lambda n: pltpu.SemaphoreType.DMA((n,))

    def lateral(row_kind, lane_kind, array):
        a, b = swap_perm(row_kind, nx), swap_perm(lane_kind, ny)
        aside = nb > 1 and nb % 2 == 0
        pairs = []
        for body in range(nb):
            for i, j in itertools.product(range(nx), range(ny)):
                wraps = abs(a[i][1] - i) > 1 or abs(b[j][1] - j) > 1
                here, there = (body, i, j), (body, a[i][1], b[j][1])
                if wraps and aside:
                    there = (body ^ 1, i, j)
                pairs.append(tuple((p * nx + q) * ny + r for p, q, r in (here, there)))
        return lax.ppermute(array, ALL, pairs)

    def across(kind, array):
        side = nx * ny
        pairs = []
        for b, to in swap_perm(kind, nb):
            for i in range(side):
                pairs.append((b * side + i, to * side + i) if abs(to - b) == 1 else (b * side + i, b * side + (i ^ 1)))
        return lax.ppermute(array, ALL, pairs)

    def spread(moments, faces):
        return lax.all_to_all(moments, ALL, 0, 0, tiled=True), [across(k, f) for k, f in zip(plan.sb, faces)]

    kinds = [(k, "") for k in plan.sx] + [("", k) for k in plan.sy] + [(a, b) for a in plan.sx for b in plan.sy]
    vec, stack = held(*plan.vec), held(2, layers, buf, LANES)
    face = shaped(ORDER + 1, plan.face, LANES)
    message = shaped(count, 1, LANES)
    mask = held(2, buf, LANES)
    pairing, tables = held(2, pairs, 2, buf, LANES), held(SPAN * SPAN, 2, buf, LANES)
    cells = (layers, rows, LANES)
    shifted = pltpu.VMEM((2, SPAN, 2, buf, LANES), F32)

    shapes = [shaped(plan.piece_rows, LANES) for _ in plan.sx]
    shapes += [shaped(plan.strip_tiles, rows, LANES) for _ in plan.sy]
    shapes += [shaped(plan.unit_tiles, 8, LANES) for _ in plan.sx for _ in plan.sy]
    b0, diag, codes, weights, *packed = call(
        bind(pack_kernel),
        (),
        [vec, stack, held(pairs, rows, LANES, dtype=jnp.int32), held(pairs, rows, LANES)] + shapes,
        [sems(4)],
        hbm_args=(load, stiffness, pair_code, pair_weight),
    )
    halos = []
    for (a, b), m in zip(kinds, packed):
        halos.append(lateral(a, b, m))
    b0, diag, pair, inside, table, b1, b2, *blank = call(
        bind(prepare_kernel),
        (b0, diag, codes, weights),
        [vec, stack, pairing, mask, tables] + [vec] * (2 + ORDER),
        aliases={0: 0, 1: 1},
    )
    nx_msgs, ny_msgs = len(plan.sx), len(plan.sy)
    row_halos, lane_halos, corner_halos = halos[:nx_msgs], halos[nx_msgs : nx_msgs + ny_msgs], halos[nx_msgs + ny_msgs :]
    b0, diag, pair, b1, b2, table, b3 = call(
        bind(inner_kernel),
        (*lane_halos, inside, b0, diag, pair, b1, b2, table),
        [vec, stack, pairing, vec, vec, tables, vec],
        aliases={ny_msgs + 1 + i: i for i in range(6)},
    )
    at = len(row_halos) + len(corner_halos) + 1
    moments, *rest = call(
        bind(krylov_kernel),
        (*row_halos, *corner_halos, inside, b0, diag, pair, b1, b2, table, b3),
        [message] + [face] * nf + [vec, stack, pairing, vec, vec, tables, vec],
        aliases={at + i: 1 + nf + i for i in range(7)},
    )
    faces, (b0, diag, _, b1, b2, table, b3) = rest[:nf], rest[nf:]
    moments, faces = spread(moments, faces)
    moments, *rest = call(
        bind(middle_kernel),
        (moments, *faces, b0, b1, b2, b3, diag, inside, table, *blank),
        [message] + [face] * nf + [vec] * 3 + [held(*cells), mask, held(buf, LANES), held(nb, LANES)],
        [shifted],
        {1 + nf + 7 + i: 1 + nf + i for i in range(ORDER)},
    )
    faces, kept_arrays = rest[:nf], rest[nf:]
    moments, faces = spread(moments, faces)
    found, lifted, again = call(
        bind(final_kernel),
        (moments, *faces, *kept_arrays, table),
        [kept(*cells)] * 2 + [jax.ShapeDtypeStruct((1, 1), jnp.int32)],
        [pltpu.VMEM(cells, F32), pltpu.VMEM(cells, F32), pltpu.VMEM((2, buf, LANES), F32), shifted, sems(5)],
    )

    def same(arrays, flag):
        vmem = pl.BlockSpec(memory_space=pltpu.VMEM)
        return pl.pallas_call(
copy_refs,
            out_shape=[jax.ShapeDtypeStruct(a.shape, a.dtype) for a in arrays],
            in_specs=[pl.BlockSpec(memory_space=pltpu.SMEM)] + [vmem] * len(arrays),
            out_specs=[vmem] * len(arrays),
            name="same",
        )(flag, *arrays)

    def redo(state):
        inputs = same((load, stiffness, pair_code, pair_weight), state[2])
        return (*same(step_by_step(*inputs), state[2]), jnp.zeros_like(state[2]))

    found, lifted, _ = lax.while_loop(lambda state: state[2][0, 0] > 0, redo, (found, lifted, again))
    return found, lifted


def solution(mesh):
    def whole(*args):
        return per_device(mesh, *args)

    step = jax.shard_map(
        whole,
        mesh=mesh,
        in_specs=(P("body", "gx", "gy"), P("body", "gx", "gy"), P(None, "gx", "gy"), P(None, "gx", "gy")),
        out_specs=(P("body", "gx", "gy"), P("body", "gx", "gy")),
        check_vma=False,
    )
    if "B" not in swaps_of(mesh.shape["gy"]) or not swaps_of(mesh.shape["gx"]):
        return step
    return step
```
